128 devices in a mesh: enc: 8 (over z, core), gen: 16 (over x, y).
Axes of the slice: x: 4, y: 4, z: 4, core: 2. Of those that a mesh axis runs over, the one named last changes fastest.
Arguments:
- hidden_states: bfloat16 [8192, 4096], P('gen'), may hold values from -60 to 60
- grad_out: bfloat16 [8192, 4096], P('gen'), may hold values from -0.29882812 to 0.29882812
- nbr_embed: bfloat16 [256, 128, 1024], P(('enc', 'gen')), may hold values from -60 to 60
- nbr_index: int32 [128, 2], replicated, may hold values from 0 to 255, as said below
- gain: float32 [4096], replicated, may hold values from 0.5 to 1.5
- w_query: bfloat16 [4096, 4096], P(None, 'enc'), may hold values from -0.1875 to 0.1875
- w_out: bfloat16 [4096, 4096], P('enc'), may hold values from -0.09375 to 0.09375
- w_key: bfloat16 [1024, 4096], P(None, 'enc'), may hold values from -0.1875 to 0.1875
- w_value: bfloat16 [1024, 4096], P(None, 'enc'), may hold values from -0.75 to 0.75
- enc_gain: float32 [1024], replicated, may hold values from 0.5 to 1.5
- enc_qkv: bfloat16 [1024, 3072], replicated, may hold values from -0.1875 to 0.1875
- enc_out: bfloat16 [1024, 1024], replicated, may hold values from -0.1875 to 0.1875
Outputs:
- grad_encoded: float32 [256, 128, 1024], P(('enc', 'gen'))
- grad_w_out: float32 [4096, 4096], P('enc', 'gen')
- grad_w_key: float32 [1024, 4096], P('gen', 'enc')
- grad_w_value: float32 [1024, 4096], P('gen', 'enc')
The draws below stay inside these ranges and needn't reach their ends.
Inputs may be any that keep to these rules, and one draw needn't show every extreme that they name: `nbr_index`: every entry 0 to 255 is named exactly once. Entry p is held by index (p // 2) % 16 of gen; block c belongs to index c * 64 // 512 of gen. The blocks of one index of gen name at most 2 entries held by one index of gen, and some pair of indices reaches 2 in every draw.
All inputs are finite; a program needn't handle non-finite values.
Results may differ from the reference program's by a relative error of at most 0.038.
Values may be sent and summed in bfloat16 or wider, within the bound.
A program may use at most 128 MiB of HBM per device.

```python
import jax
import jax.numpy as jnp
from jax import lax

D = 4096
H = 32
DE = 1024
EH = 8
CH = 64
K = 2
R = 128
NB_DEV = 2
TOK_DEV = 512
TOKENS = 8192
BLOCKS = 128
POOL = 256
N_ENC = 8
N_GEN = 16


def scaled_field(key, field_shape):
    key_base, key_rows, key_cols = jax.random.split(key, 3)
    row_shape = field_shape[:-1] + (1,)
    col_shape = (1,) * (len(field_shape) - 1) + (field_shape[-1],)
    cols = jnp.exp(jax.random.uniform(key_cols, col_shape, jnp.float32, -1.15, 1.15))
    base = jax.random.truncated_normal(key_base, -4.0, 4.0, field_shape, jnp.float32)
    rows = jnp.exp(jax.random.uniform(key_rows, row_shape, jnp.float32, -1.15, 1.15))
    return base * rows * cols


def draw_hidden_states(key, part):
    return scaled_field(jax.random.fold_in(key, 11), (TOKENS, D)).astype(jnp.bfloat16)


def draw_nbr_embed(key, part):
    return scaled_field(jax.random.fold_in(key, 23), (POOL, R, DE)).astype(jnp.bfloat16)


def row_permutations(key, groups, length):
    keys_list = jax.random.split(key, groups)
    return jax.vmap(lambda single: jax.random.permutation(single, length))(keys_list).astype(jnp.int32)


def draw_nbr_index(key, part):
    row_size = NB_DEV * N_ENC
    groups = N_GEN
    capacity = max(2, 2 * row_size // groups)
    remain = row_size - capacity
    base_count = remain // (groups - 2)
    extra_count = remain % (groups - 2)
    order = jnp.arange(groups, dtype=jnp.int32)
    pattern = jnp.where(order == 0, capacity, jnp.where(order == 1, 0, base_count + (order - 2 < extra_count).astype(jnp.int32))).astype(jnp.int32)
    key_src, key_dst, key_shuffle, key_pick = jax.random.split(key, 4)
    perm_src = jax.random.permutation(key_src, groups).astype(jnp.int32)
    perm_dst = jax.random.permutation(key_dst, groups).astype(jnp.int32)
    inverse_src = jnp.zeros((groups,), jnp.int32).at[perm_src].set(order)
    bounds = jnp.cumsum(pattern)
    slot_in_row = jnp.arange(row_size, dtype=jnp.int32)
    offsets = jnp.sum((bounds[None, :] <= slot_in_row[:, None]).astype(jnp.int32), axis=1)
    sources = inverse_src[(offsets[None, :] - perm_dst[:, None]) % groups]
    shuffles = row_permutations(key_shuffle, groups, row_size)
    sources = jnp.take_along_axis(sources, shuffles, axis=1)
    flat_source = sources.reshape(-1)
    onehot = (flat_source[:, None] == order[None, :]).astype(jnp.int32)
    rank_in = jnp.sum((jnp.cumsum(onehot, axis=0) - onehot) * onehot, axis=1)
    picks = row_permutations(key_pick, groups, row_size)
    column = picks[flat_source, rank_in]
    entries = column // NB_DEV * (N_GEN * NB_DEV) + flat_source * NB_DEV + column % NB_DEV
    return entries.reshape(BLOCKS, K).astype(jnp.int32)


def level_of(own_key, dims, pieces, smallest, top_value):
    loudness = 1.0
    for axis_at, shards_of in pieces:
        draws = jax.random.uniform(jax.random.fold_in(jax.random.fold_in(own_key, 6), axis_at), (shards_of,), jnp.float32, smallest / len(pieces), top_value / len(pieces))
        loudness = loudness * jnp.repeat(jnp.exp(draws), dims[axis_at] // shards_of).reshape((-1,) + (1,) * (len(dims) - 1 - axis_at))
    return loudness


def bell_draw(own_key, shape, spread, bound, shards=(), kind=jnp.bfloat16):
    factor_of = level_of(own_key, shape, shards, -0.22, 0.18) if shards else 1.0
    values = jax.random.normal(own_key, shape, jnp.float32) * spread * factor_of
    return jnp.minimum(jnp.maximum(values, -bound), bound).astype(kind)


def setup_inputs(seed: int = 0) -> dict:
    arg_keys = jax.random.split(jax.random.key(seed), 13)
    return {
        "hidden_states": draw_hidden_states(jax.random.fold_in(arg_keys[12], 71), 0),
        "grad_out": bell_draw(arg_keys[1], (TOKENS, D), 0.05, 0.29882812, ((0, 16),)),
        "nbr_embed": draw_nbr_embed(jax.random.fold_in(arg_keys[12], 71), 0),
        "nbr_index": draw_nbr_index(jax.random.fold_in(arg_keys[12], 71), 0),
        "gain": jnp.clip(1.0 + 0.1 * jax.random.normal(arg_keys[4], (D,), jnp.float32), 0.5, 1.5),
        "w_query": bell_draw(arg_keys[5], (D, D), (D // 4) ** -0.5, 0.1875, ((1, 8),)),
        "w_out": bell_draw(arg_keys[6], (D, D), D ** -0.5, 0.09375, ((0, 8),)),
        "w_key": bell_draw(arg_keys[7], (DE, D), DE ** -0.5, 0.1875, ((1, 8),)),
        "w_value": bell_draw(arg_keys[8], (DE, D), (DE // 16) ** -0.5, 0.75, ((1, 8),)),
        "enc_gain": jnp.clip(1.0 + 0.1 * jax.random.normal(arg_keys[9], (DE,), jnp.float32), 0.5, 1.5),
        "enc_qkv": bell_draw(arg_keys[10], (DE, 3 * DE), DE ** -0.5, 0.1875),
        "enc_out": bell_draw(arg_keys[11], (DE, DE), DE ** -0.5, 0.1875),
    }


SOFTCAP = 5.0
EPSILON = 1e-06

def rms_scale(values, gain):
    wide = values.astype(jnp.float32)
    factor = lax.rsqrt(lax.optimization_barrier(jnp.mean(wide * wide, axis=-1, keepdims=True)) + EPSILON)
    return (wide * factor * gain.astype(jnp.float32)).astype(jnp.bfloat16)

def attention_parts(queries, keys_all, values_all):
    head_width = queries.shape[-1]
    raw_scores = jnp.einsum('bqhd,bkhd->bhqk', queries.astype(jnp.float32), keys_all.astype(jnp.float32)) * head_width ** (-0.5)
    capped = SOFTCAP * jnp.tanh(raw_scores / SOFTCAP)
    expo_terms = jnp.exp(capped)
    probs_full = expo_terms / lax.optimization_barrier(jnp.sum(expo_terms, axis=-1, keepdims=True))
    probs_low = probs_full.astype(jnp.bfloat16)
    mixed = jnp.einsum('bhqk,bkhd->bqhd', probs_low.astype(jnp.float32), values_all.astype(jnp.float32)).astype(jnp.bfloat16)
    return (raw_scores, probs_full, probs_low, mixed)

def attention_grads(queries, values_all, raw_scores, probs_full, probs_low, d_mixed):
    head_width = queries.shape[-1]
    d_probs = jnp.einsum('bqhd,bkhd->bhqk', d_mixed.astype(jnp.float32), values_all.astype(jnp.float32))
    d_capped = probs_full * (d_probs - lax.optimization_barrier(jnp.sum(probs_full * d_probs, axis=-1, keepdims=True)))
    slope = jnp.tanh(raw_scores / SOFTCAP)
    d_raw = (d_capped * (1.0 - slope * slope) * head_width ** (-0.5)).astype(jnp.bfloat16)
    d_keys = jnp.einsum('bhqk,bqhd->bkhd', d_raw.astype(jnp.float32), queries.astype(jnp.float32)).astype(jnp.bfloat16)
    d_values = jnp.einsum('bhqk,bqhd->bkhd', probs_low.astype(jnp.float32), d_mixed.astype(jnp.float32)).astype(jnp.bfloat16)
    return (d_keys, d_values)

def encode(nbr_embed, enc_gain, enc_qkv, enc_out):
    entries, length, enc_width = nbr_embed.shape
    normed = rms_scale(nbr_embed, enc_gain).reshape(entries * length, enc_width)
    projected = jnp.dot(normed, enc_qkv, preferred_element_type=jnp.float32).astype(jnp.bfloat16)
    projected = projected.reshape(entries, length, 3, EH, enc_width // EH)
    outputs = attention_parts(projected[:, :, 0], projected[:, :, 1], projected[:, :, 2])
    attended = outputs[3].reshape(entries * length, enc_width)
    update = jnp.dot(attended, enc_out, preferred_element_type=jnp.float32).reshape(entries, length, enc_width)
    return (nbr_embed.astype(jnp.float32) + update).astype(jnp.bfloat16)

def reference(hidden_states, grad_out, nbr_embed, nbr_index, gain, w_query, w_out, w_key, w_value, enc_gain, enc_qkv, enc_out):
    encoded = encode(nbr_embed, enc_gain, enc_qkv, enc_out)
    row_size = NB_DEV * N_ENC
    blocks_row = TOK_DEV // CH
    head_width = D // H
    group_width = D // N_ENC
    slot_entries = nbr_index.reshape(-1).astype(jnp.int32)

    def row_step(totals, row_index):
        sum_out, sum_key, sum_value = totals
        states = lax.dynamic_slice_in_dim(hidden_states, row_index * TOK_DEV, TOK_DEV, 0)
        cotangent = lax.dynamic_slice_in_dim(grad_out, row_index * TOK_DEV, TOK_DEV, 0)
        entries = lax.dynamic_slice_in_dim(slot_entries, row_index * row_size, row_size, 0)
        slot_encoded = jnp.take(encoded, entries, axis=0).reshape(row_size * R, DE)
        normed = rms_scale(states, gain)
        queries = jnp.dot(normed, w_query, preferred_element_type=jnp.float32).astype(jnp.bfloat16)
        queries = queries.reshape(blocks_row, CH, H, head_width)
        keys_all = jnp.dot(slot_encoded, w_key, preferred_element_type=jnp.float32).astype(jnp.bfloat16)
        values_all = jnp.dot(slot_encoded, w_value, preferred_element_type=jnp.float32).astype(jnp.bfloat16)
        keys_all = keys_all.reshape(blocks_row, K * R, H, head_width)
        values_all = values_all.reshape(blocks_row, K * R, H, head_width)
        raw_scores, probs_full, probs_low, mixed = attention_parts(queries, keys_all, values_all)
        mixed_rows = mixed.reshape(TOK_DEV, D)
        d_mixed = jnp.dot(cotangent, w_out.T, preferred_element_type=jnp.float32).astype(jnp.bfloat16)
        sum_out = sum_out + jnp.dot(mixed_rows.T, cotangent, preferred_element_type=jnp.float32)
        d_keys, d_values = attention_grads(queries, values_all, raw_scores, probs_full, probs_low, d_mixed.reshape(blocks_row, CH, H, head_width))
        d_keys_rows = d_keys.reshape(row_size * R, D)
        d_values_rows = d_values.reshape(row_size * R, D)
        sum_key = sum_key + jnp.dot(slot_encoded.T, d_keys_rows, preferred_element_type=jnp.float32)
        sum_value = sum_value + jnp.dot(slot_encoded.T, d_values_rows, preferred_element_type=jnp.float32)
        enc_grad = jnp.zeros((row_size * R, DE), jnp.float32)
        for group_index in range(N_ENC):
            start_col = group_index * group_width
            group_term = jnp.dot(d_keys_rows[:, start_col:start_col + group_width], w_key[:, start_col:start_col + group_width].T, preferred_element_type=jnp.float32)
            group_term = group_term + jnp.dot(d_values_rows[:, start_col:start_col + group_width], w_value[:, start_col:start_col + group_width].T, preferred_element_type=jnp.float32)
            rounded = lax.optimization_barrier(group_term.astype(jnp.bfloat16))
            enc_grad = enc_grad + rounded.astype(jnp.float32)
        return ((sum_out, sum_key, sum_value), enc_grad.reshape(row_size, R, DE))
    start_totals = (jnp.zeros((D, D), jnp.float32), jnp.zeros((DE, D), jnp.float32), jnp.zeros((DE, D), jnp.float32))
    totals, slot_grads = lax.scan(row_step, start_totals, jnp.arange(N_GEN, dtype=jnp.int32))
    slot_grads = slot_grads.reshape(POOL, R, DE)
    grad_encoded = jnp.zeros((POOL, R, DE), jnp.float32).at[slot_entries].set(slot_grads)
    return (grad_encoded, totals[0], totals[1], totals[2])
```

```python
import jax
import jax.numpy as jnp
from jax import lax
from jax.sharding import PartitionSpec as P

H = 32
EH = 8
CH = 64
K = 2


SOFTCAP = 5.0
EPSILON = 1e-06


def rms_scale(values, gain):
    wide = values.astype(jnp.float32)
    factor = lax.rsqrt(jnp.mean(wide * wide, axis=-1, keepdims=True) + EPSILON)
    return (wide * factor * gain).astype(jnp.bfloat16)


def attention_parts(queries, keys_all, values_all):
    head_width = queries.shape[-1]
    raw_scores = jnp.einsum(
        "bqhd,bkhd->bhqk", queries, keys_all, preferred_element_type=jnp.float32
    ) * head_width ** (-0.5)
    capped = SOFTCAP * jnp.tanh(raw_scores / SOFTCAP)
    expo_terms = jnp.exp(capped)
    probs_full = expo_terms / jnp.sum(expo_terms, axis=-1, keepdims=True)
    probs_low = probs_full.astype(jnp.bfloat16)
    mixed = jnp.einsum(
        "bhqk,bkhd->bqhd", probs_low, values_all, preferred_element_type=jnp.float32
    ).astype(jnp.bfloat16)
    return (raw_scores, probs_full, probs_low, mixed)


def attention_grads(queries, values_all, raw_scores, probs_full, probs_low, d_mixed):
    head_width = queries.shape[-1]
    d_probs = jnp.einsum("bqhd,bkhd->bhqk", d_mixed, values_all, preferred_element_type=jnp.float32)
    d_capped = probs_full * (d_probs - jnp.sum(probs_full * d_probs, axis=-1, keepdims=True))
    slope = jnp.tanh(raw_scores / SOFTCAP)
    d_raw = (d_capped * (1.0 - slope * slope) * head_width ** (-0.5)).astype(jnp.bfloat16)
    d_keys = jnp.einsum(
        "bhqk,bqhd->bkhd", d_raw, queries, preferred_element_type=jnp.float32
    ).astype(jnp.bfloat16)
    d_values = jnp.einsum(
        "bhqk,bqhd->bkhd", probs_low, d_mixed, preferred_element_type=jnp.float32
    ).astype(jnp.bfloat16)
    return (d_keys, d_values)


def encode(nbr_embed, enc_gain, enc_qkv, enc_out):
    entries, length, enc_width = nbr_embed.shape
    normed = rms_scale(nbr_embed, enc_gain).reshape(entries * length, enc_width)
    projected = jnp.dot(normed, enc_qkv, preferred_element_type=jnp.float32).astype(jnp.bfloat16)
    projected = projected.reshape(entries, length, 3, EH, enc_width // EH)
    outputs = attention_parts(projected[:, :, 0], projected[:, :, 1], projected[:, :, 2])
    attended = outputs[3].reshape(entries * length, enc_width)
    update = jnp.dot(attended, enc_out, preferred_element_type=jnp.float32).reshape(
        entries, length, enc_width
    )
    return (nbr_embed.astype(jnp.float32) + update).astype(jnp.bfloat16)


def routing(nbr_index, row_index, gen_count, per_device, row_size, capacity):
    slot_entries = nbr_index.reshape(-1)
    entry_count = slot_entries.shape[0]
    slot_ids = jnp.arange(entry_count, dtype=jnp.int32)
    target = slot_ids // row_size
    source = slot_entries // per_device % gen_count
    column = slot_entries // (per_device * gen_count) * per_device + slot_entries % per_device
    pair_ids = target * gen_count + source
    pair_onehot = (
        pair_ids[:, None] == jnp.arange(gen_count * gen_count, dtype=jnp.int32)[None, :]
    ).astype(jnp.int32)
    earlier = jnp.cumsum(pair_onehot, axis=0) - pair_onehot
    rank_in = jnp.sum(earlier * pair_onehot, axis=1)
    send_slot = target * capacity + rank_in
    buffer_ids = jnp.arange(gen_count * capacity, dtype=jnp.int32)
    is_mine = (source == row_index).astype(jnp.int32)
    send_match = (send_slot[:, None] == buffer_ids[None, :]).astype(jnp.int32) * is_mine[:, None]
    send_column = jnp.sum(send_match * column[:, None], axis=0)
    column_ids = jnp.arange(row_size, dtype=jnp.int32)
    column_match = (column[:, None] == column_ids[None, :]).astype(jnp.int32) * is_mine[:, None]
    column_position = jnp.sum(column_match * send_slot[:, None], axis=0)
    own_source = lax.dynamic_slice_in_dim(source, row_index * row_size, row_size)
    own_rank = lax.dynamic_slice_in_dim(rank_in, row_index * row_size, row_size)
    receive_position = own_source * capacity + own_rank
    receive_match = (receive_position[:, None] == buffer_ids[None, :]).astype(jnp.int32)
    position_slot = jnp.sum(receive_match * column_ids[:, None], axis=0)
    return (send_column, column_position, receive_position, position_slot)


def to_blocks(rows, enc_count, block_count, head_count):
    features = rows.shape[1]
    keys = rows.shape[0] // block_count
    rows = rows.reshape(enc_count, block_count, keys // enc_count, features)
    return rows.transpose(1, 0, 2, 3).reshape(block_count, keys, head_count, features // head_count)


def from_blocks(blocks, enc_count):
    block_count, keys, head_count, head_width = blocks.shape
    rows = blocks.reshape(block_count, enc_count, keys // enc_count, head_count * head_width)
    return rows.transpose(1, 0, 2, 3).reshape(block_count * keys, head_count * head_width)


def local(
    hidden_states,
    grad_out,
    nbr_embed,
    nbr_index,
    gain,
    w_query,
    w_out,
    w_key,
    w_value,
    enc_gain,
    enc_qkv,
    enc_out,
):
    enc_count = lax.axis_size("enc")
    gen_count = lax.axis_size("gen")
    row_index = lax.axis_index("gen")
    per_device, length, enc_width = nbr_embed.shape
    row_size = per_device * enc_count
    capacity = max(2, 2 * row_size // gen_count)
    token_count, model_width = hidden_states.shape
    head_feats = w_query.shape[1]
    head_width = model_width // H
    head_count = head_feats // head_width
    block_count = token_count // CH
    send_column, column_position, receive_position, position_slot = routing(
        nbr_index, row_index, gen_count, per_device, row_size, capacity
    )
    chunk = length // enc_count
    encoded = encode(nbr_embed, enc_gain, enc_qkv, enc_out)
    pieces = encoded.reshape(per_device, enc_count, chunk, enc_width).transpose(1, 0, 2, 3)
    columns = lax.all_to_all(pieces, "enc", split_axis=0, concat_axis=0, tiled=True)
    columns = columns.reshape(row_size, chunk, enc_width)
    outgoing = jnp.take(columns, send_column, axis=0)
    incoming = lax.all_to_all(outgoing, "gen", split_axis=0, concat_axis=0, tiled=True)
    slot_pieces = jnp.take(incoming, receive_position, axis=0)
    slot_encoded = lax.all_gather(slot_pieces, "enc", axis=0, tiled=False)
    slot_rows = slot_encoded.reshape(row_size * length, enc_width)
    normed = rms_scale(hidden_states, gain)
    queries = jnp.dot(normed, w_query, preferred_element_type=jnp.float32).astype(jnp.bfloat16)
    queries = queries.reshape(block_count, CH, head_count, head_width)
    keys_all = jnp.dot(slot_rows, w_key, preferred_element_type=jnp.float32).astype(jnp.bfloat16)
    values_all = jnp.dot(slot_rows, w_value, preferred_element_type=jnp.float32).astype(
        jnp.bfloat16
    )
    keys_all = to_blocks(keys_all, enc_count, block_count, head_count)
    values_all = to_blocks(values_all, enc_count, block_count, head_count)
    raw_scores, probs_full, probs_low, mixed = attention_parts(queries, keys_all, values_all)
    mixed_rows = mixed.reshape(token_count, head_feats)
    d_mixed = jnp.dot(grad_out, w_out.T, preferred_element_type=jnp.float32).astype(jnp.bfloat16)
    out_term = jnp.dot(mixed_rows.T, grad_out, preferred_element_type=jnp.float32)
    d_keys, d_values = attention_grads(
        queries,
        values_all,
        raw_scores,
        probs_full,
        probs_low,
        d_mixed.reshape(block_count, CH, head_count, head_width),
    )
    d_keys_rows = from_blocks(d_keys, enc_count)
    d_values_rows = from_blocks(d_values, enc_count)
    key_term = jnp.dot(slot_rows.T, d_keys_rows, preferred_element_type=jnp.float32)
    value_term = jnp.dot(slot_rows.T, d_values_rows, preferred_element_type=jnp.float32)
    enc_term = jnp.dot(d_keys_rows, w_key.T, preferred_element_type=jnp.float32) + jnp.dot(
        d_values_rows, w_value.T, preferred_element_type=jnp.float32
    )
    enc_term_low = enc_term.astype(jnp.bfloat16).reshape(enc_count, row_size, chunk, enc_width)
    summed = lax.psum_scatter(enc_term_low, "enc", scatter_dimension=0, tiled=False)
    returning = jnp.take(summed, position_slot, axis=0)
    returned = lax.all_to_all(returning, "gen", split_axis=0, concat_axis=0, tiled=True)
    row_grads = jnp.take(returned, column_position, axis=0)
    home = lax.all_to_all(
        row_grads.reshape(enc_count, per_device, chunk, enc_width),
        "enc",
        split_axis=0,
        concat_axis=0,
        tiled=True,
    )
    grad_encoded = (
        home.transpose(1, 0, 2, 3).reshape(per_device, length, enc_width).astype(jnp.float32)
    )
    grad_w_out, grad_w_key, grad_w_value = (
        lax.psum_scatter(
            out_term.astype(jnp.bfloat16), "gen", scatter_dimension=1, tiled=True
        ).astype(jnp.float32),
        lax.psum_scatter(
            key_term.astype(jnp.bfloat16), "gen", scatter_dimension=0, tiled=True
        ).astype(jnp.float32),
        lax.psum_scatter(
            value_term.astype(jnp.bfloat16), "gen", scatter_dimension=0, tiled=True
        ).astype(jnp.float32),
    )
    return (grad_encoded, grad_w_out, grad_w_key, grad_w_value)


def solution(mesh):
    return jax.shard_map(
        local,
        mesh=mesh,
        in_specs=(
            P("gen", None),
            P("gen", None),
            P(("enc", "gen"), None, None),
            P(),
            P(),
            P(None, "enc"),
            P("enc", None),
            P(None, "enc"),
            P(None, "enc"),
            P(),
            P(),
            P(),
        ),
        out_specs=(
            P(("enc", "gen"), None, None),
            P("enc", "gen"),
            P("gen", "enc"),
            P("gen", "enc"),
        ),
        check_vma=False,
    )
```

```python
import jax
import jax.numpy as jnp
from jax import lax
from jax.experimental import pallas as pl
from jax.experimental.pallas import tpu as pltpu
from jax.sharding import PartitionSpec as P

H = 32
EH = 8
CH = 64
K = 2

MESH = pl.DeviceIdType.MESH


SOFTCAP = 5.0
EPSILON = 1e-06


def rms_scale(values, gain):
    wide = values.astype(jnp.float32)
    factor = lax.rsqrt(jnp.mean(wide * wide, axis=-1, keepdims=True) + EPSILON)
    return (wide * factor * gain).astype(jnp.bfloat16)


def attention_parts(queries, keys_all, values_all):
    head_width = queries.shape[-1]
    raw_scores = jnp.einsum(
        "bqhd,bkhd->bhqk", queries, keys_all, preferred_element_type=jnp.float32
    ) * head_width ** (-0.5)
    capped = SOFTCAP * jnp.tanh(raw_scores / SOFTCAP)
    expo_terms = jnp.exp(capped)
    probs_full = expo_terms / jnp.sum(expo_terms, axis=-1, keepdims=True)
    probs_low = probs_full.astype(jnp.bfloat16)
    mixed = jnp.einsum(
        "bhqk,bkhd->bqhd", probs_low, values_all, preferred_element_type=jnp.float32
    ).astype(jnp.bfloat16)
    return (raw_scores, probs_full, probs_low, mixed)


def attention_grads(queries, values_all, raw_scores, probs_full, probs_low, d_mixed):
    head_width = queries.shape[-1]
    d_probs = jnp.einsum("bqhd,bkhd->bhqk", d_mixed, values_all, preferred_element_type=jnp.float32)
    d_capped = probs_full * (d_probs - jnp.sum(probs_full * d_probs, axis=-1, keepdims=True))
    slope = jnp.tanh(raw_scores / SOFTCAP)
    d_raw = (d_capped * (1.0 - slope * slope) * head_width ** (-0.5)).astype(jnp.bfloat16)
    d_keys = jnp.einsum(
        "bhqk,bqhd->bkhd", d_raw, queries, preferred_element_type=jnp.float32
    ).astype(jnp.bfloat16)
    d_values = jnp.einsum(
        "bhqk,bqhd->bkhd", probs_low, d_mixed, preferred_element_type=jnp.float32
    ).astype(jnp.bfloat16)
    return (d_keys, d_values)


def encode(nbr_embed, enc_gain, enc_qkv, enc_out):
    entries, length, enc_width = nbr_embed.shape
    normed = rms_scale(nbr_embed, enc_gain).reshape(entries * length, enc_width)
    projected = jnp.dot(normed, enc_qkv, preferred_element_type=jnp.float32).astype(jnp.bfloat16)
    projected = projected.reshape(entries, length, 3, EH, enc_width // EH)
    outputs = attention_parts(projected[:, :, 0], projected[:, :, 1], projected[:, :, 2])
    attended = outputs[3].reshape(entries * length, enc_width)
    update = jnp.dot(attended, enc_out, preferred_element_type=jnp.float32).reshape(
        entries, length, enc_width
    )
    return (nbr_embed.astype(jnp.float32) + update).astype(jnp.bfloat16)


def routing(nbr_index, row_index, gen_count, per_device, row_size, capacity):
    slot_entries = nbr_index.reshape(-1)
    entry_count = slot_entries.shape[0]
    slot_ids = jnp.arange(entry_count, dtype=jnp.int32)
    target = slot_ids // row_size
    source = slot_entries // per_device % gen_count
    column = slot_entries // (per_device * gen_count) * per_device + slot_entries % per_device
    pair_ids = target * gen_count + source
    pair_onehot = (
        pair_ids[:, None] == jnp.arange(gen_count * gen_count, dtype=jnp.int32)[None, :]
    ).astype(jnp.int32)
    earlier = jnp.cumsum(pair_onehot, axis=0) - pair_onehot
    rank_in = jnp.sum(earlier * pair_onehot, axis=1)
    send_slot = target * capacity + rank_in
    buffer_ids = jnp.arange(gen_count * capacity, dtype=jnp.int32)
    is_mine = (source == row_index).astype(jnp.int32)
    send_match = (send_slot[:, None] == buffer_ids[None, :]).astype(jnp.int32) * is_mine[:, None]
    send_column = jnp.sum(send_match * column[:, None], axis=0)
    column_ids = jnp.arange(row_size, dtype=jnp.int32)
    column_match = (column[:, None] == column_ids[None, :]).astype(jnp.int32) * is_mine[:, None]
    column_position = jnp.sum(column_match * send_slot[:, None], axis=0)
    own_source = lax.dynamic_slice_in_dim(source, row_index * row_size, row_size)
    own_rank = lax.dynamic_slice_in_dim(rank_in, row_index * row_size, row_size)
    receive_position = own_source * capacity + own_rank
    receive_match = (receive_position[:, None] == buffer_ids[None, :]).astype(jnp.int32)
    position_slot = jnp.sum(receive_match * column_ids[:, None], axis=0)
    return (send_column, column_position, receive_position, position_slot)


def to_blocks(rows, enc_count, block_count, head_count):
    features = rows.shape[1]
    keys = rows.shape[0] // block_count
    rows = rows.reshape(enc_count, block_count, keys // enc_count, features)
    return rows.transpose(1, 0, 2, 3).reshape(block_count, keys, head_count, features // head_count)


def from_blocks(blocks, enc_count):
    block_count, keys, head_count, head_width = blocks.shape
    rows = blocks.reshape(block_count, enc_count, keys // enc_count, head_count * head_width)
    return rows.transpose(1, 0, 2, 3).reshape(block_count * keys, head_count * head_width)


def neighbours():
    enc, gen = lax.axis_index("enc"), lax.axis_index("gen")
    z, core, x, y = enc // 2, enc % 2, gen // 4, gen % 4

    def at(axis, step):
        if axis == "x":
            return (enc, (x + step) % 4 * 4 + y)
        if axis == "y":
            return (enc, x * 4 + (y + step) % 4)
        if axis == "z":
            return ((z + step) % 4 * 2 + core, gen)
        return (z * 2 + (1 - core), gen)

    return enc, gen, {"x": x, "y": y, "z": z, "core": core}, at


def entry_barrier(enc, gen):
    barrier = pltpu.get_barrier_semaphore()

    def greet_gen(step, carry):
        pl.semaphore_signal(barrier, inc=1, device_id=(enc, (gen + step) % 16), device_id_type=MESH)
        return carry

    def greet_enc(step, carry):
        pl.semaphore_signal(barrier, inc=1, device_id=((enc + step) % 8, gen), device_id_type=MESH)
        return carry

    lax.fori_loop(1, 16, greet_gen, 0)
    lax.fori_loop(1, 8, greet_enc, 0)
    pl.semaphore_wait(barrier, 22)


def send(src, dst, sems, number, device):
    return pltpu.make_async_remote_copy(
        src_ref=src,
        dst_ref=dst,
        send_sem=sems.at[0, number],
        recv_sem=sems.at[1, number],
        device_id=device,
        device_id_type=MESH,
    )


def add_rows(out, out_at, terms, rows, step):
    def body(i, carry):
        total = None
        for ref, at in terms:
            value = ref[pl.ds(pl.multiple_of(at + i * step, step), step), :].astype(jnp.float32)
            total = value if total is None else total + value
        if len(out.shape) == 3:
            out[out_at + i] = total.astype(out.dtype)
        else:
            out[pl.ds(pl.multiple_of(out_at + i * step, step), step), :] = total.astype(out.dtype)
        return carry

    lax.fori_loop(0, rows // step, body, 0)


class Ring:
    def __init__(self, src, buf, sems, axis, where, at):
        self.src, self.buf = src, buf
        self.rows = src.shape[0] // 4
        self.half = self.rows // 2
        self.me = where[axis]
        half = self.half
        self.plus, self.minus = (self.me + 1) % 4, (self.me + 3) % 4
        across = (self.me + 2) % 4
        pieces = (
            (across, 0, 1),
            (self.plus, 1, 1),
            (self.plus, 0, 1),
            (across, 1, 3),
            (self.minus, 0, 3),
            (self.minus, 1, 3),
        )
        self.copies = []
        for number, (chunk, side, step) in enumerate(pieces):
            start = pl.multiple_of(chunk * self.rows + side * half, half)
            self.copies.append(
                send(
                    src.at[pl.ds(start, half), :],
                    buf.at[pl.ds(number * half, half), :],
                    sems,
                    number,
                    at(axis, step),
                )
            )

    def first(self):
        self.copies[0].start()
        self.copies[3].start()

    def second(self):
        self.copies[1].start()
        self.copies[4].start()

    def third(self, step):
        half = self.half
        self.copies[0].wait_recv()
        start = self.plus * self.rows
        add_rows(self.src, start, ((self.src, start), (self.buf, 0)), half, step)
        self.copies[2].start()
        self.copies[3].wait_recv()
        start = self.minus * self.rows + half
        add_rows(self.src, start, ((self.src, start), (self.buf, 3 * half)), half, step)
        self.copies[5].start()

    def last(self, out, out_at, step):
        half = self.half
        for number in (1, 2, 4, 5):
            self.copies[number].wait_recv()
        start = self.me * self.rows
        add_rows(out, out_at, ((self.src, start), (self.buf, 2 * half), (self.buf, 4 * half)), half, step)
        add_rows(
            out, out_at + (half // step if len(out.shape) == 3 else half), ((self.src, start + half), (self.buf, half), (self.buf, 5 * half)), half, step
        )

    def drain(self):
        for copy in self.copies:
            copy.wait_send()


def back_kernel(
    position_ref, column_ref,
    mixed_hbm, cot_hbm, rows_hbm, dk_hbm, dv_hbm, wk_hbm, wv_hbm,
    enc_out, wo_out, wk_out, wv_out,
    mixed, cot, rows, dk, dv, wk, wv, mixed_t,
    ot_a, ot_b, kt, vt, ot_a2, ot_b2, kt2, vt2, peers, mine, from_peer, piece, outgoing, returned, grads, home,
    b_ota, b_otb, b_kt, b_vt, b_ota2, b_otb2, b_kt2, b_vt2, b_z,
    load_sems, s_ota, s_otb, s_kt, s_vt, s_ota2, s_otb2, s_kt2, s_vt2, s_z, s_core, s_gen, s_enc,
):
    loads = []
    for number, (src, dst) in enumerate(
        (
            (mixed_hbm, mixed), (cot_hbm, cot), (dk_hbm, dk), (dv_hbm, dv),
            (wk_hbm, wk), (wv_hbm, wv), (rows_hbm, rows),
        )
    ):
        copy = pltpu.make_async_copy(src, dst, load_sems.at[number])
        copy.start()
        loads.append(copy)
    enc, gen, where, at = neighbours()
    x, y, z, core = where["x"], where["y"], where["z"], where["core"]
    entry_barrier(enc, gen)
    ring_oa = Ring(ot_a, b_ota, s_ota, "x", where, at)
    ring_ob = Ring(ot_b, b_otb, s_otb, "y", where, at)
    ring_k = Ring(kt, b_kt, s_kt, "x", where, at)
    ring_v = Ring(vt, b_vt, s_vt, "y", where, at)
    ring_oa2 = Ring(ot_a2, b_ota2, s_ota2, "y", where, at)
    ring_ob2 = Ring(ot_b2, b_otb2, s_otb2, "x", where, at)
    ring_k2 = Ring(kt2, b_kt2, s_kt2, "y", where, at)
    ring_v2 = Ring(vt2, b_vt2, s_vt2, "x", where, at)
    ring_z = Ring(mine, b_z, s_z, "z", where, at)

    loads[0].wait()
    mixed_t[...] = mixed[...].T
    loads[1].wait()

    def out_terms(i, carry):
        to_x, to_y = (x + 2 - i + 4) % 4, (y + 2 - i + 4) % 4

        def tile(j, carry):
            lane_a = pl.multiple_of((to_x * 4 + j) * 256, 256)
            term = jnp.dot(mixed_t[0:256, :], cot[:, pl.ds(lane_a, 256)], preferred_element_type=jnp.float32)
            ot_a[pl.ds(pl.multiple_of(lane_a, 256), 256), :] = term.astype(jnp.bfloat16)
            lane_b = pl.multiple_of((j * 4 + to_y) * 256, 256)
            term = jnp.dot(mixed_t[256:512, :], cot[:, pl.ds(lane_b, 256)], preferred_element_type=jnp.float32)
            ot_b[pl.ds(pl.multiple_of((to_y * 4 + j) * 256, 256), 256), :] = term.astype(jnp.bfloat16)
            return carry

        lax.fori_loop(0, 4, tile, 0)

        @pl.when(i == 0)
        def _():
            ring_oa.first()
            ring_ob.first()

        return carry

    lax.fori_loop(0, 4, out_terms, 0)
    ring_oa.second()
    ring_ob.second()

    for number in (2, 3, 4, 5):
        loads[number].wait()
    core_copies = [
        send(peers.at[pl.ds(k * 256, 256), :], from_peer.at[pl.ds(k * 256, 256), :], s_core, k, at("core", 1))
        for k in range(4)
    ]

    def enc_piece(piece_at, out, out_at):
        def tile(j, carry):
            start = pl.multiple_of(piece_at * 256 + j * 128, 128)
            term = lax.dot_general(
                dk[pl.ds(start, 128), :], wk[...], (((1,), (1,)), ((), ())), preferred_element_type=jnp.float32
            )
            term = term + lax.dot_general(
                dv[pl.ds(start, 128), :], wv[...], (((1,), (1,)), ((), ())), preferred_element_type=jnp.float32
            )
            out[pl.ds(pl.multiple_of(out_at + j * 128, 128), 128), :] = term.astype(jnp.bfloat16)
            return carry

        lax.fori_loop(0, 2, tile, 0)

    def to_peer(k, carry):
        enc_piece(k * 2 + (1 - core), peers, k * 256)
        for number in range(4):

            @pl.when(k == number)
            def _():
                core_copies[number].start()

        return carry

    lax.fori_loop(0, 4, to_peer, 0)

    def to_own(k, carry):
        enc_piece(k * 2 + core, mine, k * 256)
        return carry

    lax.fori_loop(0, 4, to_own, 0)
    for k in range(4):
        core_copies[k].wait_recv()
    add_rows(mine, 0, ((mine, 0), (from_peer, 0)), 1024, 32)
    ring_z.first()
    ring_z.second()
    ring_oa.third(64)
    ring_ob.third(64)

    loads[6].wait()

    def key_terms(i, carry):
        lane = pl.multiple_of(i * 128, 128)
        block = rows[:, pl.ds(lane, 128)]
        term = lax.dot_general(block, dk[...], (((0,), (0,)), ((), ())), preferred_element_type=jnp.float32)
        kt[pl.ds(pl.multiple_of(i * 128, 128), 128), :] = term.astype(jnp.bfloat16)
        term = lax.dot_general(block, dv[...], (((0,), (0,)), ((), ())), preferred_element_type=jnp.float32)
        low = term.astype(jnp.bfloat16)
        for part in range(2):
            to_x, to_y = (i * 2 + part) // 4, (i * 2 + part) % 4
            vt[pl.ds(pl.multiple_of(to_y * 256 + to_x * 64, 64), 64), :] = low[part * 64 : part * 64 + 64]
        return carry

    lax.fori_loop(0, 8, key_terms, 0)
    ring_k.first()
    ring_v.first()
    ring_k.second()
    ring_v.second()

    ring_z.third(32)
    ring_k.third(64)
    ring_v.third(64)

    ring_oa.last(ot_a2, 0, 64)
    ring_oa2.first()
    ring_oa2.second()
    ring_ob.last(ot_b2, 0, 64)
    ring_ob2.first()
    ring_ob2.second()

    ring_z.last(piece, 0, 16)
    for j in range(32):
        outgoing[j] = piece[position_ref[j]]
    own_at = gen * 2

    def gen_copy(step):
        peer = (gen + step) % 16
        return send(
            outgoing.at[pl.ds(peer * 2, 2)],
            returned.at[pl.ds(own_at, 2)],
            s_gen,
            step - 1,
            (enc, peer),
        )

    def start_gen(step, carry):
        gen_copy(step).start()
        return carry

    lax.fori_loop(1, 16, start_gen, 0)
    returned[pl.ds(own_at, 2)] = outgoing[pl.ds(own_at, 2)]

    ring_k.last(kt2, 0, 64)
    ring_k2.first()
    ring_k2.second()
    ring_v.last(vt2, 0, 64)
    ring_v2.first()
    ring_v2.second()
    ring_oa2.third(64)
    ring_ob2.third(64)
    ring_k2.third(32)
    ring_v2.third(32)

    def wait_gen(step, carry):
        gen_copy(step).wait_recv()
        return carry

    lax.fori_loop(1, 16, wait_gen, 0)
    for j in range(16):
        grads[j // 2, j % 2] = returned[column_ref[j]]
    row_at = pl.multiple_of(enc * 16, 16)

    def enc_copy(step):
        peer = (enc + step) % 8
        return send(grads.at[peer], home.at[:, pl.ds(row_at, 16), :], s_enc, step - 1, (peer, gen))

    def start_enc(step, carry):
        enc_copy(step).start()
        return carry

    lax.fori_loop(1, 8, start_enc, 0)
    home[:, pl.ds(row_at, 16), :] = grads[enc]

    ring_oa2.last(wo_out, 0, 64)
    ring_ob2.last(wo_out, 256, 64)
    ring_k2.last(wk_out, 0, 32)
    ring_v2.last(wv_out, 0, 32)

    def wait_enc(step, carry):
        enc_copy(step).wait_recv()
        return carry

    lax.fori_loop(1, 8, wait_enc, 0)
    enc_out[...] = home[...]

    for ring in (ring_oa, ring_ob, ring_k, ring_v, ring_oa2, ring_ob2, ring_k2, ring_v2, ring_z):
        ring.drain()
    for k in range(4):
        core_copies[k].wait_send()

    def drain_gen(step, carry):
        gen_copy(step).wait_send()
        return carry

    def drain_enc(step, carry):
        enc_copy(step).wait_send()
        return carry

    lax.fori_loop(1, 16, drain_gen, 0)
    lax.fori_loop(1, 8, drain_enc, 0)


def back(position, column, mixed, cot, rows, dk, dv, wk, wv):
    low = jnp.bfloat16

    def ring_buffer(src):
        return pltpu.VMEM((src[0] // 4 * 3, src[1]), low)

    srcs = ((4096, 256), (4096, 256), (1024, 512), (1024, 512), (1024, 256), (1024, 256), (256, 512), (256, 512))
    anywhere = pl.BlockSpec(memory_space=pl.ANY)
    scalars = pl.BlockSpec(memory_space=pltpu.SMEM)
    whole = pl.BlockSpec(memory_space=pltpu.VMEM)
    operands = (mixed, cot, rows, dk, dv, wk, wv)
    return pl.pallas_call(
        back_kernel,
        out_shape=(
            jax.ShapeDtypeStruct((2, 128, 1024), low),
            jax.ShapeDtypeStruct((512, 256), low),
            jax.ShapeDtypeStruct((64, 512), low),
            jax.ShapeDtypeStruct((64, 512), low),
        ),
        in_specs=[scalars] * 2 + [anywhere] * 7,
        out_specs=(whole,) * 4,
        scratch_shapes=[pltpu.VMEM(a.shape, low) for a in operands]
        + [pltpu.VMEM((512, 512), low)]
        + [pltpu.VMEM(s, low) for s in srcs]
        + [
            pltpu.VMEM((1024, 1024), low),
            pltpu.VMEM((1024, 1024), low),
            pltpu.VMEM((1024, 1024), low),
            pltpu.VMEM((16, 16, 1024), low),
            pltpu.VMEM((32, 16, 1024), low),
            pltpu.VMEM((32, 16, 1024), low),
            pltpu.VMEM((8, 2, 16, 1024), low),
            pltpu.VMEM((2, 128, 1024), low),
        ]
        + [ring_buffer(s) for s in srcs]
        + [ring_buffer((1024, 1024))]
        + [pltpu.SemaphoreType.DMA((7,))]
        + [pltpu.SemaphoreType.DMA((2, 6))] * 9
        + [pltpu.SemaphoreType.DMA((2, 4)), pltpu.SemaphoreType.DMA((2, 15)), pltpu.SemaphoreType.DMA((2, 7))],
        compiler_params=pltpu.CompilerParams(
            collective_id=1, has_side_effects=True, vmem_limit_bytes=62 * 1024 * 1024
        ),
    )(position, column, *operands)


def local(
    hidden_states,
    grad_out,
    nbr_embed,
    nbr_index,
    gain,
    w_query,
    w_out,
    w_key,
    w_value,
    enc_gain,
    enc_qkv,
    enc_out,
):
    enc_count = lax.axis_size("enc")
    gen_count = lax.axis_size("gen")
    row_index = lax.axis_index("gen")
    per_device, length, enc_width = nbr_embed.shape
    row_size = per_device * enc_count
    capacity = max(2, 2 * row_size // gen_count)
    token_count, model_width = hidden_states.shape
    head_feats = w_query.shape[1]
    head_width = model_width // H
    head_count = head_feats // head_width
    block_count = token_count // CH
    send_column, column_position, receive_position, position_slot = routing(
        nbr_index, row_index, gen_count, per_device, row_size, capacity
    )
    chunk = length // enc_count
    encoded = encode(nbr_embed, enc_gain, enc_qkv, enc_out)
    pieces = encoded.reshape(per_device, enc_count, chunk, enc_width).transpose(1, 0, 2, 3)
    columns = lax.all_to_all(pieces, "enc", split_axis=0, concat_axis=0, tiled=True)
    columns = columns.reshape(row_size, chunk, enc_width)
    outgoing = jnp.take(columns, send_column, axis=0)
    incoming = lax.all_to_all(outgoing, "gen", split_axis=0, concat_axis=0, tiled=True)
    slot_pieces = jnp.take(incoming, receive_position, axis=0)
    slot_encoded = lax.all_gather(slot_pieces, "enc", axis=0, tiled=False)
    slot_rows = slot_encoded.reshape(row_size * length, enc_width)
    normed = rms_scale(hidden_states, gain)
    queries = jnp.dot(normed, w_query, preferred_element_type=jnp.float32).astype(jnp.bfloat16)
    queries = queries.reshape(block_count, CH, head_count, head_width)
    keys_all = jnp.dot(slot_rows, w_key, preferred_element_type=jnp.float32).astype(jnp.bfloat16)
    values_all = jnp.dot(slot_rows, w_value, preferred_element_type=jnp.float32).astype(
        jnp.bfloat16
    )
    keys_all = to_blocks(keys_all, enc_count, block_count, head_count)
    values_all = to_blocks(values_all, enc_count, block_count, head_count)
    raw_scores, probs_full, probs_low, mixed = attention_parts(queries, keys_all, values_all)
    mixed_rows = mixed.reshape(token_count, head_feats)
    d_mixed = jnp.dot(grad_out, w_out.T, preferred_element_type=jnp.float32).astype(jnp.bfloat16)
    d_keys, d_values = attention_grads(
        queries,
        values_all,
        raw_scores,
        probs_full,
        probs_low,
        d_mixed.reshape(block_count, CH, head_count, head_width),
    )
    d_keys_rows = from_blocks(d_keys, enc_count)
    d_values_rows = from_blocks(d_values, enc_count)
    outputs = back(
        position_slot,
        column_position,
        mixed_rows,
        grad_out,
        slot_rows,
        d_keys_rows,
        d_values_rows,
        w_key,
        w_value,
    )
    return tuple(output.astype(jnp.float32) for output in outputs)


def solution(mesh):
    return jax.shard_map(
        local,
        mesh=mesh,
        in_specs=(
            P("gen", None),
            P("gen", None),
            P(("enc", "gen"), None, None),
            P(),
            P(),
            P(None, "enc"),
            P("enc", None),
            P(None, "enc"),
            P(None, "enc"),
            P(),
            P(),
            P(),
        ),
        out_specs=(
            P(("enc", "gen"), None, None),
            P("enc", "gen"),
            P("gen", "enc"),
            P("gen", "enc"),
        ),
        check_vma=False,
    )
```

```python
import jax
import jax.numpy as jnp
from jax import lax
from jax.experimental import pallas as pl
from jax.experimental.pallas import tpu as pltpu
from jax.sharding import PartitionSpec as P

H = 32
EH = 8
CH = 64
K = 2

MESH = pl.DeviceIdType.MESH


SOFTCAP = 5.0
EPSILON = 1e-06


def rms_scale(values, gain):
    wide = values.astype(jnp.float32)
    factor = lax.rsqrt(jnp.mean(wide * wide, axis=-1, keepdims=True) + EPSILON)
    return (wide * factor * gain).astype(jnp.bfloat16)


def attention_parts(queries, keys_all, values_all):
    head_width = queries.shape[-1]
    raw_scores = jnp.einsum(
        "bqhd,bkhd->bhqk", queries, keys_all, preferred_element_type=jnp.float32
    ) * head_width ** (-0.5)
    capped = SOFTCAP * jnp.tanh(raw_scores / SOFTCAP)
    expo_terms = jnp.exp(capped)
    probs_full = expo_terms / jnp.sum(expo_terms, axis=-1, keepdims=True)
    probs_low = probs_full.astype(jnp.bfloat16)
    mixed = jnp.einsum(
        "bhqk,bkhd->bqhd", probs_low, values_all, preferred_element_type=jnp.float32
    ).astype(jnp.bfloat16)
    return (raw_scores, probs_full, probs_low, mixed)


def encode(nbr_embed, enc_gain, enc_qkv, enc_out):
    entries, length, enc_width = nbr_embed.shape
    normed = rms_scale(nbr_embed, enc_gain).reshape(entries * length, enc_width)
    projected = jnp.dot(normed, enc_qkv, preferred_element_type=jnp.float32).astype(jnp.bfloat16)
    projected = projected.reshape(entries, length, 3, EH, enc_width // EH)
    outputs = attention_parts(projected[:, :, 0], projected[:, :, 1], projected[:, :, 2])
    attended = outputs[3].reshape(entries * length, enc_width)
    update = jnp.dot(attended, enc_out, preferred_element_type=jnp.float32).reshape(
        entries, length, enc_width
    )
    return (nbr_embed.astype(jnp.float32) + update).astype(jnp.bfloat16)


def routing(nbr_index, row_index, gen_count, per_device, row_size, capacity):
    slot_entries = nbr_index.reshape(-1)
    entry_count = slot_entries.shape[0]
    slot_ids = jnp.arange(entry_count, dtype=jnp.int32)
    target = slot_ids // row_size
    source = slot_entries // per_device % gen_count
    column = slot_entries // (per_device * gen_count) * per_device + slot_entries % per_device
    pair_ids = target * gen_count + source
    pair_onehot = (
        pair_ids[:, None] == jnp.arange(gen_count * gen_count, dtype=jnp.int32)[None, :]
    ).astype(jnp.int32)
    earlier = jnp.cumsum(pair_onehot, axis=0) - pair_onehot
    rank_in = jnp.sum(earlier * pair_onehot, axis=1)
    send_slot = target * capacity + rank_in
    buffer_ids = jnp.arange(gen_count * capacity, dtype=jnp.int32)
    is_mine = (source == row_index).astype(jnp.int32)
    send_match = (send_slot[:, None] == buffer_ids[None, :]).astype(jnp.int32) * is_mine[:, None]
    send_column = jnp.sum(send_match * column[:, None], axis=0)
    column_ids = jnp.arange(row_size, dtype=jnp.int32)
    column_match = (column[:, None] == column_ids[None, :]).astype(jnp.int32) * is_mine[:, None]
    column_position = jnp.sum(column_match * send_slot[:, None], axis=0)
    own_source = lax.dynamic_slice_in_dim(source, row_index * row_size, row_size)
    own_rank = lax.dynamic_slice_in_dim(rank_in, row_index * row_size, row_size)
    receive_position = own_source * capacity + own_rank
    receive_match = (receive_position[:, None] == buffer_ids[None, :]).astype(jnp.int32)
    position_slot = jnp.sum(receive_match * column_ids[:, None], axis=0)
    return (send_column, column_position, receive_position, position_slot)


def neighbours():
    enc, gen = lax.axis_index("enc"), lax.axis_index("gen")
    z, core, x, y = enc // 2, enc % 2, gen // 4, gen % 4

    def at(axis, step):
        if axis == "x":
            return (enc, (x + step) % 4 * 4 + y)
        if axis == "y":
            return (enc, x * 4 + (y + step) % 4)
        if axis == "z":
            return ((z + step) % 4 * 2 + core, gen)
        return (z * 2 + (1 - core), gen)

    return enc, gen, {"x": x, "y": y, "z": z, "core": core}, at


def entry_barrier(enc, gen):
    barrier = pltpu.get_barrier_semaphore()

    def greet_gen(step, carry):
        pl.semaphore_signal(barrier, inc=1, device_id=(enc, (gen + step) % 16), device_id_type=MESH)
        return carry

    def greet_enc(step, carry):
        pl.semaphore_signal(barrier, inc=1, device_id=((enc + step) % 8, gen), device_id_type=MESH)
        return carry

    lax.fori_loop(1, 16, greet_gen, 0)
    lax.fori_loop(1, 8, greet_enc, 0)
    pl.semaphore_wait(barrier, 22)


def send(src, dst, sems, number, device):
    return pltpu.make_async_remote_copy(
        src_ref=src,
        dst_ref=dst,
        send_sem=sems.at[0, number],
        recv_sem=sems.at[1, number],
        device_id=device,
        device_id_type=MESH,
    )


def add_rows(out, out_at, terms, rows, step):
    def body(i, carry):
        total = None
        for ref, at in terms:
            value = ref[pl.ds(pl.multiple_of(at + i * step, step), step), :].astype(jnp.float32)
            total = value if total is None else total + value
        if len(out.shape) == 3:
            out[out_at + i] = total.astype(out.dtype)
        else:
            out[pl.ds(pl.multiple_of(out_at + i * step, step), step), :] = total.astype(out.dtype)
        return carry

    lax.fori_loop(0, rows // step, body, 0)


class Ring:
    def __init__(self, src, buf, sems, axis, where, at):
        self.src, self.buf = src, buf
        self.rows = src.shape[0] // 4
        self.half = self.rows // 2
        self.me = where[axis]
        half = self.half
        self.plus, self.minus = (self.me + 1) % 4, (self.me + 3) % 4
        across = (self.me + 2) % 4
        pieces = (
            (across, 0, 1),
            (self.plus, 1, 1),
            (self.plus, 0, 1),
            (across, 1, 3),
            (self.minus, 0, 3),
            (self.minus, 1, 3),
        )
        self.copies = []
        for number, (chunk, side, step) in enumerate(pieces):
            start = pl.multiple_of(chunk * self.rows + side * half, half)
            self.copies.append(
                send(
                    src.at[pl.ds(start, half), :],
                    buf.at[pl.ds(number * half, half), :],
                    sems,
                    number,
                    at(axis, step),
                )
            )

    def first(self):
        self.copies[0].start()
        self.copies[3].start()

    def second(self):
        self.copies[1].start()
        self.copies[4].start()

    def third(self, step):
        half = self.half
        self.copies[0].wait_recv()
        start = self.plus * self.rows
        add_rows(self.src, start, ((self.src, start), (self.buf, 0)), half, step)
        self.copies[2].start()
        self.copies[3].wait_recv()
        start = self.minus * self.rows + half
        add_rows(self.src, start, ((self.src, start), (self.buf, 3 * half)), half, step)
        self.copies[5].start()

    def last(self, out, out_at, step):
        half = self.half
        for number in (1, 2, 4, 5):
            self.copies[number].wait_recv()
        start = self.me * self.rows
        add_rows(out, out_at, ((self.src, start), (self.buf, 2 * half), (self.buf, 4 * half)), half, step)
        add_rows(
            out, out_at + (half // step if len(out.shape) == 3 else half), ((self.src, start + half), (self.buf, half), (self.buf, 5 * half)), half, step
        )

    def drain(self):
        for copy in self.copies:
            copy.wait_send()


def back_kernel(
    position_ref, column_ref,
    mixed_hbm, cot_hbm, rows_hbm, dk_hbm, dv_hbm, wk_hbm, wv_hbm,
    enc_out, wo_out, wk_out, wv_out,
    mixed, cot, rows, dk, dv, wk, wv, mixed_t,
    ot_a, ot_b, kt, vt, ot_a2, ot_b2, kt2, vt2, peers, mine, from_peer, piece, outgoing, returned, grads, home,
    b_ota, b_otb, b_kt, b_vt, b_ota2, b_otb2, b_kt2, b_vt2, b_z,
    load_sems, s_ota, s_otb, s_kt, s_vt, s_ota2, s_otb2, s_kt2, s_vt2, s_z, s_core, s_gen, s_enc,
):
    loads = []
    for number, (src, dst) in enumerate(
        (
            (mixed_hbm, mixed), (cot_hbm, cot), (dk_hbm, dk), (dv_hbm, dv),
            (wk_hbm, wk), (wv_hbm, wv), (rows_hbm, rows),
        )
    ):
        copy = pltpu.make_async_copy(src, dst, load_sems.at[number])
        copy.start()
        loads.append(copy)
    enc, gen, where, at = neighbours()
    x, y, z, core = where["x"], where["y"], where["z"], where["core"]
    entry_barrier(enc, gen)
    ring_oa = Ring(ot_a, b_ota, s_ota, "x", where, at)
    ring_ob = Ring(ot_b, b_otb, s_otb, "y", where, at)
    ring_k = Ring(kt, b_kt, s_kt, "x", where, at)
    ring_v = Ring(vt, b_vt, s_vt, "y", where, at)
    ring_oa2 = Ring(ot_a2, b_ota2, s_ota2, "y", where, at)
    ring_ob2 = Ring(ot_b2, b_otb2, s_otb2, "x", where, at)
    ring_k2 = Ring(kt2, b_kt2, s_kt2, "y", where, at)
    ring_v2 = Ring(vt2, b_vt2, s_vt2, "x", where, at)
    ring_z = Ring(mine, b_z, s_z, "z", where, at)

    loads[0].wait()
    mixed_t[...] = mixed[...].T
    loads[1].wait()

    def out_terms(i, carry):
        to_x, to_y = (x + 2 - i + 4) % 4, (y + 2 - i + 4) % 4

        def tile(j, carry):
            lane_a = pl.multiple_of((to_x * 4 + j) * 256, 256)
            term = jnp.dot(mixed_t[0:256, :], cot[:, pl.ds(lane_a, 256)], preferred_element_type=jnp.float32)
            ot_a[pl.ds(pl.multiple_of(lane_a, 256), 256), :] = term.astype(jnp.bfloat16)
            lane_b = pl.multiple_of((j * 4 + to_y) * 256, 256)
            term = jnp.dot(mixed_t[256:512, :], cot[:, pl.ds(lane_b, 256)], preferred_element_type=jnp.float32)
            ot_b[pl.ds(pl.multiple_of((to_y * 4 + j) * 256, 256), 256), :] = term.astype(jnp.bfloat16)
            return carry

        lax.fori_loop(0, 4, tile, 0)

        @pl.when(i == 0)
        def _():
            ring_oa.first()
            ring_ob.first()

        return carry

    lax.fori_loop(0, 4, out_terms, 0)
    ring_oa.second()
    ring_ob.second()

    for number in (2, 3, 4, 5):
        loads[number].wait()
    core_copies = [
        send(peers.at[pl.ds(k * 256, 256), :], from_peer.at[pl.ds(k * 256, 256), :], s_core, k, at("core", 1))
        for k in range(4)
    ]

    def enc_piece(piece_at, out, out_at):
        def tile(j, carry):
            start = pl.multiple_of(piece_at * 256 + j * 128, 128)
            term = lax.dot_general(
                dk[pl.ds(start, 128), :], wk[...], (((1,), (1,)), ((), ())), preferred_element_type=jnp.float32
            )
            term = term + lax.dot_general(
                dv[pl.ds(start, 128), :], wv[...], (((1,), (1,)), ((), ())), preferred_element_type=jnp.float32
            )
            out[pl.ds(pl.multiple_of(out_at + j * 128, 128), 128), :] = term.astype(jnp.bfloat16)
            return carry

        lax.fori_loop(0, 2, tile, 0)

    def to_peer(k, carry):
        enc_piece(k * 2 + (1 - core), peers, k * 256)
        for number in range(4):

            @pl.when(k == number)
            def _():
                core_copies[number].start()

        return carry

    lax.fori_loop(0, 4, to_peer, 0)

    def to_own(k, carry):
        enc_piece(k * 2 + core, mine, k * 256)
        return carry

    lax.fori_loop(0, 4, to_own, 0)
    for k in range(4):
        core_copies[k].wait_recv()
    add_rows(mine, 0, ((mine, 0), (from_peer, 0)), 1024, 32)
    ring_z.first()
    ring_z.second()
    ring_oa.third(64)
    ring_ob.third(64)

    loads[6].wait()

    def key_terms(i, carry):
        lane = pl.multiple_of(i * 128, 128)
        block = rows[:, pl.ds(lane, 128)]
        term = lax.dot_general(block, dk[...], (((0,), (0,)), ((), ())), preferred_element_type=jnp.float32)
        kt[pl.ds(pl.multiple_of(i * 128, 128), 128), :] = term.astype(jnp.bfloat16)
        term = lax.dot_general(block, dv[...], (((0,), (0,)), ((), ())), preferred_element_type=jnp.float32)
        low = term.astype(jnp.bfloat16)
        for part in range(2):
            to_x, to_y = (i * 2 + part) // 4, (i * 2 + part) % 4
            vt[pl.ds(pl.multiple_of(to_y * 256 + to_x * 64, 64), 64), :] = low[part * 64 : part * 64 + 64]
        return carry

    lax.fori_loop(0, 8, key_terms, 0)
    ring_k.first()
    ring_v.first()
    ring_k.second()
    ring_v.second()

    ring_z.third(32)
    ring_k.third(64)
    ring_v.third(64)

    ring_oa.last(ot_a2, 0, 64)
    ring_oa2.first()
    ring_oa2.second()
    ring_ob.last(ot_b2, 0, 64)
    ring_ob2.first()
    ring_ob2.second()

    ring_z.last(piece, 0, 16)
    for j in range(32):
        outgoing[j] = piece[position_ref[j]]
    own_at = gen * 2

    def gen_copy(step):
        peer = (gen + step) % 16
        return send(
            outgoing.at[pl.ds(peer * 2, 2)],
            returned.at[pl.ds(own_at, 2)],
            s_gen,
            step - 1,
            (enc, peer),
        )

    def start_gen(step, carry):
        gen_copy(step).start()
        return carry

    lax.fori_loop(1, 16, start_gen, 0)
    returned[pl.ds(own_at, 2)] = outgoing[pl.ds(own_at, 2)]

    ring_k.last(kt2, 0, 64)
    ring_k2.first()
    ring_k2.second()
    ring_v.last(vt2, 0, 64)
    ring_v2.first()
    ring_v2.second()
    ring_oa2.third(64)
    ring_ob2.third(64)
    ring_k2.third(32)
    ring_v2.third(32)

    def wait_gen(step, carry):
        gen_copy(step).wait_recv()
        return carry

    lax.fori_loop(1, 16, wait_gen, 0)
    for j in range(16):
        grads[j // 2, j % 2] = returned[column_ref[j]]
    row_at = pl.multiple_of(enc * 16, 16)

    def enc_copy(step):
        peer = (enc + step) % 8
        return send(grads.at[peer], home.at[:, pl.ds(row_at, 16), :], s_enc, step - 1, (peer, gen))

    def start_enc(step, carry):
        enc_copy(step).start()
        return carry

    lax.fori_loop(1, 8, start_enc, 0)
    home[:, pl.ds(row_at, 16), :] = grads[enc]

    ring_oa2.last(wo_out, 0, 64)
    ring_ob2.last(wo_out, 256, 64)
    ring_k2.last(wk_out, 0, 32)
    ring_v2.last(wv_out, 0, 32)

    def wait_enc(step, carry):
        enc_copy(step).wait_recv()
        return carry

    lax.fori_loop(1, 8, wait_enc, 0)
    enc_out[...] = home[...]

    for ring in (ring_oa, ring_ob, ring_k, ring_v, ring_oa2, ring_ob2, ring_k2, ring_v2, ring_z):
        ring.drain()
    for k in range(4):
        core_copies[k].wait_send()

    def drain_gen(step, carry):
        gen_copy(step).wait_send()
        return carry

    def drain_enc(step, carry):
        enc_copy(step).wait_send()
        return carry

    lax.fori_loop(1, 16, drain_gen, 0)
    lax.fori_loop(1, 8, drain_enc, 0)


def back(position, column, mixed, cot, rows, dk, dv, wk, wv):
    low = jnp.bfloat16

    def ring_buffer(src):
        return pltpu.VMEM((src[0] // 4 * 3, src[1]), low)

    srcs = ((4096, 256), (4096, 256), (1024, 512), (1024, 512), (1024, 256), (1024, 256), (256, 512), (256, 512))
    anywhere = pl.BlockSpec(memory_space=pl.ANY)
    scalars = pl.BlockSpec(memory_space=pltpu.SMEM)
    whole = pl.BlockSpec(memory_space=pltpu.VMEM)
    operands = (mixed, cot, rows, dk, dv, wk, wv)
    return pl.pallas_call(
        back_kernel,
        out_shape=(
            jax.ShapeDtypeStruct((2, 128, 1024), low),
            jax.ShapeDtypeStruct((512, 256), low),
            jax.ShapeDtypeStruct((64, 512), low),
            jax.ShapeDtypeStruct((64, 512), low),
        ),
        in_specs=[scalars] * 2 + [anywhere] * 7,
        out_specs=(whole,) * 4,
        scratch_shapes=[pltpu.VMEM(a.shape, low) for a in operands]
        + [pltpu.VMEM((512, 512), low)]
        + [pltpu.VMEM(s, low) for s in srcs]
        + [
            pltpu.VMEM((1024, 1024), low),
            pltpu.VMEM((1024, 1024), low),
            pltpu.VMEM((1024, 1024), low),
            pltpu.VMEM((16, 16, 1024), low),
            pltpu.VMEM((32, 16, 1024), low),
            pltpu.VMEM((32, 16, 1024), low),
            pltpu.VMEM((8, 2, 16, 1024), low),
            pltpu.VMEM((2, 128, 1024), low),
        ]
        + [ring_buffer(s) for s in srcs]
        + [ring_buffer((1024, 1024))]
        + [pltpu.SemaphoreType.DMA((7,))]
        + [pltpu.SemaphoreType.DMA((2, 6))] * 9
        + [pltpu.SemaphoreType.DMA((2, 4)), pltpu.SemaphoreType.DMA((2, 15)), pltpu.SemaphoreType.DMA((2, 7))],
        compiler_params=pltpu.CompilerParams(
            collective_id=1, has_side_effects=True, vmem_limit_bytes=62 * 1024 * 1024
        ),
    )(position, column, *operands)


def project_queries(hidden, gain, wq, normed, out):
    def norm(i, carry):
        at = pl.ds(pl.multiple_of(i * 16, 16), 16)
        wide = hidden[at, :].astype(jnp.float32)
        factor = lax.rsqrt(jnp.mean(wide * wide, axis=-1, keepdims=True) + EPSILON)
        normed[at, :] = (wide * factor * gain[...]).astype(jnp.bfloat16)
        return carry

    lax.fori_loop(0, hidden.shape[0] // 16, norm, 0)

    def tile(i, carry):
        at = pl.ds(pl.multiple_of(i * 256, 256), 256)
        out[at, :] = jnp.dot(normed[at, :], wq[...], preferred_element_type=jnp.float32).astype(jnp.bfloat16)
        return carry

    lax.fori_loop(0, hidden.shape[0] // 256, tile, 0)


def project_cotangents(cot, wo, out):
    def tile(i, carry):
        at = pl.ds(pl.multiple_of(i * 256, 256), 256)
        out[at, :] = lax.dot_general(
            cot[at, :], wo[...], (((1,), (1,)), ((), ())), preferred_element_type=jnp.float32
        ).astype(jnp.bfloat16)
        return carry

    lax.fori_loop(0, cot.shape[0] // 256, tile, 0)


def front_kernel(
    send_ref, receive_ref,
    encoded, gain, hidden_hbm, cot_hbm, wq_hbm, wo_hbm, wk_hbm, wv_hbm,
    q_out, dm_out, k_out, v_out, rows_out,
    hidden, cot, wq, wo, wk, wv, normed, columns, outgoing, incoming, rows,
    load_sems, s_enc, s_gen, s_ring, s_core, rows_sems,
):
    loads = []
    for number, (src, dst) in enumerate(
        ((hidden_hbm, hidden), (wq_hbm, wq), (cot_hbm, cot), (wo_hbm, wo), (wk_hbm, wk), (wv_hbm, wv))
    ):
        copy = pltpu.make_async_copy(src, dst, load_sems.at[number])
        copy.start()
        loads.append(copy)
    enc, gen, where, at = neighbours()
    z, core = where["z"], where["core"]
    entry_barrier(enc, gen)

    def enc_copy(step):
        peer = (enc + step) % 8
        return send(
            encoded.at[:, pl.ds(pl.multiple_of(peer * 16, 16), 16), :],
            columns.at[pl.ds(enc * 2, 2)],
            s_enc,
            step - 1,
            (peer, gen),
        )

    def start_enc(step, carry):
        enc_copy(step).start()
        return carry

    lax.fori_loop(1, 8, start_enc, 0)
    columns[pl.ds(enc * 2, 2)] = encoded[:, pl.ds(pl.multiple_of(enc * 16, 16), 16), :]

    loads[0].wait()
    loads[1].wait()
    project_queries(hidden, gain, wq, normed, q_out)

    def wait_enc(step, carry):
        enc_copy(step).wait_recv()
        return carry

    lax.fori_loop(1, 8, wait_enc, 0)
    for j in range(32):
        outgoing[j] = columns[send_ref[j]]

    def gen_copy(step):
        peer = (gen + step) % 16
        return send(
            outgoing.at[pl.ds(peer * 2, 2)], incoming.at[pl.ds(gen * 2, 2)], s_gen, step - 1, (enc, peer)
        )

    def start_gen(step, carry):
        gen_copy(step).start()
        return carry

    lax.fori_loop(1, 16, start_gen, 0)
    incoming[pl.ds(gen * 2, 2)] = outgoing[pl.ds(gen * 2, 2)]
    loads[2].wait()
    loads[3].wait()
    project_cotangents(cot, wo, dm_out)

    def wait_gen(step, carry):
        gen_copy(step).wait_recv()
        return carry

    lax.fori_loop(1, 16, wait_gen, 0)
    for j in range(16):
        rows[enc, j * 16 : j * 16 + 16, :] = incoming[receive_ref[j]]

    minus, plus, across = (z + 3) % 4 * 2 + core, (z + 1) % 4 * 2 + core, (z + 2) % 4 * 2 + core
    first, second = pl.ds(0, 128), pl.ds(128, 128)

    def share(ref, sems, number, device):
        return send(ref, ref, sems, number, device)

    up, down, peer = at("z", 1), at("z", 3), at("core", 1)
    ring = [
        share(rows.at[enc], s_ring, 0, up),
        share(rows.at[enc], s_ring, 1, down),
        share(rows.at[minus, first], s_ring, 2, up),
        share(rows.at[plus, second], s_ring, 3, down),
    ]
    cross = [
        share(rows.at[enc], s_core, 0, peer),
        share(rows.at[minus], s_core, 1, peer),
        share(rows.at[plus], s_core, 2, peer),
        share(rows.at[across, first], s_core, 3, peer),
        share(rows.at[across, second], s_core, 4, peer),
    ]
    ring[0].start()
    ring[1].start()
    cross[0].start()
    loads[4].wait()
    loads[5].wait()

    def project(piece):
        k_out[piece] = jnp.dot(rows[piece], wk[...], preferred_element_type=jnp.float32).astype(jnp.bfloat16)
        v_out[piece] = jnp.dot(rows[piece], wv[...], preferred_element_type=jnp.float32).astype(jnp.bfloat16)

    def of_peer(piece):
        return piece + 1 - 2 * core

    project(enc)
    ring[0].wait_recv()
    ring[2].start()
    cross[1].start()
    ring[1].wait_recv()
    ring[3].start()
    cross[2].start()
    cross[0].wait_recv()

    def project_some(pieces):
        def body(i, carry):
            piece = pieces[0]
            for number in range(1, len(pieces)):
                piece = jnp.where(i == number, pieces[number], piece)
            project(piece)
            return carry

        lax.fori_loop(0, len(pieces), body, 0)

    project_some((of_peer(enc), minus, plus))
    ring[2].wait_recv()
    cross[3].start()
    ring[3].wait_recv()
    cross[4].start()
    cross[1].wait_recv()
    cross[2].wait_recv()
    project_some((across, of_peer(minus), of_peer(plus)))
    cross[3].wait_recv()
    cross[4].wait_recv()
    keep = pltpu.make_async_copy(rows, rows_out, rows_sems.at[0])
    keep.start()
    project(of_peer(across))
    keep.wait()

    def drain_gen(step, carry):
        gen_copy(step).wait_send()
        return carry

    def drain_enc(step, carry):
        enc_copy(step).wait_send()
        return carry

    lax.fori_loop(1, 16, drain_gen, 0)
    lax.fori_loop(1, 8, drain_enc, 0)
    for copy in ring + cross:
        copy.wait_send()


def front(send_column, receive_position, encoded, gain, hidden, cot, wq, wo, wk, wv):
    low = jnp.bfloat16
    anywhere = pl.BlockSpec(memory_space=pl.ANY)
    scalars = pl.BlockSpec(memory_space=pltpu.SMEM)
    whole = pl.BlockSpec(memory_space=pltpu.VMEM)
    operands = (hidden, cot, wq, wo, wk, wv)
    return pl.pallas_call(
        front_kernel,
        out_shape=(
            jax.ShapeDtypeStruct((512, 512), low),
            jax.ShapeDtypeStruct((512, 512), low),
            jax.ShapeDtypeStruct((8, 256, 512), low),
            jax.ShapeDtypeStruct((8, 256, 512), low),
            jax.ShapeDtypeStruct((8, 256, 1024), low),
        ),
        in_specs=[scalars] * 2 + [whole] * 2 + [anywhere] * 6,
        out_specs=(whole,) * 4 + (anywhere,),
        scratch_shapes=[pltpu.VMEM(a.shape, low) for a in operands]
        + [
            pltpu.VMEM((512, 4096), low),
            pltpu.VMEM((16, 16, 1024), low),
            pltpu.VMEM((32, 16, 1024), low),
            pltpu.VMEM((32, 16, 1024), low),
            pltpu.VMEM((8, 256, 1024), low),
            pltpu.SemaphoreType.DMA((6,)),
            pltpu.SemaphoreType.DMA((2, 7)),
            pltpu.SemaphoreType.DMA((2, 15)),
            pltpu.SemaphoreType.DMA((2, 4)),
            pltpu.SemaphoreType.DMA((2, 5)),
            pltpu.SemaphoreType.DMA((1,)),
        ],
        compiler_params=pltpu.CompilerParams(
            collective_id=2, has_side_effects=True, vmem_limit_bytes=44 * 1024 * 1024
        ),
    )(send_column, receive_position, encoded, gain.reshape(1, -1), *operands)


def attention_block(b, h, q_ref, dm_ref, k_ref, v_ref, mixed_ref, dk_ref, dv_ref):
    width = 128
    lanes = slice(h * width, h * width + width)
    tokens = pl.ds(pl.multiple_of(b * CH, CH), CH)
    keys = pl.ds(pl.multiple_of(b * 32, 32), 32)
    scale = width ** (-0.5)
    q, dm = q_ref[tokens, lanes], dm_ref[tokens, lanes]
    k, v = k_ref[:, keys, lanes].reshape(256, width), v_ref[:, keys, lanes].reshape(256, width)
    across = (((1,), (1,)), ((), ()))
    raw = lax.dot_general(q, k, across, preferred_element_type=jnp.float32)
    slope = jnp.tanh(raw * (scale / SOFTCAP))
    expo = jnp.exp(SOFTCAP * slope)
    probs = expo / jnp.sum(expo, axis=-1, keepdims=True)
    low = probs.astype(jnp.bfloat16)
    mixed_ref[tokens, lanes] = jnp.dot(low, v, preferred_element_type=jnp.float32).astype(jnp.bfloat16)
    d_probs = lax.dot_general(dm, v, across, preferred_element_type=jnp.float32)
    d_capped = probs * (d_probs - jnp.sum(probs * d_probs, axis=-1, keepdims=True))
    d_raw = (d_capped * (1.0 - slope * slope) * scale).astype(jnp.bfloat16)
    down = (((0,), (0,)), ((), ()))
    d_keys = lax.dot_general(d_raw, q, down, preferred_element_type=jnp.float32)
    d_values = lax.dot_general(low, dm, down, preferred_element_type=jnp.float32)
    dk_ref[:, keys, lanes] = d_keys.astype(jnp.bfloat16).reshape(8, 32, width)
    dv_ref[:, keys, lanes] = d_values.astype(jnp.bfloat16).reshape(8, 32, width)


def attention_kernel(*refs):
    def block(b, carry):
        for h in range(4):
            attention_block(b, h, *refs)
        return carry

    lax.fori_loop(0, 8, block, 0)


def attention(q, dm, k, v):
    whole = pl.BlockSpec(memory_space=pltpu.VMEM)
    return pl.pallas_call(
        attention_kernel,
        out_shape=(
            jax.ShapeDtypeStruct(q.shape, q.dtype),
            jax.ShapeDtypeStruct(k.shape, k.dtype),
            jax.ShapeDtypeStruct(v.shape, v.dtype),
        ),
        in_specs=[whole] * 4,
        out_specs=(whole,) * 3,
        compiler_params=pltpu.CompilerParams(vmem_limit_bytes=24 * 1024 * 1024),
    )(q, dm, k, v)


def local(
    hidden_states,
    grad_out,
    nbr_embed,
    nbr_index,
    gain,
    w_query,
    w_out,
    w_key,
    w_value,
    enc_gain,
    enc_qkv,
    enc_out,
):
    enc_count = lax.axis_size("enc")
    gen_count = lax.axis_size("gen")
    row_index = lax.axis_index("gen")
    per_device, length, enc_width = nbr_embed.shape
    row_size = per_device * enc_count
    capacity = max(2, 2 * row_size // gen_count)
    send_column, column_position, receive_position, position_slot = routing(
        nbr_index, row_index, gen_count, per_device, row_size, capacity
    )
    encoded = encode(nbr_embed, enc_gain, enc_qkv, enc_out)
    queries, d_mixed, keys_all, values_all, slot_rows = front(
        send_column,
        receive_position,
        encoded,
        gain,
        hidden_states,
        grad_out,
        w_query,
        w_out,
        w_key,
        w_value,
    )
    mixed, d_keys, d_values = attention(queries, d_mixed, keys_all, values_all)
    outputs = back(
        position_slot,
        column_position,
        mixed,
        grad_out,
        slot_rows.reshape(row_size * length, enc_width),
        d_keys.reshape(row_size * length, -1),
        d_values.reshape(row_size * length, -1),
        w_key,
        w_value,
    )
    return tuple(output.astype(jnp.float32) for output in outputs)


def solution(mesh):
    return jax.shard_map(
        local,
        mesh=mesh,
        in_specs=(
            P("gen", None),
            P("gen", None),
            P(("enc", "gen"), None, None),
            P(),
            P(),
            P(None, "enc"),
            P("enc", None),
            P(None, "enc"),
            P(None, "enc"),
            P(),
            P(),
            P(),
        ),
        out_specs=(
            P(("enc", "gen"), None, None),
            P("enc", "gen"),
            P("gen", "enc"),
            P("gen", "enc"),
        ),
        check_vma=False,
    )
```

```python
import functools
import types

import jax
import jax.numpy as jnp
from jax import lax
from jax.experimental import pallas as pl
from jax.experimental.pallas import tpu as pltpu
from jax.sharding import PartitionSpec as P

EH = 8
CH = 64
SOFTCAP = 5.0
EPSILON = 1e-06
MESH = pl.DeviceIdType.MESH


def neighbours():
    enc, gen = lax.axis_index("enc"), lax.axis_index("gen")
    z, core, x, y = enc // 2, enc % 2, gen // 4, gen % 4

    def at(axis, step):
        if axis == "x":
            return (enc, (x + step) % 4 * 4 + y)
        if axis == "y":
            return (enc, x * 4 + (y + step) % 4)
        if axis == "z":
            return ((z + step) % 4 * 2 + core, gen)
        return (z * 2 + (1 - core), gen)

    return enc, gen, {"x": x, "y": y, "z": z, "core": core}, at


def send(src, dst, sems, number, device):
    return pltpu.make_async_remote_copy(
        src_ref=src,
        dst_ref=dst,
        send_sem=sems.at[0, number],
        recv_sem=sems.at[1, number],
        device_id=device,
        device_id_type=MESH,
    )


def add_rows(out, out_at, terms, rows, step):
    def body(i, carry):
        total = None
        for ref, at in terms:
            value = ref[pl.ds(pl.multiple_of(at + i * step, step), step), :].astype(jnp.float32)
            total = value if total is None else total + value
        if len(out.shape) == 3:
            out[out_at + i] = total.astype(out.dtype)
        else:
            out[pl.ds(pl.multiple_of(out_at + i * step, step), step), :] = total.astype(out.dtype)
        return carry

    lax.fori_loop(0, rows // step, body, 0)


class Ring:
    def __init__(self, src, buf, sems, axis, where, at):
        self.src, self.buf = src, buf
        self.rows = src.shape[0] // 4
        self.half = self.rows // 2
        self.me = where[axis]
        half = self.half
        self.plus, self.minus = (self.me + 1) % 4, (self.me + 3) % 4
        across = (self.me + 2) % 4
        pieces = (
            (across, 0, 1),
            (self.plus, 1, 1),
            (self.plus, 0, 1),
            (across, 1, 3),
            (self.minus, 0, 3),
            (self.minus, 1, 3),
        )
        self.copies = []
        for number, (chunk, side, step) in enumerate(pieces):
            start = pl.multiple_of(chunk * self.rows + side * half, half)
            self.copies.append(
                send(
                    src.at[pl.ds(start, half), :],
                    buf.at[pl.ds(number * half, half), :],
                    sems,
                    number,
                    at(axis, step),
                )
            )

    def first(self):
        self.copies[0].start()
        self.copies[3].start()

    def second(self):
        self.copies[1].start()
        self.copies[4].start()

    def third(self, step):
        half = self.half
        self.copies[0].wait_recv()
        start = self.plus * self.rows
        add_rows(self.src, start, ((self.src, start), (self.buf, 0)), half, step)
        self.copies[2].start()
        self.copies[3].wait_recv()
        start = self.minus * self.rows + half
        add_rows(self.src, start, ((self.src, start), (self.buf, 3 * half)), half, step)
        self.copies[5].start()

    def last(self, out, out_at, step):
        half = self.half
        for number in (1, 2, 4, 5):
            self.copies[number].wait_recv()
        start = self.me * self.rows
        add_rows(out, out_at, ((self.src, start), (self.buf, 2 * half), (self.buf, 4 * half)), half, step)
        add_rows(
            out, out_at + (half // step if len(out.shape) == 3 else half), ((self.src, start + half), (self.buf, half), (self.buf, 5 * half)), half, step
        )

    def drain(self):
        for copy in self.copies:
            copy.wait_send()


HALVES = 2
DOWN = (((0,), (0,)), ((), ()))
ACROSS = (((1,), (1,)), ((), ()))


def dot(a, b, dims=(((1,), (0,)), ((), ()))):
    return lax.dot_general(a, b, dims, preferred_element_type=jnp.float32)


def loop(low, high, body):
    def step(i, carry):
        body(i)
        return carry

    lax.fori_loop(low, high, step, 0)


def rows_of(start, size):
    return pl.ds(pl.multiple_of(start, size), size)


def normalise(values, gain, out):
    def body(i):
        at = rows_of(i * 16, 16)
        wide = values[at, :].astype(jnp.float32)
        factor = lax.rsqrt(jnp.mean(wide * wide, axis=-1, keepdims=True) + EPSILON)
        out[at, :] = (wide * factor * gain[...]).astype(jnp.bfloat16)

    loop(0, values.shape[0] // 16, body)


def softcapped(q, k):
    scale = q.shape[-1] ** (-0.5)
    slope = jnp.tanh(dot(q, k, ACROSS) * (scale / SOFTCAP))
    expo = jnp.exp(SOFTCAP * slope)
    return slope, expo / jnp.sum(expo, axis=-1, keepdims=True)


def encoder_attention(i, projected, attended):
    at = rows_of(i * 128, 128)
    for h in range(EH):
        q, k, v = (projected[at, part * 1024 + h * 128 : part * 1024 + h * 128 + 128] for part in range(3))
        _, probs = softcapped(q, k)
        attended[at, h * 128 : h * 128 + 128] = dot(probs.astype(jnp.bfloat16), v).astype(jnp.bfloat16)


def pair_refs(b, p, r):
    keys, rows = rows_of(b * 32, 32), rows_of((b * 2 + p) * 128, 128)
    k = r.kv[:, keys, p * 256 : p * 256 + 256].reshape(256, 256)
    v = r.kv[:, keys, 512 + p * 256 : 512 + p * 256 + 256].reshape(256, 256)
    return keys, rows, k, v


def pair_probs(k, q_pair):
    slope = jnp.tanh(dot(k, q_pair, ACROSS) * (128 ** (-0.5) / SOFTCAP))
    expo = jnp.exp(SOFTCAP * slope)
    return slope, expo * (1.0 / jnp.sum(expo, axis=0, keepdims=True))


def attention_forward(b, r, mixed):
    tokens = rows_of(b * CH, CH)
    for p in range(2):
        keys, rows, k, v = pair_refs(b, p, r)
        _, probs = pair_probs(k, r.q_pairs[rows, :])
        both = dot(probs.astype(jnp.bfloat16), v, DOWN).astype(jnp.bfloat16)
        mixed[tokens, p * 256 : p * 256 + 128] = both[0:64, 0:128]
        mixed[tokens, p * 256 + 128 : p * 256 + 256] = both[64:128, 128:256]


def attention_backward(b, r):
    for p in range(2):
        keys, rows, k, v = pair_refs(b, p, r)
        q_pair, dm_pair = r.q_pairs[rows, :], r.dm_pairs[rows, :]
        slope, probs = pair_probs(k, q_pair)
        d_probs = dot(v, dm_pair, ACROSS)
        d_capped = probs * (d_probs - jnp.sum(probs * d_probs, axis=0, keepdims=True))
        d_raw = (d_capped * (1.0 - slope * slope) * 128 ** (-0.5)).astype(jnp.bfloat16)
        d_keys = dot(d_raw, q_pair).astype(jnp.bfloat16)
        d_values = dot(probs.astype(jnp.bfloat16), dm_pair).astype(jnp.bfloat16)
        r.dkv[:, keys, p * 256 : p * 256 + 256] = d_keys.reshape(8, 32, 256)
        r.dkv[:, keys, 512 + p * 256 : 512 + p * 256 + 256] = d_values.reshape(8, 32, 256)


class Exchange:
    def __init__(self, count, copy):
        self.count, self.copy = count, copy

    def start(self):
        loop(1, self.count, lambda step: self.copy(step).start())

    def receive(self):
        loop(1, self.count, lambda step: self.copy(step).wait_recv())

    def drain(self):
        loop(1, self.count, lambda step: self.copy(step).wait_send())


def whole_kernel(tree, *refs):
    r = jax.tree.unflatten(tree, refs)
    r = types.SimpleNamespace(**{name: ref for part in r for name, ref in part.items()})
    r.ringed = types.SimpleNamespace(**r.ringed)

    def load(number):
        src = (r.eo_hbm, r.hidden_hbm, r.wq_hbm, r.cot_hbm, r.wo_hbm, r.wk_hbm, r.wv_hbm)[number]
        w_pair = [r.wkv.at[:, pl.ds(at, 512)] for at in (0, 512)]
        dst = (r.eo, r.hidden, r.wq, r.cot, r.wo, *w_pair)[number]
        return pltpu.make_async_copy(src, dst, r.load_sems.at[number])

    def load_third(third):
        lanes = pl.ds(third * 1024, 1024)
        return pltpu.make_async_copy(r.qkv_hbm.at[:, lanes], r.qkv.at[:, lanes], r.load_sems.at[7 + third])

    for third in range(3):
        load_third(third).start()
    load(0).start()
    enc, gen, where, at = neighbours()
    x, y, z, core = where["x"], where["y"], where["z"], where["core"]
    barrier = pltpu.get_barrier_semaphore()
    loop(1, 16, lambda step: pl.semaphore_signal(barrier, inc=1, device_id=(enc, (gen + step) % 16), device_id_type=MESH))
    loop(1, 8, lambda step: pl.semaphore_signal(barrier, inc=1, device_id=((enc + step) % 8, gen), device_id_type=MESH))

    normalise(r.nbr, r.enc_gain, r.enc_normed)
    for third in range(3):
        load_third(third).wait()
        lanes = slice(third * 1024, third * 1024 + 1024)
        r.projected[:, lanes] = dot(r.enc_normed[...], r.qkv[:, lanes]).astype(jnp.bfloat16)
    for number in range(1, 7):
        load(number).start()
    loop(0, 2, lambda i: encoder_attention(i, r.projected, r.enc_normed))
    load(0).wait()
    for i in range(2):
        rows = slice(i * 128, i * 128 + 128)
        update = dot(r.enc_normed[rows, :], r.eo[...])
        r.encoded[i] = (r.nbr[rows, :].astype(jnp.float32) + update).astype(jnp.bfloat16)
    pl.semaphore_wait(barrier, 22)

    own_rows = rows_of(enc * 16, 16)

    def out_enc(half):
        lanes = pl.ds(half * 512, 512)

        def copy(step):
            peer = (enc + step) % 8
            return send(
                r.encoded.at[:, rows_of(peer * 16, 16), lanes],
                r.columns[half].at[pl.ds(enc * 2, 2)],
                r.s_oenc[half],
                step - 1,
                (peer, gen),
            )

        return Exchange(8, copy)

    def over_gen(half, target, sems):
        def copy(step):
            peer = (gen + step) % 16
            return send(
                r.outgoing[half].at[pl.ds(peer * 2, 2)],
                target[half].at[pl.ds(gen * 2, 2)],
                sems[half],
                step - 1,
                (enc, peer),
            )

        return Exchange(16, copy)

    out_encs = [out_enc(half) for half in range(HALVES)]
    out_gens = [over_gen(half, r.incoming, r.s_ogen) for half in range(HALVES)]
    for half in range(HALVES):
        out_encs[half].start()
    for half in range(HALVES):
        r.columns[half][pl.ds(enc * 2, 2)] = r.encoded[:, own_rows, half * 512 : half * 512 + 512]

    def start_out_gen(half):
        out_encs[half].receive()
        for j in range(32):
            r.outgoing[half][j] = r.columns[half][r.send[j]]
        out_gens[half].start()
        own = pl.ds(gen * 2, 2)
        r.incoming[half][own] = r.outgoing[half][own]

    def store_pairs(out, i, low):
        for block in range(4):
            for head in range(4):
                start = i * 1024 + block * 256 + head // 2 * 128 + head % 2 * 64
                out[rows_of(start, 64), head % 2 * 128 : head % 2 * 128 + 128] = low[
                    block * 64 : block * 64 + 64, head * 128 : head * 128 + 128
                ]

    def query_tile(i):
        low = dot(r.hidden[rows_of(i * 256, 256), :], r.wq[...]).astype(jnp.bfloat16)
        store_pairs(r.q_pairs, i, low)

    def cotangent_tile(i):
        low = dot(r.cot[rows_of(i * 256, 256), :], r.wo[...], ACROSS).astype(jnp.bfloat16)
        store_pairs(r.dm_pairs, i, low)

    r.q_pairs[...] = jnp.zeros_like(r.q_pairs)
    r.dm_pairs[...] = jnp.zeros_like(r.dm_pairs)
    load(1).wait()
    normalise(r.hidden, r.gain, r.hidden)
    load(2).wait()
    start_out_gen(0)
    loop(0, 1, query_tile)
    start_out_gen(1)
    loop(1, 2, query_tile)
    load(3).wait()
    load(4).wait()
    loop(0, 2, cotangent_tile)

    minus, plus, across = (z + 3) % 4 * 2 + core, (z + 1) % 4 * 2 + core, (z + 2) % 4 * 2 + core
    up, down, peer = at("z", 1), at("z", 3), at("core", 1)
    rings, crosses = [], []
    for half in range(HALVES):
        rows = r.rows.at[:, :, pl.ds(half * 512, 512)]
        first, second = pl.ds(0, 128), pl.ds(128, 128)

        def share(ref, sems, number, device):
            return send(ref, ref, sems, number, device)

        rings.append(
            [
                share(rows.at[enc], r.s_ring[half], 0, up),
                share(rows.at[enc], r.s_ring[half], 1, down),
                share(rows.at[minus, first], r.s_ring[half], 2, up),
                share(rows.at[plus, second], r.s_ring[half], 3, down),
            ]
        )
        crosses.append(
            [
                share(rows.at[enc], r.s_cross[half], 0, peer),
                share(rows.at[minus], r.s_cross[half], 1, peer),
                share(rows.at[plus], r.s_cross[half], 2, peer),
                share(rows.at[across, first], r.s_cross[half], 3, peer),
                share(rows.at[across, second], r.s_cross[half], 4, peer),
            ]
        )

    def take_slots(half):
        out_gens[half].receive()
        for j in range(16):
            r.rows[enc, j * 16 : j * 16 + 16, half * 512 : half * 512 + 512] = r.incoming[half][r.receive[j]]

    def gather_own(half):
        rings[half][0].start()
        rings[half][1].start()
        crosses[half][0].start()

    def gather_next(half):
        rings[half][0].wait_recv()
        rings[half][2].start()
        crosses[half][1].start()
        rings[half][1].wait_recv()
        rings[half][3].start()
        crosses[half][2].start()

    def gather_last(half):
        rings[half][2].wait_recv()
        crosses[half][3].start()
        rings[half][3].wait_recv()
        crosses[half][4].start()

    def of_peer(piece):
        return piece + 1 - 2 * core

    def project(piece):
        r.kv[piece] = dot(r.rows[piece], r.wkv[...]).astype(jnp.bfloat16)

    def project_some(pieces):
        def body(i):
            piece = pieces[0]
            for number in range(1, len(pieces)):
                piece = jnp.where(i == number, pieces[number], piece)
            project(piece)

        loop(0, len(pieces), body)

    load(5).wait()
    load(6).wait()
    take_slots(0)
    gather_own(0)
    take_slots(1)
    gather_next(0)
    gather_own(1)
    gather_last(0)
    crosses[1][0].wait_recv()
    crosses[0][0].wait_recv()
    project_some((enc, of_peer(enc)))
    gather_next(1)
    for number in (1, 2):
        crosses[0][number].wait_recv()
    project_some((minus, plus))
    for number in (1, 2):
        crosses[1][number].wait_recv()
    project_some((of_peer(minus), of_peer(plus)))
    gather_last(1)
    for number in (3, 4):
        crosses[0][number].wait_recv()
        crosses[1][number].wait_recv()
    project_some((across, of_peer(across)))

    ot_a, ot_b = r.wq.at[:, pl.ds(0, 256)], r.wq.at[:, pl.ds(256, 256)]
    kt, vt = r.eo.at[:, pl.ds(0, 512)], r.eo.at[:, pl.ds(512, 512)]
    mixed, mixed_t = r.hidden.at[:, pl.ds(0, 512)], r.hidden.at[:, pl.ds(512, 512)]
    ring_oa = Ring(ot_a, r.ringed.ota[0], r.ringed.ota[1], "x", where, at)
    ring_ob = Ring(ot_b, r.ringed.otb[0], r.ringed.otb[1], "y", where, at)
    ring_k = Ring(kt, r.ringed.kt[0], r.ringed.kt[1], "x", where, at)
    ring_v = Ring(vt, r.ringed.vt[0], r.ringed.vt[1], "y", where, at)
    ring_oa2 = Ring(r.ot_a2, r.ringed.ota2[0], r.ringed.ota2[1], "y", where, at)
    ring_ob2 = Ring(r.ot_b2, r.ringed.otb2[0], r.ringed.otb2[1], "x", where, at)
    ring_k2 = Ring(r.kt2, r.ringed.kt2[0], r.ringed.kt2[1], "y", where, at)
    ring_v2 = Ring(r.vt2, r.ringed.vt2[0], r.ringed.vt2[1], "x", where, at)
    mine = [r.qkv.at[:, pl.ds(half * 512, 512)] for half in range(HALVES)]
    peers = [r.qkv.at[:, pl.ds(1024 + half * 512, 512)] for half in range(HALVES)]
    from_peer = [r.qkv.at[:, pl.ds(2048 + half * 512, 512)] for half in range(HALVES)]
    ring_z = [Ring(mine[half], r.ring_z[half][0], r.ring_z[half][1], "z", where, at) for half in range(HALVES)]

    loop(0, 8, lambda b: attention_forward(b, r, mixed))
    mixed_t[...] = mixed[...].T

    def out_terms(i):
        to_x, to_y = (x + 2 - i + 4) % 4, (y + 2 - i + 4) % 4

        def tile(j):
            lane_a = pl.multiple_of((to_x * 4 + j) * 256, 256)
            term = dot(mixed_t[0:256, :], r.cot[:, pl.ds(lane_a, 256)])
            ot_a[pl.ds(lane_a, 256), :] = term.astype(jnp.bfloat16)
            lane_b = pl.multiple_of((j * 4 + to_y) * 256, 256)
            term = dot(mixed_t[256:512, :], r.cot[:, pl.ds(lane_b, 256)])
            ot_b[rows_of((to_y * 4 + j) * 256, 256), :] = term.astype(jnp.bfloat16)

        loop(0, 4, tile)

        @pl.when(i == 0)
        def _():
            ring_oa.first()
            ring_ob.first()

    loop(0, 4, out_terms)
    ring_oa.second()
    ring_ob.second()
    loop(0, 8, lambda b: attention_backward(b, r))
    ring_oa.third(64)
    ring_ob.third(64)

    core_copies = [
        [
            send(
                peers[half].at[pl.ds(k * 256, 256), :],
                from_peer[half].at[pl.ds(k * 256, 256), :],
                r.s_core[half],
                k,
                peer,
            )
            for k in range(4)
        ]
        for half in range(HALVES)
    ]

    def enc_piece(half, piece_at, out, out_at):
        feats = slice(half * 512, half * 512 + 512)
        term = dot(r.dkv[piece_at], r.wkv[feats, :], ACROSS)
        out[rows_of(out_at, 256), :] = term.astype(jnp.bfloat16)

    def enc_half(half):
        def to_peer(k):
            enc_piece(half, k * 2 + (1 - core), peers[half], k * 256)
            for number in range(4):

                @pl.when(k == number)
                def _():
                    core_copies[half][number].start()

        loop(0, 4, to_peer)
        loop(0, 4, lambda k: enc_piece(half, k * 2 + core, mine[half], k * 256))
        for k in range(4):
            core_copies[half][k].wait_recv()
        add_rows(mine[half], 0, ((mine[half], 0), (from_peer[half], 0)), 1024, 64)
        ring_z[half].first()
        ring_z[half].second()

    def key_terms(part):
        lanes = pl.ds(pl.multiple_of(part * 128, 128), 128)
        term = dot(r.rows[:, :, lanes].reshape(2048, 128), r.dkv[...].reshape(2048, 1024), DOWN)
        low = term.astype(jnp.bfloat16)
        kt[rows_of(part * 128, 128), :] = low[:, 0:512]
        for side in range(2):
            to_x, to_y = (part * 2 + side) // 4, (part * 2 + side) % 4
            vt[rows_of(to_y * 256 + to_x * 64, 64), :] = low[side * 64 : side * 64 + 64, 512:1024]

    enc_half(0)
    enc_half(1)
    loop(0, 4, key_terms)
    ring_z[0].third(64)
    loop(4, 8, key_terms)
    ring_k.first()
    ring_v.first()
    ring_k.second()
    ring_v.second()

    back_gens = [over_gen(half, r.returned, r.s_bgen) for half in range(HALVES)]

    def start_back_gen(half):
        ring_z[half].last(r.piece[half], 0, 16)
        out_gens[half].drain()
        for j in range(32):
            r.outgoing[half][j] = r.piece[half][r.position[j]]
        back_gens[half].start()
        own = pl.ds(gen * 2, 2)
        r.returned[half][own] = r.outgoing[half][own]

    def back_enc(half):
        def copy(step):
            to = (enc + step) % 8
            return send(
                r.grads[half].at[to],
                r.home.at[:, own_rows, pl.ds(half * 512, 512)],
                r.s_benc[half],
                step - 1,
                (to, gen),
            )

        return Exchange(8, copy)

    back_encs = [back_enc(half) for half in range(HALVES)]

    def start_back_enc(half):
        back_gens[half].receive()
        for j in range(16):
            r.grads[half][j // 2, j % 2] = r.returned[half][r.column[j]]
        back_encs[half].start()
        r.home[:, own_rows, half * 512 : half * 512 + 512] = r.grads[half][enc]

    start_back_gen(0)
    ring_z[1].third(64)
    ring_oa.last(r.ot_a2, 0, 64)
    ring_oa2.first()
    ring_oa2.second()
    ring_ob.last(r.ot_b2, 0, 64)
    ring_ob2.first()
    ring_ob2.second()
    ring_k.third(64)
    ring_v.third(64)
    ring_oa2.third(64)
    ring_ob2.third(64)
    start_back_gen(1)
    ring_k.last(r.kt2, 0, 64)
    ring_k2.first()
    ring_k2.second()
    ring_v.last(r.vt2, 0, 64)
    ring_v2.first()
    ring_v2.second()
    start_back_enc(0)
    ring_oa2.last(r.wo_out, 0, 64)
    ring_ob2.last(r.wo_out, 256, 64)
    ring_k2.third(32)
    ring_v2.third(32)
    start_back_enc(1)
    ring_k2.last(r.wk_out, 0, 32)
    ring_v2.last(r.wv_out, 0, 32)
    for half in range(HALVES):
        back_encs[half].receive()
    r.enc_out[...] = r.home[...]

    rings_all = [ring_oa, ring_ob, ring_k, ring_v, ring_oa2, ring_ob2, ring_k2, ring_v2] + ring_z
    for ring in rings_all:
        ring.drain()
    for half in range(HALVES):
        for copy in core_copies[half] + rings[half] + crosses[half]:
            copy.wait_send()
        for exchange in (out_encs[half], back_gens[half], back_encs[half]):
            exchange.drain()


def whole(tables, nbr, enc_gain, gain, qkv, eo, hidden, cot, wq, wo, wk, wv):
    low = jnp.bfloat16
    vmem = lambda *shape: pltpu.VMEM(shape, low)
    sems = lambda *shape: pltpu.SemaphoreType.DMA(shape)
    both = lambda make, *shape: [make(*shape) for _ in range(HALVES)]
    ring = lambda count, width: [vmem(count // 4 * 3, width), sems(2, 6)]
    anywhere = pl.BlockSpec(memory_space=pl.ANY)
    scalars = pl.BlockSpec(memory_space=pltpu.SMEM)
    local = pl.BlockSpec(memory_space=pltpu.VMEM)
    send_table, position_table, receive_table, column_table = tables
    small = dict(send=send_table, position=position_table, receive=receive_table, column=column_table)
    near = dict(nbr=nbr.reshape(256, 1024), enc_gain=enc_gain.reshape(1, -1), gain=gain.reshape(1, -1))
    big = dict(
        qkv_hbm=qkv, eo_hbm=eo, hidden_hbm=hidden, wq_hbm=wq, cot_hbm=cot, wo_hbm=wo, wk_hbm=wk, wv_hbm=wv
    )
    outputs = dict(
        enc_out=jax.ShapeDtypeStruct((2, 128, 1024), low),
        wo_out=jax.ShapeDtypeStruct((512, 256), low),
        wk_out=jax.ShapeDtypeStruct((64, 512), low),
        wv_out=jax.ShapeDtypeStruct((64, 512), low),
    )
    scratch = dict(
        qkv=vmem(1024, 3072),
        eo=vmem(1024, 1024),
        hidden=vmem(512, 4096),
        wq=vmem(4096, 512),
        cot=vmem(512, 4096),
        wo=vmem(512, 4096),
        wkv=vmem(1024, 1024),
        enc_normed=vmem(256, 1024),
        projected=vmem(256, 3072),
        encoded=vmem(2, 128, 1024),
        q_pairs=vmem(2048, 256),
        dm_pairs=vmem(2048, 256),
        kv=vmem(8, 256, 1024),
        dkv=vmem(8, 256, 1024),
        rows=vmem(8, 256, 1024),
        ot_a2=vmem(1024, 256),
        ot_b2=vmem(1024, 256),
        kt2=vmem(256, 512),
        vt2=vmem(256, 512),
        home=vmem(2, 128, 1024),
        ringed=dict(
            ota=ring(4096, 256),
            otb=ring(4096, 256),
            kt=ring(1024, 512),
            vt=ring(1024, 512),
            ota2=ring(1024, 256),
            otb2=ring(1024, 256),
            kt2=ring(256, 512),
            vt2=ring(256, 512),
        ),
        ring_z=both(ring, 1024, 512),
        columns=both(vmem, 16, 16, 512),
        outgoing=both(vmem, 32, 16, 512),
        incoming=both(vmem, 32, 16, 512),
        returned=both(vmem, 32, 16, 512),
        piece=both(vmem, 16, 16, 512),
        grads=both(vmem, 8, 2, 16, 512),
        s_oenc=both(sems, 2, 7),
        s_benc=both(sems, 2, 7),
        s_ogen=both(sems, 2, 15),
        s_bgen=both(sems, 2, 15),
        s_ring=both(sems, 2, 4),
        s_cross=both(sems, 2, 5),
        s_core=both(sems, 2, 4),
        load_sems=sems(10),
    )
    operands = small | near | big
    leaves, _ = jax.tree.flatten(scratch)
    tree = jax.tree.structure((operands, outputs, scratch))
    by_name = lambda part: [part[name] for name in sorted(part)]
    place = dict.fromkeys(small, scalars) | dict.fromkeys(near, local) | dict.fromkeys(big, anywhere)
    return pl.pallas_call(
        functools.partial(whole_kernel, tree),
        name="retro_whole",
        out_shape=tuple(by_name(outputs)),
        in_specs=by_name(place),
        out_specs=(local,) * len(outputs),
        scratch_shapes=leaves,
        compiler_params=pltpu.CompilerParams(
            collective_id=1, has_side_effects=True, vmem_limit_bytes=61 * 1024 * 1024
        ),
    )(*by_name(operands))


def widen_kernel(*refs):
    sources, targets, near, sems = refs[:4], refs[4:8], refs[8:12], refs[12]
    copies = [
        pltpu.make_async_copy(src, dst, sems.at[number]) for number, (src, dst) in enumerate(zip(sources, near))
    ]
    for copy in copies:
        copy.start()
    for copy, src, dst in zip(copies, near, targets):
        copy.wait()
        dst[...] = src[...].astype(jnp.float32)


def widen(values):
    return pl.pallas_call(
        widen_kernel,
        name="widen",
        out_shape=tuple(jax.ShapeDtypeStruct(value.shape, jnp.float32) for value in values),
        in_specs=[pl.BlockSpec(memory_space=pl.ANY)] * 4,
        out_specs=(pl.BlockSpec(memory_space=pltpu.VMEM),) * 4,
        scratch_shapes=[pltpu.VMEM(value.shape, value.dtype) for value in values] + [pltpu.SemaphoreType.DMA((4,))],
        compiler_params=pltpu.CompilerParams(vmem_limit_bytes=8 * 1024 * 1024),
    )(*values)


def routing(nbr_index, row_index, gen_count, per_device, row_size, capacity):
    entries = nbr_index.reshape(gen_count, row_size)
    source = entries // per_device % gen_count
    column = entries // (per_device * gen_count) * per_device + entries % per_device
    places = jnp.arange(row_size, dtype=jnp.int32)
    same = (source[:, :, None] == source[:, None, :]) & (places[None, None, :] < places[None, :, None])
    rank = jnp.sum(same.astype(jnp.int32), axis=2)
    rows = jnp.arange(gen_count, dtype=jnp.int32)
    send_slot = (rows[:, None] * capacity + rank).reshape(-1)
    mine = (source == row_index).reshape(-1)
    flat_column = column.reshape(-1)
    buffers = jnp.arange(gen_count * capacity, dtype=jnp.int32)
    send_match = (send_slot[:, None] == buffers[None, :]) & mine[:, None]
    send_column = jnp.sum(jnp.where(send_match, flat_column[:, None], 0), axis=0)
    column_match = (flat_column[:, None] == places[None, :]) & mine[:, None]
    column_position = jnp.sum(jnp.where(column_match, send_slot[:, None], 0), axis=0)
    own = (rows == row_index)[:, None]
    receive_position = jnp.sum(jnp.where(own, source * capacity + rank, 0), axis=0)
    receive_match = receive_position[:, None] == buffers[None, :]
    position_slot = jnp.sum(jnp.where(receive_match, places[:, None], 0), axis=0)
    return (send_column, position_slot, receive_position, column_position)


def local(
    hidden_states,
    grad_out,
    nbr_embed,
    nbr_index,
    gain,
    w_query,
    w_out,
    w_key,
    w_value,
    enc_gain,
    enc_qkv,
    enc_out,
):
    gen_count = lax.axis_size("gen")
    per_device = nbr_embed.shape[0]
    row_size = per_device * lax.axis_size("enc")
    capacity = max(2, 2 * row_size // gen_count)
    tables = routing(nbr_index, lax.axis_index("gen"), gen_count, per_device, row_size, capacity)
    grad_encoded, grad_key, grad_out_proj, grad_value = (
        whole(
            tables,
            nbr_embed,
            enc_gain,
            gain,
            enc_qkv,
            enc_out,
            hidden_states,
            grad_out,
            w_query,
            w_out,
            w_key,
            w_value,
        )
    )
    return widen((grad_encoded, grad_out_proj, grad_key, grad_value))


def solution(mesh):
    return jax.shard_map(
        local,
        mesh=mesh,
        in_specs=(
            P("gen", None),
            P("gen", None),
            P(("enc", "gen"), None, None),
            P(),
            P(),
            P(None, "enc"),
            P("enc", None),
            P(None, "enc"),
            P(None, "enc"),
            P(),
            P(),
            P(),
        ),
        out_specs=(
            P(("enc", "gen"), None, None),
            P("enc", "gen"),
            P("gen", "enc"),
            P("gen", "enc"),
        ),
        check_vma=False,
    )
```

```python
import functools
import types

import jax
import jax.numpy as jnp
from jax import lax
from jax.experimental import pallas as pl
from jax.experimental.pallas import tpu as pltpu
from jax.sharding import PartitionSpec as P

EH = 8
CH = 64
SOFTCAP = 5.0
EPSILON = 1e-06
MESH = pl.DeviceIdType.MESH


def neighbours():
    enc, gen = lax.axis_index("enc"), lax.axis_index("gen")
    z, core, x, y = enc // 2, enc % 2, gen // 4, gen % 4

    def at(axis, step):
        if axis == "x":
            return (enc, (x + step) % 4 * 4 + y)
        if axis == "y":
            return (enc, x * 4 + (y + step) % 4)
        if axis == "z":
            return ((z + step) % 4 * 2 + core, gen)
        return (z * 2 + (1 - core), gen)

    return enc, gen, {"x": x, "y": y, "z": z, "core": core}, at


def send(src, dst, sems, number, device):
    return pltpu.make_async_remote_copy(
        src_ref=src,
        dst_ref=dst,
        send_sem=sems.at[0, number],
        recv_sem=sems.at[1, number],
        device_id=device,
        device_id_type=MESH,
    )


def add_rows(out, out_at, terms, rows, step):
    def body(i, carry):
        total = None
        for ref, at in terms:
            value = ref[pl.ds(pl.multiple_of(at + i * step, step), step), :].astype(jnp.float32)
            total = value if total is None else total + value
        if len(out.shape) == 3:
            out[out_at + i] = total.astype(out.dtype)
        else:
            out[pl.ds(pl.multiple_of(out_at + i * step, step), step), :] = total.astype(out.dtype)
        return carry

    lax.fori_loop(0, rows // step, body, 0)


class Ring:
    def __init__(self, src, buf, sems, axis, where, at):
        self.src, self.buf = src, buf
        self.rows = src.shape[0] // 4
        self.half = self.rows // 2
        self.me = where[axis]
        half = self.half
        self.plus, self.minus = (self.me + 1) % 4, (self.me + 3) % 4
        across = (self.me + 2) % 4
        pieces = (
            (across, 0, 1),
            (self.plus, 1, 1),
            (self.plus, 0, 1),
            (across, 1, 3),
            (self.minus, 0, 3),
            (self.minus, 1, 3),
        )
        self.copies = []
        for number, (chunk, side, step) in enumerate(pieces):
            start = pl.multiple_of(chunk * self.rows + side * half, half)
            self.copies.append(
                send(
                    src.at[pl.ds(start, half), :],
                    buf.at[pl.ds(number * half, half), :],
                    sems,
                    number,
                    at(axis, step),
                )
            )

    def first(self):
        self.copies[0].start()
        self.copies[3].start()

    def second(self):
        self.copies[1].start()
        self.copies[4].start()

    def third(self, step, with_second=False):
        half = self.half
        self.copies[0].wait_recv()
        if with_second:
            self.copies[3].wait_recv()
            self.second()
        start = self.plus * self.rows
        add_rows(self.src, start, ((self.src, start), (self.buf, 0)), half, step)
        self.copies[2].start()
        if not with_second:
            self.copies[3].wait_recv()
        start = self.minus * self.rows + half
        add_rows(self.src, start, ((self.src, start), (self.buf, 3 * half)), half, step)
        self.copies[5].start()

    def last(self, out, out_at, step):
        half = self.half
        for number in (1, 2, 4, 5):
            self.copies[number].wait_recv()
        start = self.me * self.rows
        add_rows(out, out_at, ((self.src, start), (self.buf, 2 * half), (self.buf, 4 * half)), half, step)
        add_rows(
            out, out_at + (half // step if len(out.shape) == 3 else half), ((self.src, start + half), (self.buf, half), (self.buf, 5 * half)), half, step
        )

    def drain(self):
        for copy in self.copies:
            copy.wait_send()


HALVES = 2
DOWN = (((0,), (0,)), ((), ()))
ACROSS = (((1,), (1,)), ((), ()))


def dot(a, b, dims=(((1,), (0,)), ((), ()))):
    return lax.dot_general(a, b, dims, preferred_element_type=jnp.float32)


def loop(low, high, body):
    def step(i, carry):
        body(i)
        return carry

    lax.fori_loop(low, high, step, 0)


def rows_of(start, size):
    return pl.ds(pl.multiple_of(start, size), size)


def normalise(values, gain, out):
    def body(i):
        at = rows_of(i * 16, 16)
        wide = values[at, :].astype(jnp.float32)
        factor = lax.rsqrt(jnp.mean(wide * wide, axis=-1, keepdims=True) + EPSILON)
        out[at, :] = (wide * factor * gain[...]).astype(jnp.bfloat16)

    loop(0, values.shape[0] // 16, body)


def softcapped(q, k):
    scale = q.shape[-1] ** (-0.5)
    slope = jnp.tanh(dot(q, k, ACROSS) * (scale / SOFTCAP))
    expo = jnp.exp(SOFTCAP * slope)
    return slope, expo / jnp.sum(expo, axis=-1, keepdims=True)


def encoder_attention(i, projected, attended):
    at = rows_of(i * 128, 128)
    for h in range(EH):
        q, k, v = (projected[at, part * 1024 + h * 128 : part * 1024 + h * 128 + 128] for part in range(3))
        _, probs = softcapped(q, k)
        attended[at, h * 128 : h * 128 + 128] = dot(probs.astype(jnp.bfloat16), v).astype(jnp.bfloat16)


def pair_refs(b, p, r):
    keys, rows = rows_of(b * 32, 32), rows_of((b * 2 + p) * 128, 128)
    k = r.kv[:, keys, p * 256 : p * 256 + 256].reshape(256, 256)
    v = r.kv[:, keys, 512 + p * 256 : 512 + p * 256 + 256].reshape(256, 256)
    return keys, rows, k, v


def pair_probs(k, q_pair):
    slope = jnp.tanh(dot(k, q_pair, ACROSS) * (128 ** (-0.5) / SOFTCAP))
    expo = jnp.exp(SOFTCAP * slope)
    return slope, expo * (1.0 / jnp.sum(expo, axis=0, keepdims=True))


def attention_forward(b, r, mixed):
    tokens = rows_of(b * CH, CH)
    for p in range(2):
        keys, rows, k, v = pair_refs(b, p, r)
        _, probs = pair_probs(k, r.q_pairs[rows, :])
        both = dot(probs.astype(jnp.bfloat16), v, DOWN).astype(jnp.bfloat16)
        mixed[tokens, p * 256 : p * 256 + 128] = both[0:64, 0:128]
        mixed[tokens, p * 256 + 128 : p * 256 + 256] = both[64:128, 128:256]


def attention_backward(b, r):
    for p in range(2):
        keys, rows, k, v = pair_refs(b, p, r)
        q_pair, dm_pair = r.q_pairs[rows, :], r.dm_pairs[rows, :]
        slope, probs = pair_probs(k, q_pair)
        d_probs = dot(v, dm_pair, ACROSS)
        d_capped = probs * (d_probs - jnp.sum(probs * d_probs, axis=0, keepdims=True))
        d_raw = (d_capped * (1.0 - slope * slope) * 128 ** (-0.5)).astype(jnp.bfloat16)
        d_keys = dot(d_raw, q_pair).astype(jnp.bfloat16)
        d_values = dot(probs.astype(jnp.bfloat16), dm_pair).astype(jnp.bfloat16)
        r.dkv[:, keys, p * 256 : p * 256 + 256] = d_keys.reshape(8, 32, 256)
        r.dkv[:, keys, 512 + p * 256 : 512 + p * 256 + 256] = d_values.reshape(8, 32, 256)


class Exchange:
    def __init__(self, count, copy):
        self.count, self.copy = count, copy

    def start(self):
        loop(1, self.count, lambda step: self.copy(step).start())

    def receive(self):
        loop(1, self.count, lambda step: self.copy(step).wait_recv())

    def drain(self):
        loop(1, self.count, lambda step: self.copy(step).wait_send())


def whole_kernel(tree, *refs):
    r = jax.tree.unflatten(tree, refs)
    r = types.SimpleNamespace(**{name: ref for part in r for name, ref in part.items()})
    r.ringed = types.SimpleNamespace(**r.ringed)

    def load(number):
        src = (r.eo_hbm, r.hidden_hbm, r.wq_hbm, r.cot_hbm, r.wo_hbm, r.wk_hbm, r.wv_hbm)[number]
        w_pair = [r.wkv.at[:, pl.ds(at, 512)] for at in (0, 512)]
        dst = (r.eo, r.hidden, r.wq, r.cot, r.wo, *w_pair)[number]
        return pltpu.make_async_copy(src, dst, r.load_sems.at[number])

    def load_third(third):
        lanes = pl.ds(third * 1024, 1024)
        return pltpu.make_async_copy(r.qkv_hbm.at[:, lanes], r.qkv.at[:, lanes], r.load_sems.at[7 + third])

    for third in range(3):
        load_third(third).start()
    load(0).start()
    enc, gen, where, at = neighbours()
    x, y, z, core = where["x"], where["y"], where["z"], where["core"]
    barrier = pltpu.get_barrier_semaphore()
    loop(1, 16, lambda step: pl.semaphore_signal(barrier, inc=1, device_id=(enc, (gen + step) % 16), device_id_type=MESH))
    loop(1, 8, lambda step: pl.semaphore_signal(barrier, inc=1, device_id=((enc + step) % 8, gen), device_id_type=MESH))

    normalise(r.nbr, r.enc_gain, r.enc_normed)
    for third in range(3):
        load_third(third).wait()
        lanes = slice(third * 1024, third * 1024 + 1024)
        r.projected[:, lanes] = dot(r.enc_normed[...], r.qkv[:, lanes]).astype(jnp.bfloat16)
    for number in range(1, 7):
        load(number).start()
    loop(0, 2, lambda i: encoder_attention(i, r.projected, r.enc_normed))
    load(0).wait()

    def finish(half):
        lanes = slice(half * 512, half * 512 + 512)
        update = dot(r.enc_normed[...], r.eo[:, lanes])
        low = (r.nbr[:, lanes].astype(jnp.float32) + update).astype(jnp.bfloat16)
        r.encoded[:, :, lanes] = low.reshape(2, 128, 512)

    finish(0)
    pl.semaphore_wait(barrier, 22)

    own_rows = rows_of(enc * 16, 16)

    def out_enc(half):
        lanes = pl.ds(half * 512, 512)

        def copy(step):
            peer = (enc + step) % 8
            return send(
                r.encoded.at[:, rows_of(peer * 16, 16), lanes],
                r.columns[half].at[pl.ds(enc * 2, 2)],
                r.s_oenc[half],
                step - 1,
                (peer, gen),
            )

        return Exchange(8, copy)

    def over_gen(half, target, sems):
        def copy(step):
            peer = (gen + step) % 16
            return send(
                r.outgoing[half].at[pl.ds(peer * 2, 2)],
                target[half].at[pl.ds(gen * 2, 2)],
                sems[half],
                step - 1,
                (enc, peer),
            )

        return Exchange(16, copy)

    out_encs = [out_enc(half) for half in range(HALVES)]
    out_gens = [over_gen(half, r.incoming, r.s_ogen) for half in range(HALVES)]
    out_encs[0].start()
    finish(1)
    for half in range(HALVES):
        r.columns[half][pl.ds(enc * 2, 2)] = r.encoded[:, own_rows, half * 512 : half * 512 + 512]

    def pick_out_gen(half):
        for j in range(32):
            r.outgoing[half][j] = r.columns[half][r.send[j]]
        own = pl.ds(gen * 2, 2)
        r.incoming[half][own] = r.outgoing[half][own]

    def store_pairs(out, i, low):
        for block in range(4):
            for head in range(4):
                start = i * 1024 + block * 256 + head // 2 * 128 + head % 2 * 64
                out[rows_of(start, 64), head % 2 * 128 : head % 2 * 128 + 128] = low[
                    block * 64 : block * 64 + 64, head * 128 : head * 128 + 128
                ]

    def query_tile(i):
        low = dot(r.hidden[rows_of(i * 256, 256), :], r.wq[...]).astype(jnp.bfloat16)
        store_pairs(r.q_pairs, i, low)

    def cotangent_tile(i):
        low = dot(r.cot[rows_of(i * 256, 256), :], r.wo[...], ACROSS).astype(jnp.bfloat16)
        store_pairs(r.dm_pairs, i, low)

    r.q_pairs[...] = jnp.zeros_like(r.q_pairs)
    r.dm_pairs[...] = jnp.zeros_like(r.dm_pairs)
    out_encs[0].receive()
    out_encs[1].start()
    pick_out_gen(0)
    out_gens[0].start()
    load(1).wait()
    normalise(r.hidden, r.gain, r.hidden)
    load(2).wait()
    loop(0, 2, query_tile)
    out_encs[1].receive()
    pick_out_gen(1)
    load(3).wait()
    load(4).wait()

    minus, plus, across = (z + 3) % 4 * 2 + core, (z + 1) % 4 * 2 + core, (z + 2) % 4 * 2 + core
    up, down, peer = at("z", 1), at("z", 3), at("core", 1)
    rings, crosses = [], []
    for half in range(HALVES):
        rows = r.rows.at[:, :, pl.ds(half * 512, 512)]
        first, second = pl.ds(0, 128), pl.ds(128, 128)

        def share(ref, sems, number, device):
            return send(ref, ref, sems, number, device)

        rings.append(
            [
                share(rows.at[enc], r.s_ring[half], 0, up),
                share(rows.at[enc], r.s_ring[half], 1, down),
                share(rows.at[minus, first], r.s_ring[half], 2, up),
                share(rows.at[plus, second], r.s_ring[half], 3, down),
            ]
        )
        crosses.append(
            [
                share(rows.at[enc], r.s_cross[half], 0, peer),
                share(rows.at[minus], r.s_cross[half], 1, peer),
                share(rows.at[plus], r.s_cross[half], 2, peer),
                share(rows.at[across, first], r.s_cross[half], 3, peer),
                share(rows.at[across, second], r.s_cross[half], 4, peer),
            ]
        )

    def take_slots(half):
        out_gens[half].receive()
        for j in range(16):
            r.rows[enc, j * 16 : j * 16 + 16, half * 512 : half * 512 + 512] = r.incoming[half][r.receive[j]]

    def gather_own(half):
        rings[half][0].start()
        rings[half][1].start()
        crosses[half][0].start()

    def gather_next(half):
        rings[half][0].wait_recv()
        rings[half][2].start()
        crosses[half][1].start()
        rings[half][1].wait_recv()
        rings[half][3].start()
        crosses[half][2].start()

    def gather_last(half):
        rings[half][2].wait_recv()
        crosses[half][3].start()
        rings[half][3].wait_recv()
        crosses[half][4].start()

    def of_peer(piece):
        return piece + 1 - 2 * core

    def project(piece):
        r.kv[piece] = dot(r.rows[piece], r.wkv[...]).astype(jnp.bfloat16)

    def project_some(pieces):
        def body(i):
            piece = pieces[0]
            for number in range(1, len(pieces)):
                piece = jnp.where(i == number, pieces[number], piece)
            project(piece)

        loop(0, len(pieces), body)

    load(5).wait()
    load(6).wait()
    take_slots(0)
    out_gens[1].start()
    gather_own(0)
    loop(0, 2, cotangent_tile)
    gather_next(0)
    gather_last(0)
    take_slots(1)
    gather_own(1)
    crosses[1][0].wait_recv()
    crosses[0][0].wait_recv()
    project_some((enc, of_peer(enc)))
    gather_next(1)
    for number in (1, 2):
        crosses[0][number].wait_recv()
    project_some((minus, plus))
    for number in (1, 2):
        crosses[1][number].wait_recv()
    project_some((of_peer(minus), of_peer(plus)))
    gather_last(1)
    for number in (3, 4):
        crosses[0][number].wait_recv()
        crosses[1][number].wait_recv()
    project_some((across, of_peer(across)))

    ot_a, ot_b = r.wq.at[:, pl.ds(0, 256)], r.wq.at[:, pl.ds(256, 256)]
    kt, vt = r.eo.at[:, pl.ds(0, 512)], r.eo.at[:, pl.ds(512, 512)]
    mixed, mixed_t = r.hidden.at[:, pl.ds(0, 512)], r.hidden.at[:, pl.ds(512, 512)]
    ring_oa = Ring(ot_a, r.ringed.ota[0], r.ringed.ota[1], "x", where, at)
    ring_ob = Ring(ot_b, r.ringed.otb[0], r.ringed.otb[1], "y", where, at)
    ring_k = Ring(kt, r.ringed.kt[0], r.ringed.kt[1], "x", where, at)
    ring_v = Ring(vt, r.ringed.vt[0], r.ringed.vt[1], "y", where, at)
    ring_oa2 = Ring(r.ot_a2, r.ringed.ota2[0], r.ringed.ota2[1], "y", where, at)
    ring_ob2 = Ring(r.ot_b2, r.ringed.otb2[0], r.ringed.otb2[1], "x", where, at)
    ring_k2 = Ring(r.kt2, r.ringed.kt2[0], r.ringed.kt2[1], "y", where, at)
    ring_v2 = Ring(r.vt2, r.ringed.vt2[0], r.ringed.vt2[1], "x", where, at)
    mine = [r.qkv.at[:, pl.ds(half * 512, 512)] for half in range(HALVES)]
    peers = [r.qkv.at[:, pl.ds(1024 + half * 512, 512)] for half in range(HALVES)]
    from_peer = [r.qkv.at[:, pl.ds(2048 + half * 512, 512)] for half in range(HALVES)]
    ring_z = [Ring(mine[half], r.ring_z[half][0], r.ring_z[half][1], "z", where, at) for half in range(HALVES)]

    loop(0, 8, lambda b: attention_forward(b, r, mixed))
    mixed_t[...] = mixed[...].T

    def out_terms(i):
        to_x, to_y = (x + 2 - i + 4) % 4, (y + 2 - i + 4) % 4

        def tile(j):
            lane_a = pl.multiple_of((to_x * 4 + j) * 256, 256)
            term = dot(mixed_t[0:256, :], r.cot[:, pl.ds(lane_a, 256)])
            ot_a[pl.ds(lane_a, 256), :] = term.astype(jnp.bfloat16)
            lane_b = pl.multiple_of((j * 4 + to_y) * 256, 256)
            term = dot(mixed_t[256:512, :], r.cot[:, pl.ds(lane_b, 256)])
            ot_b[rows_of((to_y * 4 + j) * 256, 256), :] = term.astype(jnp.bfloat16)

        loop(0, 4, tile)

        @pl.when(i == 0)
        def _():
            ring_oa.first()
            ring_ob.first()

    loop(0, 4, out_terms)
    ring_oa.second()
    ring_ob.second()
    loop(0, 8, lambda b: attention_backward(b, r))

    core_copies = [
        [
            send(
                peers[half].at[pl.ds(k * 256, 256), :],
                from_peer[half].at[pl.ds(k * 256, 256), :],
                r.s_core[half],
                k,
                peer,
            )
            for k in range(4)
        ]
        for half in range(HALVES)
    ]

    def enc_piece(half, piece_at, out, out_at):
        feats = slice(half * 512, half * 512 + 512)
        term = dot(r.dkv[piece_at], r.wkv[feats, :], ACROSS)
        out[rows_of(out_at, 256), :] = term.astype(jnp.bfloat16)

    def enc_half(half):
        def to_peer(k):
            enc_piece(half, k * 2 + (1 - core), peers[half], k * 256)
            for number in range(4):

                @pl.when(k == number)
                def _():
                    core_copies[half][number].start()

        loop(0, 4, to_peer)
        loop(0, 4, lambda k: enc_piece(half, k * 2 + core, mine[half], k * 256))

    def add_peer(half):
        for k in range(4):
            core_copies[half][k].wait_recv()
        add_rows(mine[half], 0, ((mine[half], 0), (from_peer[half], 0)), 1024, 64)

    def key_terms(part):
        lanes = pl.ds(pl.multiple_of(part * 128, 128), 128)
        term = dot(r.rows[:, :, lanes].reshape(2048, 128), r.dkv[...].reshape(2048, 1024), DOWN)
        low = term.astype(jnp.bfloat16)
        kt[rows_of(part * 128, 128), :] = low[:, 0:512]
        for side in range(2):
            to_x, to_y = (part * 2 + side) // 4, (part * 2 + side) % 4
            vt[rows_of(to_y * 256 + to_x * 64, 64), :] = low[side * 64 : side * 64 + 64, 512:1024]

    enc_half(0)
    add_peer(0)
    ring_z[0].first()
    ring_oa.third(64)
    ring_ob.third(64)
    enc_half(1)
    ring_z[0].third(64, True)
    add_peer(1)
    loop(0, 8, key_terms)
    ring_z[1].first()
    ring_k.first()
    ring_v.first()
    ring_k.second()
    ring_v.second()

    back_gens = [over_gen(half, r.returned, r.s_bgen) for half in range(HALVES)]

    def start_back_gen(half):
        ring_z[half].last(r.piece[half], 0, 16)
        out_gens[half].drain()
        for j in range(32):
            r.outgoing[half][j] = r.piece[half][r.position[j]]
        back_gens[half].start()
        own = pl.ds(gen * 2, 2)
        r.returned[half][own] = r.outgoing[half][own]

    def back_enc(half):
        def copy(step):
            to = (enc + step) % 8
            return send(
                r.grads[half].at[to],
                r.home.at[:, own_rows, pl.ds(half * 512, 512)],
                r.s_benc[half],
                step - 1,
                (to, gen),
            )

        return Exchange(8, copy)

    back_encs = [back_enc(half) for half in range(HALVES)]

    def start_back_enc(half):
        back_gens[half].receive()
        for j in range(16):
            r.grads[half][j // 2, j % 2] = r.returned[half][r.column[j]]
        back_encs[half].start()
        r.home[:, own_rows, half * 512 : half * 512 + 512] = r.grads[half][enc]

    start_back_gen(0)
    ring_z[1].third(64, True)
    ring_oa.last(r.ot_a2, 0, 64)
    ring_oa2.first()
    ring_oa2.second()
    ring_ob.last(r.ot_b2, 0, 64)
    ring_ob2.first()
    ring_ob2.second()
    ring_k.third(64)
    ring_v.third(64)
    ring_oa2.third(64)
    ring_ob2.third(64)
    start_back_gen(1)
    ring_k.last(r.kt2, 0, 64)
    ring_k2.first()
    ring_k2.second()
    ring_v.last(r.vt2, 0, 64)
    ring_v2.first()
    ring_v2.second()
    start_back_enc(0)
    ring_oa2.last(r.wo_out, 0, 64)
    ring_ob2.last(r.wo_out, 256, 64)
    ring_k2.third(32)
    ring_v2.third(32)
    start_back_enc(1)
    ring_k2.last(r.wk_out, 0, 32)
    ring_v2.last(r.wv_out, 0, 32)
    for half in range(HALVES):
        back_encs[half].receive()
    r.enc_out[...] = r.home[...]

    rings_all = [ring_oa, ring_ob, ring_k, ring_v, ring_oa2, ring_ob2, ring_k2, ring_v2] + ring_z
    for ring in rings_all:
        ring.drain()
    for half in range(HALVES):
        for copy in core_copies[half] + rings[half] + crosses[half]:
            copy.wait_send()
        for exchange in (out_encs[half], back_gens[half], back_encs[half]):
            exchange.drain()


def whole(tables, nbr, enc_gain, gain, qkv, eo, hidden, cot, wq, wo, wk, wv):
    low = jnp.bfloat16
    vmem = lambda *shape: pltpu.VMEM(shape, low)
    sems = lambda *shape: pltpu.SemaphoreType.DMA(shape)
    both = lambda make, *shape: [make(*shape) for _ in range(HALVES)]
    ring = lambda count, width: [vmem(count // 4 * 3, width), sems(2, 6)]
    anywhere = pl.BlockSpec(memory_space=pl.ANY)
    scalars = pl.BlockSpec(memory_space=pltpu.SMEM)
    local = pl.BlockSpec(memory_space=pltpu.VMEM)
    send_table, position_table, receive_table, column_table = tables
    small = dict(send=send_table, position=position_table, receive=receive_table, column=column_table)
    near = dict(nbr=nbr.reshape(256, 1024), enc_gain=enc_gain.reshape(1, -1), gain=gain.reshape(1, -1))
    big = dict(
        qkv_hbm=qkv, eo_hbm=eo, hidden_hbm=hidden, wq_hbm=wq, cot_hbm=cot, wo_hbm=wo, wk_hbm=wk, wv_hbm=wv
    )
    outputs = dict(
        enc_out=jax.ShapeDtypeStruct((2, 128, 1024), low),
        wo_out=jax.ShapeDtypeStruct((512, 256), low),
        wk_out=jax.ShapeDtypeStruct((64, 512), low),
        wv_out=jax.ShapeDtypeStruct((64, 512), low),
    )
    scratch = dict(
        qkv=vmem(1024, 3072),
        eo=vmem(1024, 1024),
        hidden=vmem(512, 4096),
        wq=vmem(4096, 512),
        cot=vmem(512, 4096),
        wo=vmem(512, 4096),
        wkv=vmem(1024, 1024),
        enc_normed=vmem(256, 1024),
        projected=vmem(256, 3072),
        encoded=vmem(2, 128, 1024),
        q_pairs=vmem(2048, 256),
        dm_pairs=vmem(2048, 256),
        kv=vmem(8, 256, 1024),
        dkv=vmem(8, 256, 1024),
        rows=vmem(8, 256, 1024),
        ot_a2=vmem(1024, 256),
        ot_b2=vmem(1024, 256),
        kt2=vmem(256, 512),
        vt2=vmem(256, 512),
        home=vmem(2, 128, 1024),
        ringed=dict(
            ota=ring(4096, 256),
            otb=ring(4096, 256),
            kt=ring(1024, 512),
            vt=ring(1024, 512),
            ota2=ring(1024, 256),
            otb2=ring(1024, 256),
            kt2=ring(256, 512),
            vt2=ring(256, 512),
        ),
        ring_z=both(ring, 1024, 512),
        columns=both(vmem, 16, 16, 512),
        outgoing=both(vmem, 32, 16, 512),
        incoming=both(vmem, 32, 16, 512),
        returned=both(vmem, 32, 16, 512),
        piece=both(vmem, 16, 16, 512),
        grads=both(vmem, 8, 2, 16, 512),
        s_oenc=both(sems, 2, 7),
        s_benc=both(sems, 2, 7),
        s_ogen=both(sems, 2, 15),
        s_bgen=both(sems, 2, 15),
        s_ring=both(sems, 2, 4),
        s_cross=both(sems, 2, 5),
        s_core=both(sems, 2, 4),
        load_sems=sems(10),
    )
    operands = small | near | big
    leaves, _ = jax.tree.flatten(scratch)
    tree = jax.tree.structure((operands, outputs, scratch))
    by_name = lambda part: [part[name] for name in sorted(part)]
    place = dict.fromkeys(small, scalars) | dict.fromkeys(near, local) | dict.fromkeys(big, anywhere)
    return pl.pallas_call(
        functools.partial(whole_kernel, tree),
        name="retro_whole",
        out_shape=tuple(by_name(outputs)),
        in_specs=by_name(place),
        out_specs=(local,) * len(outputs),
        scratch_shapes=leaves,
        compiler_params=pltpu.CompilerParams(
            collective_id=1, has_side_effects=True, vmem_limit_bytes=61 * 1024 * 1024
        ),
    )(*by_name(operands))


def widen_kernel(*refs):
    sources, targets, near, sems = refs[:4], refs[4:8], refs[8:12], refs[12]
    copies = [
        pltpu.make_async_copy(src, dst, sems.at[number]) for number, (src, dst) in enumerate(zip(sources, near))
    ]
    for copy in copies:
        copy.start()
    for copy, src, dst in zip(copies, near, targets):
        copy.wait()
        dst[...] = src[...].astype(jnp.float32)


def widen(values):
    return pl.pallas_call(
        widen_kernel,
        name="widen",
        out_shape=tuple(jax.ShapeDtypeStruct(value.shape, jnp.float32) for value in values),
        in_specs=[pl.BlockSpec(memory_space=pl.ANY)] * 4,
        out_specs=(pl.BlockSpec(memory_space=pltpu.VMEM),) * 4,
        scratch_shapes=[pltpu.VMEM(value.shape, value.dtype) for value in values] + [pltpu.SemaphoreType.DMA((4,))],
        compiler_params=pltpu.CompilerParams(vmem_limit_bytes=60 * 1024 * 1024),
    )(*values)


def routing(nbr_index, row_index, gen_count, per_device, row_size, capacity):
    entries = nbr_index.reshape(gen_count, row_size)
    source = entries // per_device % gen_count
    column = entries // (per_device * gen_count) * per_device + entries % per_device
    places = jnp.arange(row_size, dtype=jnp.int32)
    same = (source[:, :, None] == source[:, None, :]) & (places[None, None, :] < places[None, :, None])
    rank = jnp.sum(same.astype(jnp.int32), axis=2)
    rows = jnp.arange(gen_count, dtype=jnp.int32)
    send_slot = (rows[:, None] * capacity + rank).reshape(-1)
    mine = (source == row_index).reshape(-1)
    flat_column = column.reshape(-1)
    buffers = jnp.arange(gen_count * capacity, dtype=jnp.int32)
    send_match = (send_slot[:, None] == buffers[None, :]) & mine[:, None]
    send_column = jnp.sum(jnp.where(send_match, flat_column[:, None], 0), axis=0)
    column_match = (flat_column[:, None] == places[None, :]) & mine[:, None]
    column_position = jnp.sum(jnp.where(column_match, send_slot[:, None], 0), axis=0)
    own = (rows == row_index)[:, None]
    receive_position = jnp.sum(jnp.where(own, source * capacity + rank, 0), axis=0)
    receive_match = receive_position[:, None] == buffers[None, :]
    position_slot = jnp.sum(jnp.where(receive_match, places[:, None], 0), axis=0)
    return (send_column, position_slot, receive_position, column_position)


def local(
    hidden_states,
    grad_out,
    nbr_embed,
    nbr_index,
    gain,
    w_query,
    w_out,
    w_key,
    w_value,
    enc_gain,
    enc_qkv,
    enc_out,
):
    gen_count = lax.axis_size("gen")
    per_device = nbr_embed.shape[0]
    row_size = per_device * lax.axis_size("enc")
    capacity = max(2, 2 * row_size // gen_count)
    tables = routing(nbr_index, lax.axis_index("gen"), gen_count, per_device, row_size, capacity)
    grad_encoded, grad_key, grad_out_proj, grad_value = (
        whole(
            tables,
            nbr_embed,
            enc_gain,
            gain,
            enc_qkv,
            enc_out,
            hidden_states,
            grad_out,
            w_query,
            w_out,
            w_key,
            w_value,
        )
    )
    return widen((grad_encoded, grad_out_proj, grad_key, grad_value))


def solution(mesh):
    return jax.shard_map(
        local,
        mesh=mesh,
        in_specs=(
            P("gen", None),
            P("gen", None),
            P(("enc", "gen"), None, None),
            P(),
            P(),
            P(None, "enc"),
            P("enc", None),
            P(None, "enc"),
            P(None, "enc"),
            P(),
            P(),
            P(),
        ),
        out_specs=(
            P(("enc", "gen"), None, None),
            P("enc", "gen"),
            P("gen", "enc"),
            P("gen", "enc"),
        ),
        check_vma=False,
    )
```

```python
import functools
import types

import jax
import jax.numpy as jnp
from jax import lax
from jax.experimental import pallas as pl
from jax.experimental.pallas import tpu as pltpu
from jax.sharding import PartitionSpec as P

EH = 8
CH = 64
SOFTCAP = 5.0
EPSILON = 1e-06
MESH = pl.DeviceIdType.MESH


def neighbours():
    enc, gen = lax.axis_index("enc"), lax.axis_index("gen")
    z, core, x, y = enc // 2, enc % 2, gen // 4, gen % 4

    def at(axis, step):
        if axis == "x":
            return (enc, (x + step) % 4 * 4 + y)
        if axis == "y":
            return (enc, x * 4 + (y + step) % 4)
        if axis == "z":
            return ((z + step) % 4 * 2 + core, gen)
        return (z * 2 + (1 - core), gen)

    return enc, gen, {"x": x, "y": y, "z": z, "core": core}, at


def send(src, dst, sems, number, device):
    return pltpu.make_async_remote_copy(
        src_ref=src,
        dst_ref=dst,
        send_sem=sems.at[0, number],
        recv_sem=sems.at[1, number],
        device_id=device,
        device_id_type=MESH,
    )


def add_rows(out, out_at, terms, rows, step):
    def body(i, carry):
        total = None
        for ref, at in terms:
            value = ref[pl.ds(pl.multiple_of(at + i * step, step), step), :].astype(jnp.float32)
            total = value if total is None else total + value
        if len(out.shape) == 3:
            out[out_at + i] = total.astype(out.dtype)
        else:
            out[pl.ds(pl.multiple_of(out_at + i * step, step), step), :] = total.astype(out.dtype)
        return carry

    lax.fori_loop(0, rows // step, body, 0)


class Ring:
    def __init__(self, src, buf, sems, axis, where, at):
        self.src, self.buf = src, buf
        self.rows = src.shape[0] // 4
        self.half = self.rows // 2
        self.me = where[axis]
        half = self.half
        self.plus, self.minus = (self.me + 1) % 4, (self.me + 3) % 4
        across = (self.me + 2) % 4
        pieces = (
            (across, 0, 1),
            (self.plus, 1, 1),
            (self.plus, 0, 1),
            (across, 1, 3),
            (self.minus, 0, 3),
            (self.minus, 1, 3),
        )
        self.copies = []
        for number, (chunk, side, step) in enumerate(pieces):
            start = pl.multiple_of(chunk * self.rows + side * half, half)
            self.copies.append(
                send(
                    src.at[pl.ds(start, half), :],
                    buf.at[pl.ds(number * half, half), :],
                    sems,
                    number,
                    at(axis, step),
                )
            )

    def first(self):
        self.copies[0].start()
        self.copies[3].start()

    def second(self):
        self.copies[1].start()
        self.copies[4].start()

    def third(self, step, with_second=False):
        half = self.half
        self.copies[0].wait_recv()
        if with_second:
            self.copies[3].wait_recv()
            self.second()
        start = self.plus * self.rows
        add_rows(self.src, start, ((self.src, start), (self.buf, 0)), half, step)
        self.copies[2].start()
        if not with_second:
            self.copies[3].wait_recv()
        start = self.minus * self.rows + half
        add_rows(self.src, start, ((self.src, start), (self.buf, 3 * half)), half, step)
        self.copies[5].start()

    def last(self, out, out_at, step):
        half = self.half
        for number in (1, 2, 4, 5):
            self.copies[number].wait_recv()
        start = self.me * self.rows
        add_rows(out, out_at, ((self.src, start), (self.buf, 2 * half), (self.buf, 4 * half)), half, step)
        add_rows(
            out, out_at + (half // step if len(out.shape) == 3 else half), ((self.src, start + half), (self.buf, half), (self.buf, 5 * half)), half, step
        )

    def drain(self):
        for copy in self.copies:
            copy.wait_send()


HALVES = 2
DOWN = (((0,), (0,)), ((), ()))
ACROSS = (((1,), (1,)), ((), ()))


def dot(a, b, dims=(((1,), (0,)), ((), ()))):
    return lax.dot_general(a, b, dims, preferred_element_type=jnp.float32)


def loop(low, high, body):
    def step(i, carry):
        body(i)
        return carry

    lax.fori_loop(low, high, step, 0)


def rows_of(start, size):
    return pl.ds(pl.multiple_of(start, size), size)


def normalise(values, gain, out):
    def body(i):
        at = rows_of(i * 16, 16)
        wide = values[at, :].astype(jnp.float32)
        factor = lax.rsqrt(jnp.mean(wide * wide, axis=-1, keepdims=True) + EPSILON)
        out[at, :] = (wide * factor * gain[...]).astype(jnp.bfloat16)

    loop(0, values.shape[0] // 16, body)


def softcapped(q, k):
    scale = q.shape[-1] ** (-0.5)
    slope = jnp.tanh(dot(q, k, ACROSS) * (scale / SOFTCAP))
    expo = jnp.exp(SOFTCAP * slope)
    return slope, expo / jnp.sum(expo, axis=-1, keepdims=True)


def encoder_attention(i, projected, attended):
    at = rows_of(i * 128, 128)
    for h in range(EH):
        q, k, v = (projected[at, part * 1024 + h * 128 : part * 1024 + h * 128 + 128] for part in range(3))
        _, probs = softcapped(q, k)
        attended[at, h * 128 : h * 128 + 128] = dot(probs.astype(jnp.bfloat16), v).astype(jnp.bfloat16)


def pair_refs(b, p, r):
    keys, rows = rows_of(b * 32, 32), rows_of((b * 2 + p) * 128, 128)
    k = r.kv[:, keys, p * 256 : p * 256 + 256].reshape(256, 256)
    v = r.kv[:, keys, 512 + p * 256 : 512 + p * 256 + 256].reshape(256, 256)
    return keys, rows, k, v


def pair_probs(k, q_pair):
    slope = jnp.tanh(dot(k, q_pair, ACROSS) * (128 ** (-0.5) / SOFTCAP))
    expo = jnp.exp(SOFTCAP * slope)
    return slope, expo * (1.0 / jnp.sum(expo, axis=0, keepdims=True))


def attention_forward(b, r, mixed):
    tokens = rows_of(b * CH, CH)
    for p in range(2):
        keys, rows, k, v = pair_refs(b, p, r)
        slope, probs = pair_probs(k, r.q_pairs[rows, :])
        low = probs.astype(jnp.bfloat16)
        lanes = pl.ds(pl.multiple_of((b * 2 + p) * 128, 128), 128)
        r.wo[0:256, lanes] = low
        r.wo[256:512, lanes] = ((1.0 - slope * slope) * 128 ** (-0.5)).astype(jnp.bfloat16)
        both = dot(low, v, DOWN).astype(jnp.bfloat16)
        mixed[tokens, p * 256 : p * 256 + 128] = both[0:64, 0:128]
        mixed[tokens, p * 256 + 128 : p * 256 + 256] = both[64:128, 128:256]


def attention_backward(b, r):
    for p in range(2):
        keys, rows, k, v = pair_refs(b, p, r)
        q_pair, dm_pair = r.q_pairs[rows, :], r.dm_pairs[rows, :]
        lanes = pl.ds(pl.multiple_of((b * 2 + p) * 128, 128), 128)
        low, slope = r.wo[0:256, lanes], r.wo[256:512, lanes].astype(jnp.float32)
        probs = low.astype(jnp.float32)
        d_probs = dot(v, dm_pair, ACROSS)
        d_capped = probs * (d_probs - jnp.sum(probs * d_probs, axis=0, keepdims=True))
        d_raw = (d_capped * slope).astype(jnp.bfloat16)
        d_keys = dot(d_raw, q_pair).astype(jnp.bfloat16)
        d_values = dot(low, dm_pair).astype(jnp.bfloat16)
        r.dkv[:, keys, p * 256 : p * 256 + 256] = d_keys.reshape(8, 32, 256)
        r.dkv[:, keys, 512 + p * 256 : 512 + p * 256 + 256] = d_values.reshape(8, 32, 256)


class Exchange:
    def __init__(self, count, copy):
        self.count, self.copy = count, copy

    def start(self):
        loop(1, self.count, lambda step: self.copy(step).start())

    def receive(self):
        loop(1, self.count, lambda step: self.copy(step).wait_recv())

    def drain(self):
        loop(1, self.count, lambda step: self.copy(step).wait_send())


def whole_kernel(tree, *refs):
    r = jax.tree.unflatten(tree, refs)
    r = types.SimpleNamespace(**{name: ref for part in r for name, ref in part.items()})
    r.ringed = types.SimpleNamespace(**r.ringed)

    def load(number):
        src = (r.eo_hbm, r.hidden_hbm, r.wq_hbm, r.cot_hbm, r.wo_hbm, r.wk_hbm, r.wv_hbm)[number]
        w_pair = [r.wkv.at[:, pl.ds(at, 512)] for at in (0, 512)]
        dst = (r.eo, r.hidden, r.wq, r.cot, r.wo, *w_pair)[number]
        return pltpu.make_async_copy(src, dst, r.load_sems.at[number])

    def load_third(third):
        lanes = pl.ds(third * 1024, 1024)
        return pltpu.make_async_copy(r.qkv_hbm.at[:, lanes], r.qkv.at[:, lanes], r.load_sems.at[7 + third])

    for third in range(3):
        load_third(third).start()
    load(0).start()
    enc, gen, where, at = neighbours()
    x, y, z, core = where["x"], where["y"], where["z"], where["core"]
    barrier = pltpu.get_barrier_semaphore()
    loop(1, 16, lambda step: pl.semaphore_signal(barrier, inc=1, device_id=(enc, (gen + step) % 16), device_id_type=MESH))
    loop(1, 8, lambda step: pl.semaphore_signal(barrier, inc=1, device_id=((enc + step) % 8, gen), device_id_type=MESH))

    normalise(r.nbr, r.enc_gain, r.enc_normed)
    for third in range(3):
        load_third(third).wait()
        lanes = slice(third * 1024, third * 1024 + 1024)
        r.projected[:, lanes] = dot(r.enc_normed[...], r.qkv[:, lanes]).astype(jnp.bfloat16)
    for number in range(1, 7):
        load(number).start()
    loop(0, 2, lambda i: encoder_attention(i, r.projected, r.enc_normed))
    load(0).wait()

    def finish(half):
        lanes = slice(half * 512, half * 512 + 512)
        update = dot(r.enc_normed[...], r.eo[:, lanes])
        low = (r.nbr[:, lanes].astype(jnp.float32) + update).astype(jnp.bfloat16)
        r.encoded[:, :, lanes] = low.reshape(2, 128, 512)

    finish(0)
    pl.semaphore_wait(barrier, 22)

    own_rows = rows_of(enc * 16, 16)

    def out_enc(half):
        lanes = pl.ds(half * 512, 512)

        def copy(step):
            peer = (enc + step) % 8
            return send(
                r.encoded.at[:, rows_of(peer * 16, 16), lanes],
                r.columns[half].at[pl.ds(enc * 2, 2)],
                r.s_oenc[half],
                step - 1,
                (peer, gen),
            )

        return Exchange(8, copy)

    def over_gen(half, target, sems):
        def copy(step):
            peer = (gen + step) % 16
            return send(
                r.outgoing[half].at[pl.ds(peer * 2, 2)],
                target[half].at[pl.ds(gen * 2, 2)],
                sems[half],
                step - 1,
                (enc, peer),
            )

        return Exchange(16, copy)

    out_encs = [out_enc(half) for half in range(HALVES)]
    out_gens = [over_gen(half, r.incoming, r.s_ogen) for half in range(HALVES)]
    out_encs[0].start()
    finish(1)
    for half in range(HALVES):
        r.columns[half][pl.ds(enc * 2, 2)] = r.encoded[:, own_rows, half * 512 : half * 512 + 512]

    def pick_out_gen(half):
        for j in range(32):
            r.outgoing[half][j] = r.columns[half][r.send[j]]
        own = pl.ds(gen * 2, 2)
        r.incoming[half][own] = r.outgoing[half][own]

    def store_pairs(out, i, low):
        for block in range(4):
            for head in range(4):
                start = i * 1024 + block * 256 + head // 2 * 128 + head % 2 * 64
                out[rows_of(start, 64), head % 2 * 128 : head % 2 * 128 + 128] = low[
                    block * 64 : block * 64 + 64, head * 128 : head * 128 + 128
                ]

    def query_tile(i):
        low = dot(r.hidden[rows_of(i * 256, 256), :], r.wq[...]).astype(jnp.bfloat16)
        store_pairs(r.q_pairs, i, low)

    def cotangent_tile(i):
        low = dot(r.cot[rows_of(i * 256, 256), :], r.wo[...], ACROSS).astype(jnp.bfloat16)
        store_pairs(r.dm_pairs, i, low)

    r.q_pairs[...] = jnp.zeros_like(r.q_pairs)
    r.dm_pairs[...] = jnp.zeros_like(r.dm_pairs)
    out_encs[0].receive()
    out_encs[1].start()
    pick_out_gen(0)
    out_gens[0].start()
    load(1).wait()
    normalise(r.hidden, r.gain, r.hidden)
    load(2).wait()
    loop(0, 2, query_tile)
    out_encs[1].receive()
    pick_out_gen(1)
    load(3).wait()
    load(4).wait()

    minus, plus, across = (z + 3) % 4 * 2 + core, (z + 1) % 4 * 2 + core, (z + 2) % 4 * 2 + core
    up, down, peer = at("z", 1), at("z", 3), at("core", 1)
    rings, crosses = [], []
    for half in range(HALVES):
        rows = r.rows.at[:, :, pl.ds(half * 512, 512)]
        first, second = pl.ds(0, 128), pl.ds(128, 128)

        def share(ref, sems, number, device):
            return send(ref, ref, sems, number, device)

        rings.append(
            [
                share(rows.at[enc], r.s_ring[half], 0, up),
                share(rows.at[enc], r.s_ring[half], 1, down),
                share(rows.at[minus, first], r.s_ring[half], 2, up),
                share(rows.at[plus, second], r.s_ring[half], 3, down),
            ]
        )
        crosses.append(
            [
                share(rows.at[enc], r.s_cross[half], 0, peer),
                share(rows.at[minus], r.s_cross[half], 1, peer),
                share(rows.at[plus], r.s_cross[half], 2, peer),
                share(rows.at[across, first], r.s_cross[half], 3, peer),
                share(rows.at[across, second], r.s_cross[half], 4, peer),
            ]
        )

    def take_slots(half):
        out_gens[half].receive()
        for j in range(16):
            r.rows[enc, j * 16 : j * 16 + 16, half * 512 : half * 512 + 512] = r.incoming[half][r.receive[j]]

    def gather_own(half):
        rings[half][0].start()
        rings[half][1].start()
        crosses[half][0].start()

    def gather_next(half):
        rings[half][0].wait_recv()
        rings[half][2].start()
        crosses[half][1].start()
        rings[half][1].wait_recv()
        rings[half][3].start()
        crosses[half][2].start()

    def gather_last(half):
        rings[half][2].wait_recv()
        crosses[half][3].start()
        rings[half][3].wait_recv()
        crosses[half][4].start()

    def of_peer(piece):
        return piece + 1 - 2 * core

    def project(piece):
        r.kv[piece] = dot(r.rows[piece], r.wkv[...]).astype(jnp.bfloat16)

    def project_some(pieces):
        def body(i):
            piece = pieces[0]
            for number in range(1, len(pieces)):
                piece = jnp.where(i == number, pieces[number], piece)
            project(piece)

        loop(0, len(pieces), body)

    load(5).wait()
    load(6).wait()
    take_slots(0)
    out_gens[1].start()
    gather_own(0)
    loop(0, 2, cotangent_tile)
    gather_next(0)
    gather_last(0)
    take_slots(1)
    gather_own(1)
    crosses[1][0].wait_recv()
    crosses[0][0].wait_recv()
    project_some((enc, of_peer(enc)))
    gather_next(1)
    for number in (1, 2):
        crosses[0][number].wait_recv()
    project_some((minus, plus))
    for number in (1, 2):
        crosses[1][number].wait_recv()
    project_some((of_peer(minus), of_peer(plus)))
    gather_last(1)
    for number in (3, 4):
        crosses[0][number].wait_recv()
        crosses[1][number].wait_recv()
    project_some((across, of_peer(across)))

    ot_a, ot_b = r.wq.at[:, pl.ds(0, 256)], r.wq.at[:, pl.ds(256, 256)]
    kt, vt = r.eo.at[:, pl.ds(0, 512)], r.eo.at[:, pl.ds(512, 512)]
    mixed, mixed_t = r.hidden.at[:, pl.ds(0, 512)], r.hidden.at[:, pl.ds(512, 512)]
    ring_oa = Ring(ot_a, r.ringed.ota[0], r.ringed.ota[1], "x", where, at)
    ring_ob = Ring(ot_b, r.ringed.otb[0], r.ringed.otb[1], "y", where, at)
    ring_k = Ring(kt, r.ringed.kt[0], r.ringed.kt[1], "x", where, at)
    ring_v = Ring(vt, r.ringed.vt[0], r.ringed.vt[1], "y", where, at)
    ring_oa2 = Ring(r.ot_a2, r.ringed.ota2[0], r.ringed.ota2[1], "y", where, at)
    ring_ob2 = Ring(r.ot_b2, r.ringed.otb2[0], r.ringed.otb2[1], "x", where, at)
    ring_k2 = Ring(r.kt2, r.ringed.kt2[0], r.ringed.kt2[1], "y", where, at)
    ring_v2 = Ring(r.vt2, r.ringed.vt2[0], r.ringed.vt2[1], "x", where, at)
    mine = [r.qkv.at[:, pl.ds(half * 512, 512)] for half in range(HALVES)]
    peers = [r.qkv.at[:, pl.ds(1024 + half * 512, 512)] for half in range(HALVES)]
    from_peer = [r.qkv.at[:, pl.ds(2048 + half * 512, 512)] for half in range(HALVES)]
    ring_z = [Ring(mine[half], r.ring_z[half][0], r.ring_z[half][1], "z", where, at) for half in range(HALVES)]

    loop(0, 8, lambda b: attention_forward(b, r, mixed))
    mixed_t[...] = mixed[...].T

    def out_terms(i):
        to_x, to_y = (x + 2 - i + 4) % 4, (y + 2 - i + 4) % 4

        def tile(j):
            lane_a = pl.multiple_of((to_x * 4 + j) * 256, 256)
            term = dot(mixed_t[0:256, :], r.cot[:, pl.ds(lane_a, 256)])
            ot_a[pl.ds(lane_a, 256), :] = term.astype(jnp.bfloat16)
            lane_b = pl.multiple_of((j * 4 + to_y) * 256, 256)
            term = dot(mixed_t[256:512, :], r.cot[:, pl.ds(lane_b, 256)])
            ot_b[rows_of((to_y * 4 + j) * 256, 256), :] = term.astype(jnp.bfloat16)

        loop(0, 4, tile)

    loop(0, 1, out_terms)
    ring_oa.first()
    ring_ob.first()
    loop(0, 8, lambda b: attention_backward(b, r))

    core_copies = [
        [
            send(
                peers[half].at[pl.ds(k * 256, 256), :],
                from_peer[half].at[pl.ds(k * 256, 256), :],
                r.s_core[half],
                k,
                peer,
            )
            for k in range(4)
        ]
        for half in range(HALVES)
    ]

    def enc_piece(half, piece_at, out, out_at):
        feats = slice(half * 512, half * 512 + 512)
        term = dot(r.dkv[piece_at], r.wkv[feats, :], ACROSS)
        out[rows_of(out_at, 256), :] = term.astype(jnp.bfloat16)

    def enc_half(half):
        def to_peer(k):
            enc_piece(half, k * 2 + (1 - core), peers[half], k * 256)
            for number in range(4):

                @pl.when(k == number)
                def _():
                    core_copies[half][number].start()

        loop(0, 4, to_peer)
        loop(0, 4, lambda k: enc_piece(half, k * 2 + core, mine[half], k * 256))

    def add_peer(half):
        for k in range(4):
            core_copies[half][k].wait_recv()
        add_rows(mine[half], 0, ((mine[half], 0), (from_peer[half], 0)), 1024, 64)

    def key_terms(part):
        lanes = pl.ds(pl.multiple_of(part * 128, 128), 128)
        term = dot(r.rows[:, :, lanes].reshape(2048, 128), r.dkv[...].reshape(2048, 1024), DOWN)
        low = term.astype(jnp.bfloat16)
        kt[rows_of(part * 128, 128), :] = low[:, 0:512]
        for side in range(2):
            to_x, to_y = (part * 2 + side) // 4, (part * 2 + side) % 4
            vt[rows_of(to_y * 256 + to_x * 64, 64), :] = low[side * 64 : side * 64 + 64, 512:1024]

    enc_half(0)
    add_peer(0)
    ring_z[0].first()
    loop(1, 4, out_terms)
    ring_oa.second()
    ring_ob.second()
    ring_oa.third(64)
    ring_ob.third(64)
    ring_z[0].third(64, True)
    enc_half(1)
    add_peer(1)
    ring_z[1].first()
    loop(0, 4, key_terms)

    back_gens = [over_gen(half, r.returned, r.s_bgen) for half in range(HALVES)]

    def start_back_gen(half):
        ring_z[half].last(r.piece[half], 0, 16)
        out_gens[half].drain()
        for j in range(32):
            r.outgoing[half][j] = r.piece[half][r.position[j]]
        back_gens[half].start()
        own = pl.ds(gen * 2, 2)
        r.returned[half][own] = r.outgoing[half][own]

    def back_enc(half):
        def copy(step):
            to = (enc + step) % 8
            return send(
                r.grads[half].at[to],
                r.home.at[:, own_rows, pl.ds(half * 512, 512)],
                r.s_benc[half],
                step - 1,
                (to, gen),
            )

        return Exchange(8, copy)

    back_encs = [back_enc(half) for half in range(HALVES)]

    def start_back_enc(half):
        back_gens[half].receive()
        for j in range(16):
            r.grads[half][j // 2, j % 2] = r.returned[half][r.column[j]]
        back_encs[half].start()
        r.home[:, own_rows, half * 512 : half * 512 + 512] = r.grads[half][enc]

    start_back_gen(0)
    ring_z[1].third(64, True)
    loop(4, 8, key_terms)
    ring_k.first()
    ring_v.first()
    ring_k.second()
    ring_v.second()
    ring_oa.last(r.ot_a2, 0, 64)
    ring_oa2.first()
    ring_oa2.second()
    ring_ob.last(r.ot_b2, 0, 64)
    ring_ob2.first()
    ring_ob2.second()
    start_back_gen(1)
    ring_k.third(64)
    ring_v.third(64)
    ring_oa2.third(64)
    ring_ob2.third(64)
    start_back_enc(0)
    ring_k.last(r.kt2, 0, 64)
    ring_k2.first()
    ring_k2.second()
    ring_v.last(r.vt2, 0, 64)
    ring_v2.first()
    ring_v2.second()
    ring_oa2.last(r.wo_out, 0, 64)
    ring_ob2.last(r.wo_out, 256, 64)
    ring_k2.third(32)
    ring_v2.third(32)
    start_back_enc(1)
    ring_k2.last(r.wk_out, 0, 32)
    ring_v2.last(r.wv_out, 0, 32)
    for half in range(HALVES):
        back_encs[half].receive()
    r.enc_out[...] = r.home[...]

    rings_all = [ring_oa, ring_ob, ring_k, ring_v, ring_oa2, ring_ob2, ring_k2, ring_v2] + ring_z
    for ring in rings_all:
        ring.drain()
    for half in range(HALVES):
        for copy in core_copies[half] + rings[half] + crosses[half]:
            copy.wait_send()
        for exchange in (out_encs[half], back_gens[half], back_encs[half]):
            exchange.drain()


def whole(tables, nbr, enc_gain, gain, qkv, eo, hidden, cot, wq, wo, wk, wv):
    low = jnp.bfloat16
    vmem = lambda *shape: pltpu.VMEM(shape, low)
    sems = lambda *shape: pltpu.SemaphoreType.DMA(shape)
    both = lambda make, *shape: [make(*shape) for _ in range(HALVES)]
    ring = lambda count, width: [vmem(count // 4 * 3, width), sems(2, 6)]
    anywhere = pl.BlockSpec(memory_space=pl.ANY)
    scalars = pl.BlockSpec(memory_space=pltpu.SMEM)
    local = pl.BlockSpec(memory_space=pltpu.VMEM)
    send_table, position_table, receive_table, column_table = tables
    small = dict(send=send_table, position=position_table, receive=receive_table, column=column_table)
    near = dict(nbr=nbr.reshape(256, 1024), enc_gain=enc_gain.reshape(1, -1), gain=gain.reshape(1, -1))
    big = dict(
        qkv_hbm=qkv, eo_hbm=eo, hidden_hbm=hidden, wq_hbm=wq, cot_hbm=cot, wo_hbm=wo, wk_hbm=wk, wv_hbm=wv
    )
    outputs = dict(
        enc_out=jax.ShapeDtypeStruct((2, 128, 1024), low),
        wo_out=jax.ShapeDtypeStruct((512, 256), low),
        wk_out=jax.ShapeDtypeStruct((64, 512), low),
        wv_out=jax.ShapeDtypeStruct((64, 512), low),
    )
    scratch = dict(
        qkv=vmem(1024, 3072),
        eo=vmem(1024, 1024),
        hidden=vmem(512, 4096),
        wq=vmem(4096, 512),
        cot=vmem(512, 4096),
        wo=vmem(512, 4096),
        wkv=vmem(1024, 1024),
        enc_normed=vmem(256, 1024),
        projected=vmem(256, 3072),
        encoded=vmem(2, 128, 1024),
        q_pairs=vmem(2048, 256),
        dm_pairs=vmem(2048, 256),
        kv=vmem(8, 256, 1024),
        dkv=vmem(8, 256, 1024),
        rows=vmem(8, 256, 1024),
        ot_a2=vmem(1024, 256),
        ot_b2=vmem(1024, 256),
        kt2=vmem(256, 512),
        vt2=vmem(256, 512),
        home=vmem(2, 128, 1024),
        ringed=dict(
            ota=ring(4096, 256),
            otb=ring(4096, 256),
            kt=ring(1024, 512),
            vt=ring(1024, 512),
            ota2=ring(1024, 256),
            otb2=ring(1024, 256),
            kt2=ring(256, 512),
            vt2=ring(256, 512),
        ),
        ring_z=both(ring, 1024, 512),
        columns=both(vmem, 16, 16, 512),
        outgoing=both(vmem, 32, 16, 512),
        incoming=both(vmem, 32, 16, 512),
        returned=both(vmem, 32, 16, 512),
        piece=both(vmem, 16, 16, 512),
        grads=both(vmem, 8, 2, 16, 512),
        s_oenc=both(sems, 2, 7),
        s_benc=both(sems, 2, 7),
        s_ogen=both(sems, 2, 15),
        s_bgen=both(sems, 2, 15),
        s_ring=both(sems, 2, 4),
        s_cross=both(sems, 2, 5),
        s_core=both(sems, 2, 4),
        load_sems=sems(10),
    )
    operands = small | near | big
    leaves, _ = jax.tree.flatten(scratch)
    tree = jax.tree.structure((operands, outputs, scratch))
    by_name = lambda part: [part[name] for name in sorted(part)]
    place = dict.fromkeys(small, scalars) | dict.fromkeys(near, local) | dict.fromkeys(big, anywhere)
    return pl.pallas_call(
        functools.partial(whole_kernel, tree),
        name="retro_whole",
        out_shape=tuple(by_name(outputs)),
        in_specs=by_name(place),
        out_specs=(local,) * len(outputs),
        scratch_shapes=leaves,
        compiler_params=pltpu.CompilerParams(
            collective_id=1, has_side_effects=True, vmem_limit_bytes=61 * 1024 * 1024
        ),
    )(*by_name(operands))


def widen_kernel(*refs):
    sources, targets, near, sems = refs[:4], refs[4:8], refs[8:12], refs[12]
    copies = [
        pltpu.make_async_copy(src, dst, sems.at[number]) for number, (src, dst) in enumerate(zip(sources, near))
    ]
    for copy in copies:
        copy.start()
    for copy, src, dst in zip(copies, near, targets):
        copy.wait()
        dst[...] = src[...].astype(jnp.float32)


def widen(values):
    return pl.pallas_call(
        widen_kernel,
        name="widen",
        out_shape=tuple(jax.ShapeDtypeStruct(value.shape, jnp.float32) for value in values),
        in_specs=[pl.BlockSpec(memory_space=pl.ANY)] * 4,
        out_specs=(pl.BlockSpec(memory_space=pltpu.VMEM),) * 4,
        scratch_shapes=[pltpu.VMEM(value.shape, value.dtype) for value in values] + [pltpu.SemaphoreType.DMA((4,))],
        compiler_params=pltpu.CompilerParams(vmem_limit_bytes=60 * 1024 * 1024),
    )(*values)


def routing(nbr_index, row_index, gen_count, per_device, row_size, capacity):
    entries = nbr_index.reshape(gen_count, row_size)
    source = entries // per_device % gen_count
    column = entries // (per_device * gen_count) * per_device + entries % per_device
    places = jnp.arange(row_size, dtype=jnp.int32)
    same = (source[:, :, None] == source[:, None, :]) & (places[None, None, :] < places[None, :, None])
    rank = jnp.sum(same.astype(jnp.int32), axis=2)
    rows = jnp.arange(gen_count, dtype=jnp.int32)
    send_slot = (rows[:, None] * capacity + rank).reshape(-1)
    mine = (source == row_index).reshape(-1)
    flat_column = column.reshape(-1)
    buffers = jnp.arange(gen_count * capacity, dtype=jnp.int32)
    send_match = (send_slot[:, None] == buffers[None, :]) & mine[:, None]
    send_column = jnp.sum(jnp.where(send_match, flat_column[:, None], 0), axis=0)
    column_match = (flat_column[:, None] == places[None, :]) & mine[:, None]
    column_position = jnp.sum(jnp.where(column_match, send_slot[:, None], 0), axis=0)
    own = (rows == row_index)[:, None]
    receive_position = jnp.sum(jnp.where(own, source * capacity + rank, 0), axis=0)
    receive_match = receive_position[:, None] == buffers[None, :]
    position_slot = jnp.sum(jnp.where(receive_match, places[:, None], 0), axis=0)
    return (send_column, position_slot, receive_position, column_position)


def local(
    hidden_states,
    grad_out,
    nbr_embed,
    nbr_index,
    gain,
    w_query,
    w_out,
    w_key,
    w_value,
    enc_gain,
    enc_qkv,
    enc_out,
):
    gen_count = lax.axis_size("gen")
    per_device = nbr_embed.shape[0]
    row_size = per_device * lax.axis_size("enc")
    capacity = max(2, 2 * row_size // gen_count)
    tables = routing(nbr_index, lax.axis_index("gen"), gen_count, per_device, row_size, capacity)
    grad_encoded, grad_key, grad_out_proj, grad_value = (
        whole(
            tables,
            nbr_embed,
            enc_gain,
            gain,
            enc_qkv,
            enc_out,
            hidden_states,
            grad_out,
            w_query,
            w_out,
            w_key,
            w_value,
        )
    )
    return widen((grad_encoded, grad_out_proj, grad_key, grad_value))


def solution(mesh):
    return jax.shard_map(
        local,
        mesh=mesh,
        in_specs=(
            P("gen", None),
            P("gen", None),
            P(("enc", "gen"), None, None),
            P(),
            P(),
            P(None, "enc"),
            P("enc", None),
            P(None, "enc"),
            P(None, "enc"),
            P(),
            P(),
            P(),
        ),
        out_specs=(
            P(("enc", "gen"), None, None),
            P("enc", "gen"),
            P("gen", "enc"),
            P("gen", "enc"),
        ),
        check_vma=False,
    )
```

```python
import functools
import types

import jax
import jax.numpy as jnp
from jax import lax
from jax.experimental import pallas as pl
from jax.experimental.pallas import tpu as pltpu
from jax.sharding import PartitionSpec as P

EH = 8
CH = 64
SOFTCAP = 5.0
EPSILON = 1e-06
MESH = pl.DeviceIdType.MESH


def neighbours():
    enc, gen = lax.axis_index("enc"), lax.axis_index("gen")
    z, core, x, y = enc // 2, enc % 2, gen // 4, gen % 4

    def at(axis, step):
        if axis == "x":
            return (enc, (x + step) % 4 * 4 + y)
        if axis == "y":
            return (enc, x * 4 + (y + step) % 4)
        if axis == "z":
            return ((z + step) % 4 * 2 + core, gen)
        return (z * 2 + (1 - core), gen)

    return enc, gen, {"x": x, "y": y, "z": z, "core": core}, at


def send(src, dst, sems, number, device):
    return pltpu.make_async_remote_copy(
        src_ref=src,
        dst_ref=dst,
        send_sem=sems.at[0, number],
        recv_sem=sems.at[1, number],
        device_id=device,
        device_id_type=MESH,
    )


def add_rows(out, out_at, terms, rows, step):
    def body(i, carry):
        total = None
        for ref, at in terms:
            value = ref[pl.ds(pl.multiple_of(at + i * step, step), step), :].astype(jnp.float32)
            total = value if total is None else total + value
        if len(out.shape) == 3:
            out[out_at + i] = total.astype(out.dtype)
        else:
            out[pl.ds(pl.multiple_of(out_at + i * step, step), step), :] = total.astype(out.dtype)
        return carry

    lax.fori_loop(0, rows // step, body, 0)


class Ring:
    def __init__(self, src, buf, sems, axis, where, at):
        self.src, self.buf = src, buf
        self.rows = src.shape[0] // 4
        self.half = self.rows // 2
        self.me = where[axis]
        half = self.half
        self.plus, self.minus = (self.me + 1) % 4, (self.me + 3) % 4
        across = (self.me + 2) % 4
        pieces = (
            (across, 0, 1),
            (self.plus, 1, 1),
            (self.plus, 0, 1),
            (across, 1, 3),
            (self.minus, 0, 3),
            (self.minus, 1, 3),
        )
        self.copies = []
        for number, (chunk, side, step) in enumerate(pieces):
            start = pl.multiple_of(chunk * self.rows + side * half, half)
            self.copies.append(
                send(
                    src.at[pl.ds(start, half), :],
                    buf.at[pl.ds(number * half, half), :],
                    sems,
                    number,
                    at(axis, step),
                )
            )

    def first(self):
        self.copies[0].start()
        self.copies[3].start()

    def second(self):
        self.copies[1].start()
        self.copies[4].start()

    def third(self, step, with_second=False):
        half = self.half
        self.copies[0].wait_recv()
        if with_second:
            self.copies[3].wait_recv()
            self.second()
        start = self.plus * self.rows
        add_rows(self.src, start, ((self.src, start), (self.buf, 0)), half, step)
        self.copies[2].start()
        if not with_second:
            self.copies[3].wait_recv()
        start = self.minus * self.rows + half
        add_rows(self.src, start, ((self.src, start), (self.buf, 3 * half)), half, step)
        self.copies[5].start()

    def last(self, out, out_at, step):
        half = self.half
        for number in (1, 2, 4, 5):
            self.copies[number].wait_recv()
        start = self.me * self.rows
        add_rows(out, out_at, ((self.src, start), (self.buf, 2 * half), (self.buf, 4 * half)), half, step)
        add_rows(
            out, out_at + (half // step if len(out.shape) == 3 else half), ((self.src, start + half), (self.buf, half), (self.buf, 5 * half)), half, step
        )

    def drain(self):
        for copy in self.copies:
            copy.wait_send()


HALVES = 2
DOWN = (((0,), (0,)), ((), ()))
ACROSS = (((1,), (1,)), ((), ()))


def dot(a, b, dims=(((1,), (0,)), ((), ()))):
    return lax.dot_general(a, b, dims, preferred_element_type=jnp.float32)


def loop(low, high, body):
    def step(i, carry):
        body(i)
        return carry

    lax.fori_loop(low, high, step, 0)


def rows_of(start, size):
    return pl.ds(pl.multiple_of(start, size), size)


def normalise(values, gain, out):
    def body(i):
        at = rows_of(i * 16, 16)
        wide = values[at, :].astype(jnp.float32)
        factor = lax.rsqrt(jnp.mean(wide * wide, axis=-1, keepdims=True) + EPSILON)
        out[at, :] = (wide * factor * gain[...]).astype(jnp.bfloat16)

    loop(0, values.shape[0] // 16, body)


def softcapped(q, k):
    scale = q.shape[-1] ** (-0.5)
    slope = jnp.tanh(dot(q, k, ACROSS) * (scale / SOFTCAP))
    expo = jnp.exp(SOFTCAP * slope)
    return slope, expo / jnp.sum(expo, axis=-1, keepdims=True)


def encoder_attention(i, projected, attended):
    at = rows_of(i * 128, 128)
    for h in range(EH):
        q, k, v = (projected[at, part * 1024 + h * 128 : part * 1024 + h * 128 + 128] for part in range(3))
        _, probs = softcapped(q, k)
        attended[at, h * 128 : h * 128 + 128] = dot(probs.astype(jnp.bfloat16), v).astype(jnp.bfloat16)


def pair_refs(b, p, r):
    keys, rows = rows_of(b * 32, 32), rows_of((b * 2 + p) * 128, 128)
    k = r.kv[:, keys, p * 256 : p * 256 + 256].reshape(256, 256)
    v = r.kv[:, keys, 512 + p * 256 : 512 + p * 256 + 256].reshape(256, 256)
    return keys, rows, k, v


def pair_probs(k, q_pair):
    slope = jnp.tanh(dot(k, q_pair, ACROSS) * (128 ** (-0.5) / SOFTCAP))
    expo = jnp.exp(SOFTCAP * slope)
    return slope, expo * (1.0 / jnp.sum(expo, axis=0, keepdims=True))


def attention_forward(b, r, mixed):
    tokens = rows_of(b * CH, CH)
    for p in range(2):
        keys, rows, k, v = pair_refs(b, p, r)
        slope, probs = pair_probs(k, r.q_pairs[rows, :])
        low = probs.astype(jnp.bfloat16)
        lanes = pl.ds(pl.multiple_of((b * 2 + p) * 128, 128), 128)
        r.wo[0:256, lanes] = low
        r.wo[256:512, lanes] = ((1.0 - slope * slope) * 128 ** (-0.5)).astype(jnp.bfloat16)
        both = dot(low, v, DOWN).astype(jnp.bfloat16)
        mixed[tokens, p * 256 : p * 256 + 128] = both[0:64, 0:128]
        mixed[tokens, p * 256 + 128 : p * 256 + 256] = both[64:128, 128:256]


def attention_backward(b, r):
    for p in range(2):
        keys, rows, k, v = pair_refs(b, p, r)
        q_pair, dm_pair = r.q_pairs[rows, :], r.dm_pairs[rows, :]
        lanes = pl.ds(pl.multiple_of((b * 2 + p) * 128, 128), 128)
        low, slope = r.wo[0:256, lanes], r.wo[256:512, lanes].astype(jnp.float32)
        probs = low.astype(jnp.float32)
        d_probs = dot(v, dm_pair, ACROSS)
        d_capped = probs * (d_probs - jnp.sum(probs * d_probs, axis=0, keepdims=True))
        d_raw = (d_capped * slope).astype(jnp.bfloat16)
        d_keys = dot(d_raw, q_pair).astype(jnp.bfloat16)
        d_values = dot(low, dm_pair).astype(jnp.bfloat16)
        r.dkv[:, keys, p * 256 : p * 256 + 256] = d_keys.reshape(8, 32, 256)
        r.dkv[:, keys, 512 + p * 256 : 512 + p * 256 + 256] = d_values.reshape(8, 32, 256)


class Exchange:
    def __init__(self, count, copy):
        self.count, self.copy = count, copy

    def start(self):
        loop(1, self.count, lambda step: self.copy(step).start())

    def receive(self):
        loop(1, self.count, lambda step: self.copy(step).wait_recv())

    def drain(self):
        loop(1, self.count, lambda step: self.copy(step).wait_send())


def whole_kernel(tree, *refs):
    r = jax.tree.unflatten(tree, refs)
    r = types.SimpleNamespace(**{name: ref for part in r for name, ref in part.items()})
    r.ringed = types.SimpleNamespace(**r.ringed)

    def load(number):
        src = (r.eo_hbm, r.hidden_hbm, r.wq_hbm, r.cot_hbm, r.wo_hbm, r.wk_hbm, r.wv_hbm)[number]
        w_pair = [r.wkv.at[:, pl.ds(at, 512)] for at in (0, 512)]
        dst = (r.eo, r.hidden, r.wq, r.cot, r.wo, *w_pair)[number]
        return pltpu.make_async_copy(src, dst, r.load_sems.at[number])

    def load_third(third):
        lanes = pl.ds(third * 1024, 1024)
        return pltpu.make_async_copy(r.qkv_hbm.at[:, lanes], r.qkv.at[:, lanes], r.load_sems.at[7 + third])

    for third in range(3):
        load_third(third).start()
    load(0).start()
    enc, gen, where, at = neighbours()
    x, y, z, core = where["x"], where["y"], where["z"], where["core"]
    barrier = pltpu.get_barrier_semaphore()
    loop(1, 16, lambda step: pl.semaphore_signal(barrier, inc=1, device_id=(enc, (gen + step) % 16), device_id_type=MESH))
    loop(1, 8, lambda step: pl.semaphore_signal(barrier, inc=1, device_id=((enc + step) % 8, gen), device_id_type=MESH))

    normalise(r.nbr, r.enc_gain, r.enc_normed)
    for third in range(3):
        load_third(third).wait()
        lanes = slice(third * 1024, third * 1024 + 1024)
        r.projected[:, lanes] = dot(r.enc_normed[...], r.qkv[:, lanes]).astype(jnp.bfloat16)
    for number in range(1, 7):
        load(number).start()
    loop(0, 2, lambda i: encoder_attention(i, r.projected, r.enc_normed))
    load(0).wait()

    def finish(half):
        lanes = slice(half * 512, half * 512 + 512)
        update = dot(r.enc_normed[...], r.eo[:, lanes])
        low = (r.nbr[:, lanes].astype(jnp.float32) + update).astype(jnp.bfloat16)
        r.encoded[:, :, lanes] = low.reshape(2, 128, 512)

    finish(0)
    pl.semaphore_wait(barrier, 22)

    own_rows = rows_of(enc * 16, 16)

    def out_enc(half):
        lanes = pl.ds(half * 512, 512)

        def copy(step):
            peer = (enc + step) % 8
            return send(
                r.encoded.at[:, rows_of(peer * 16, 16), lanes],
                r.columns[half].at[pl.ds(enc * 2, 2)],
                r.s_oenc[half],
                step - 1,
                (peer, gen),
            )

        return Exchange(8, copy)

    def over_gen(half, target, sems):
        def copy(step):
            peer = (gen + step) % 16
            return send(
                r.outgoing[half].at[pl.ds(peer * 2, 2)],
                target[half].at[pl.ds(gen * 2, 2)],
                sems[half],
                step - 1,
                (enc, peer),
            )

        return Exchange(16, copy)

    out_encs = [out_enc(half) for half in range(HALVES)]
    out_gens = [over_gen(half, r.incoming, r.s_ogen) for half in range(HALVES)]
    out_encs[0].start()
    finish(1)
    for half in range(HALVES):
        r.columns[half][pl.ds(enc * 2, 2)] = r.encoded[:, own_rows, half * 512 : half * 512 + 512]

    def pick_out_gen(half):
        for j in range(32):
            r.outgoing[half][j] = r.columns[half][r.send[j]]
        own = pl.ds(gen * 2, 2)
        r.incoming[half][own] = r.outgoing[half][own]

    def store_pairs(out, i, low):
        for block in range(4):
            for head in range(4):
                start = i * 1024 + block * 256 + head // 2 * 128 + head % 2 * 64
                out[rows_of(start, 64), head % 2 * 128 : head % 2 * 128 + 128] = low[
                    block * 64 : block * 64 + 64, head * 128 : head * 128 + 128
                ]

    def query_tile(i):
        low = dot(r.hidden[rows_of(i * 256, 256), :], r.wq[...]).astype(jnp.bfloat16)
        store_pairs(r.q_pairs, i, low)

    def cotangent_tile(i):
        low = dot(r.cot[rows_of(i * 256, 256), :], r.wo[...], ACROSS).astype(jnp.bfloat16)
        store_pairs(r.dm_pairs, i, low)

    r.q_pairs[...] = jnp.zeros_like(r.q_pairs)
    r.dm_pairs[...] = jnp.zeros_like(r.dm_pairs)
    out_encs[0].receive()
    out_encs[1].start()
    pick_out_gen(0)
    out_gens[0].start()
    load(1).wait()
    normalise(r.hidden, r.gain, r.hidden)
    load(2).wait()
    loop(0, 2, query_tile)
    out_encs[1].receive()
    pick_out_gen(1)
    load(3).wait()
    load(4).wait()

    minus, plus, across = (z + 3) % 4 * 2 + core, (z + 1) % 4 * 2 + core, (z + 2) % 4 * 2 + core
    up, down, peer = at("z", 1), at("z", 3), at("core", 1)
    rings, crosses = [], []
    for half in range(HALVES):
        rows = r.rows.at[:, :, pl.ds(half * 512, 512)]
        first, second = pl.ds(0, 128), pl.ds(128, 128)

        def share(ref, sems, number, device):
            return send(ref, ref, sems, number, device)

        rings.append(
            [
                share(rows.at[enc], r.s_ring[half], 0, up),
                share(rows.at[enc], r.s_ring[half], 1, down),
                share(rows.at[minus, first], r.s_ring[half], 2, up),
                share(rows.at[plus, second], r.s_ring[half], 3, down),
            ]
        )
        crosses.append(
            [
                share(rows.at[enc], r.s_cross[half], 0, peer),
                share(rows.at[minus], r.s_cross[half], 1, peer),
                share(rows.at[plus], r.s_cross[half], 2, peer),
                share(rows.at[across, first], r.s_cross[half], 3, peer),
                share(rows.at[across, second], r.s_cross[half], 4, peer),
            ]
        )

    def take_slots(half):
        out_gens[half].receive()
        for j in range(16):
            r.rows[enc, j * 16 : j * 16 + 16, half * 512 : half * 512 + 512] = r.incoming[half][r.receive[j]]

    def gather_own(half):
        rings[half][0].start()
        rings[half][1].start()
        crosses[half][0].start()

    def gather_next(half):
        rings[half][0].wait_recv()
        rings[half][2].start()
        crosses[half][1].start()
        rings[half][1].wait_recv()
        rings[half][3].start()
        crosses[half][2].start()

    def gather_last(half):
        rings[half][2].wait_recv()
        crosses[half][3].start()
        rings[half][3].wait_recv()
        crosses[half][4].start()

    def of_peer(piece):
        return piece + 1 - 2 * core

    def project(piece):
        r.kv[piece] = dot(r.rows[piece], r.wkv[...]).astype(jnp.bfloat16)

    def project_some(pieces):
        def body(i):
            piece = pieces[0]
            for number in range(1, len(pieces)):
                piece = jnp.where(i == number, pieces[number], piece)
            project(piece)

        loop(0, len(pieces), body)

    load(5).wait()
    load(6).wait()
    take_slots(0)
    out_gens[1].start()
    gather_own(0)
    loop(0, 2, cotangent_tile)
    gather_next(0)
    take_slots(1)
    gather_own(1)
    gather_last(0)
    crosses[1][0].wait_recv()
    crosses[0][0].wait_recv()
    project_some((enc, of_peer(enc)))
    gather_next(1)
    for number in (1, 2):
        crosses[0][number].wait_recv()
    project_some((minus, plus))
    for number in (1, 2):
        crosses[1][number].wait_recv()
    project_some((of_peer(minus), of_peer(plus)))
    gather_last(1)
    for number in (3, 4):
        crosses[0][number].wait_recv()
        crosses[1][number].wait_recv()
    project_some((across, of_peer(across)))

    ot_a, ot_b = r.wq.at[:, pl.ds(0, 256)], r.wq.at[:, pl.ds(256, 256)]
    kt, vt = r.eo.at[:, pl.ds(0, 512)], r.eo.at[:, pl.ds(512, 512)]
    mixed, mixed_t = r.hidden.at[:, pl.ds(0, 512)], r.hidden.at[:, pl.ds(512, 512)]
    ring_oa = Ring(ot_a, r.ringed.ota[0], r.ringed.ota[1], "x", where, at)
    ring_ob = Ring(ot_b, r.ringed.otb[0], r.ringed.otb[1], "y", where, at)
    ring_k = Ring(kt, r.ringed.kt[0], r.ringed.kt[1], "x", where, at)
    ring_v = Ring(vt, r.ringed.vt[0], r.ringed.vt[1], "y", where, at)
    ring_oa2 = Ring(r.ot_a2, r.ringed.ota2[0], r.ringed.ota2[1], "y", where, at)
    ring_ob2 = Ring(r.ot_b2, r.ringed.otb2[0], r.ringed.otb2[1], "x", where, at)
    ring_k2 = Ring(r.kt2, r.ringed.kt2[0], r.ringed.kt2[1], "y", where, at)
    ring_v2 = Ring(r.vt2, r.ringed.vt2[0], r.ringed.vt2[1], "x", where, at)
    mine = [r.qkv.at[:, pl.ds(half * 512, 512)] for half in range(HALVES)]
    peers = [r.qkv.at[:, pl.ds(1024 + half * 512, 512)] for half in range(HALVES)]
    from_peer = [r.qkv.at[:, pl.ds(2048 + half * 512, 512)] for half in range(HALVES)]
    ring_z = [Ring(mine[half], r.ring_z[half][0], r.ring_z[half][1], "z", where, at) for half in range(HALVES)]

    loop(0, 8, lambda b: attention_forward(b, r, mixed))
    mixed_t[...] = mixed[...].T

    def out_terms(i):
        to_x, to_y = (x + 2 - i + 4) % 4, (y + 2 - i + 4) % 4

        def tile(j):
            lane_a = pl.multiple_of((to_x * 4 + j) * 256, 256)
            term = dot(mixed_t[0:256, :], r.cot[:, pl.ds(lane_a, 256)])
            ot_a[pl.ds(lane_a, 256), :] = term.astype(jnp.bfloat16)
            lane_b = pl.multiple_of((j * 4 + to_y) * 256, 256)
            term = dot(mixed_t[256:512, :], r.cot[:, pl.ds(lane_b, 256)])
            ot_b[rows_of((to_y * 4 + j) * 256, 256), :] = term.astype(jnp.bfloat16)

        loop(0, 4, tile)

    loop(0, 1, out_terms)
    ring_oa.first()
    ring_ob.first()
    loop(1, 4, out_terms)
    ring_oa.second()
    ring_ob.second()
    loop(0, 8, lambda b: attention_backward(b, r))

    core_copies = [
        [
            send(
                peers[half].at[pl.ds(k * 256, 256), :],
                from_peer[half].at[pl.ds(k * 256, 256), :],
                r.s_core[half],
                k,
                peer,
            )
            for k in range(4)
        ]
        for half in range(HALVES)
    ]

    def enc_piece(half, piece_at, out, out_at):
        feats = slice(half * 512, half * 512 + 512)
        term = dot(r.dkv[piece_at], r.wkv[feats, :], ACROSS)
        out[rows_of(out_at, 256), :] = term.astype(jnp.bfloat16)

    def enc_half(half):
        def to_peer(k):
            enc_piece(half, k * 2 + (1 - core), peers[half], k * 256)
            for number in range(4):

                @pl.when(k == number)
                def _():
                    core_copies[half][number].start()

        loop(0, 4, to_peer)
        loop(0, 4, lambda k: enc_piece(half, k * 2 + core, mine[half], k * 256))

    def add_peer(half):
        for k in range(4):
            core_copies[half][k].wait_recv()
        add_rows(mine[half], 0, ((mine[half], 0), (from_peer[half], 0)), 1024, 64)

    def key_terms(part):
        lanes = pl.ds(pl.multiple_of(part * 128, 128), 128)
        term = dot(r.rows[:, :, lanes].reshape(2048, 128), r.dkv[...].reshape(2048, 1024), DOWN)
        low = term.astype(jnp.bfloat16)
        kt[rows_of(part * 128, 128), :] = low[:, 0:512]
        for side in range(2):
            to_x, to_y = (part * 2 + side) // 4, (part * 2 + side) % 4
            vt[rows_of(to_y * 256 + to_x * 64, 64), :] = low[side * 64 : side * 64 + 64, 512:1024]

    enc_half(0)
    add_peer(0)
    ring_z[0].first()
    ring_oa.third(64)
    ring_ob.third(64)
    loop(0, 4, key_terms)
    ring_z[0].third(64, True)
    loop(4, 8, key_terms)
    ring_k.first()
    ring_v.first()
    ring_k.second()
    ring_v.second()
    enc_half(1)
    add_peer(1)
    ring_z[1].first()

    back_gens = [over_gen(half, r.returned, r.s_bgen) for half in range(HALVES)]

    def start_back_gen(half):
        ring_z[half].last(r.piece[half], 0, 16)
        out_gens[half].drain()
        for j in range(32):
            r.outgoing[half][j] = r.piece[half][r.position[j]]
        back_gens[half].start()
        own = pl.ds(gen * 2, 2)
        r.returned[half][own] = r.outgoing[half][own]

    def back_enc(half):
        def copy(step):
            to = (enc + step) % 8
            return send(
                r.grads[half].at[to],
                r.home.at[:, own_rows, pl.ds(half * 512, 512)],
                r.s_benc[half],
                step - 1,
                (to, gen),
            )

        return Exchange(8, copy)

    back_encs = [back_enc(half) for half in range(HALVES)]

    def start_back_enc(half):
        back_gens[half].receive()
        for j in range(16):
            r.grads[half][j // 2, j % 2] = r.returned[half][r.column[j]]
        back_encs[half].start()
        r.home[:, own_rows, half * 512 : half * 512 + 512] = r.grads[half][enc]

    start_back_gen(0)
    ring_oa.last(r.ot_a2, 0, 64)
    ring_oa2.first()
    ring_oa2.second()
    ring_ob.last(r.ot_b2, 0, 64)
    ring_ob2.first()
    ring_ob2.second()
    ring_z[1].third(64, True)
    ring_k.third(64)
    ring_v.third(64)
    ring_oa2.third(64)
    ring_ob2.third(64)
    start_back_gen(1)
    start_back_enc(0)
    ring_k.last(r.kt2, 0, 64)
    ring_k2.first()
    ring_k2.second()
    ring_v.last(r.vt2, 0, 64)
    ring_v2.first()
    ring_v2.second()
    ring_oa2.last(r.wo_out, 0, 64)
    ring_ob2.last(r.wo_out, 256, 64)
    ring_k2.third(32)
    ring_v2.third(32)
    start_back_enc(1)
    ring_k2.last(r.wk_out, 0, 32)
    ring_v2.last(r.wv_out, 0, 32)
    for half in range(HALVES):
        back_encs[half].receive()
    r.enc_out[...] = r.home[...]

    rings_all = [ring_oa, ring_ob, ring_k, ring_v, ring_oa2, ring_ob2, ring_k2, ring_v2] + ring_z
    for ring in rings_all:
        ring.drain()
    for half in range(HALVES):
        for copy in core_copies[half] + rings[half] + crosses[half]:
            copy.wait_send()
        for exchange in (out_encs[half], back_gens[half], back_encs[half]):
            exchange.drain()


def whole(tables, nbr, enc_gain, gain, qkv, eo, hidden, cot, wq, wo, wk, wv):
    low = jnp.bfloat16
    vmem = lambda *shape: pltpu.VMEM(shape, low)
    sems = lambda *shape: pltpu.SemaphoreType.DMA(shape)
    both = lambda make, *shape: [make(*shape) for _ in range(HALVES)]
    ring = lambda count, width: [vmem(count // 4 * 3, width), sems(2, 6)]
    anywhere = pl.BlockSpec(memory_space=pl.ANY)
    scalars = pl.BlockSpec(memory_space=pltpu.SMEM)
    local = pl.BlockSpec(memory_space=pltpu.VMEM)
    send_table, position_table, receive_table, column_table = tables
    small = dict(send=send_table, position=position_table, receive=receive_table, column=column_table)
    near = dict(nbr=nbr.reshape(256, 1024), enc_gain=enc_gain.reshape(1, -1), gain=gain.reshape(1, -1))
    big = dict(
        qkv_hbm=qkv, eo_hbm=eo, hidden_hbm=hidden, wq_hbm=wq, cot_hbm=cot, wo_hbm=wo, wk_hbm=wk, wv_hbm=wv
    )
    outputs = dict(
        enc_out=jax.ShapeDtypeStruct((2, 128, 1024), low),
        wo_out=jax.ShapeDtypeStruct((512, 256), low),
        wk_out=jax.ShapeDtypeStruct((64, 512), low),
        wv_out=jax.ShapeDtypeStruct((64, 512), low),
    )
    scratch = dict(
        qkv=vmem(1024, 3072),
        eo=vmem(1024, 1024),
        hidden=vmem(512, 4096),
        wq=vmem(4096, 512),
        cot=vmem(512, 4096),
        wo=vmem(512, 4096),
        wkv=vmem(1024, 1024),
        enc_normed=vmem(256, 1024),
        projected=vmem(256, 3072),
        encoded=vmem(2, 128, 1024),
        q_pairs=vmem(2048, 256),
        dm_pairs=vmem(2048, 256),
        kv=vmem(8, 256, 1024),
        dkv=vmem(8, 256, 1024),
        rows=vmem(8, 256, 1024),
        ot_a2=vmem(1024, 256),
        ot_b2=vmem(1024, 256),
        kt2=vmem(256, 512),
        vt2=vmem(256, 512),
        home=vmem(2, 128, 1024),
        ringed=dict(
            ota=ring(4096, 256),
            otb=ring(4096, 256),
            kt=ring(1024, 512),
            vt=ring(1024, 512),
            ota2=ring(1024, 256),
            otb2=ring(1024, 256),
            kt2=ring(256, 512),
            vt2=ring(256, 512),
        ),
        ring_z=both(ring, 1024, 512),
        columns=both(vmem, 16, 16, 512),
        outgoing=both(vmem, 32, 16, 512),
        incoming=both(vmem, 32, 16, 512),
        returned=both(vmem, 32, 16, 512),
        piece=both(vmem, 16, 16, 512),
        grads=both(vmem, 8, 2, 16, 512),
        s_oenc=both(sems, 2, 7),
        s_benc=both(sems, 2, 7),
        s_ogen=both(sems, 2, 15),
        s_bgen=both(sems, 2, 15),
        s_ring=both(sems, 2, 4),
        s_cross=both(sems, 2, 5),
        s_core=both(sems, 2, 4),
        load_sems=sems(10),
    )
    operands = small | near | big
    leaves, _ = jax.tree.flatten(scratch)
    tree = jax.tree.structure((operands, outputs, scratch))
    by_name = lambda part: [part[name] for name in sorted(part)]
    place = dict.fromkeys(small, scalars) | dict.fromkeys(near, local) | dict.fromkeys(big, anywhere)
    return pl.pallas_call(
        functools.partial(whole_kernel, tree),
        name="retro_whole",
        out_shape=tuple(by_name(outputs)),
        in_specs=by_name(place),
        out_specs=(local,) * len(outputs),
        scratch_shapes=leaves,
        compiler_params=pltpu.CompilerParams(
            collective_id=1, has_side_effects=True, vmem_limit_bytes=61 * 1024 * 1024
        ),
    )(*by_name(operands))


def widen_kernel(*refs):
    sources, targets, near, sems = refs[:4], refs[4:8], refs[8:12], refs[12]
    copies = [
        pltpu.make_async_copy(src, dst, sems.at[number]) for number, (src, dst) in enumerate(zip(sources, near))
    ]
    for copy in copies:
        copy.start()
    for copy, src, dst in zip(copies, near, targets):
        copy.wait()
        dst[...] = src[...].astype(jnp.float32)


def widen(values):
    return pl.pallas_call(
        widen_kernel,
        name="widen",
        out_shape=tuple(jax.ShapeDtypeStruct(value.shape, jnp.float32) for value in values),
        in_specs=[pl.BlockSpec(memory_space=pl.ANY)] * 4,
        out_specs=(pl.BlockSpec(memory_space=pltpu.VMEM),) * 4,
        scratch_shapes=[pltpu.VMEM(value.shape, value.dtype) for value in values] + [pltpu.SemaphoreType.DMA((4,))],
        compiler_params=pltpu.CompilerParams(vmem_limit_bytes=60 * 1024 * 1024),
    )(*values)


def routing(nbr_index, row_index, gen_count, per_device, row_size, capacity):
    entries = nbr_index.reshape(gen_count, row_size)
    source = entries // per_device % gen_count
    column = entries // (per_device * gen_count) * per_device + entries % per_device
    places = jnp.arange(row_size, dtype=jnp.int32)
    same = (source[:, :, None] == source[:, None, :]) & (places[None, None, :] < places[None, :, None])
    rank = jnp.sum(same.astype(jnp.int32), axis=2)
    rows = jnp.arange(gen_count, dtype=jnp.int32)
    send_slot = (rows[:, None] * capacity + rank).reshape(-1)
    mine = (source == row_index).reshape(-1)
    flat_column = column.reshape(-1)
    buffers = jnp.arange(gen_count * capacity, dtype=jnp.int32)
    send_match = (send_slot[:, None] == buffers[None, :]) & mine[:, None]
    send_column = jnp.sum(jnp.where(send_match, flat_column[:, None], 0), axis=0)
    column_match = (flat_column[:, None] == places[None, :]) & mine[:, None]
    column_position = jnp.sum(jnp.where(column_match, send_slot[:, None], 0), axis=0)
    own = (rows == row_index)[:, None]
    receive_position = jnp.sum(jnp.where(own, source * capacity + rank, 0), axis=0)
    receive_match = receive_position[:, None] == buffers[None, :]
    position_slot = jnp.sum(jnp.where(receive_match, places[:, None], 0), axis=0)
    return (send_column, position_slot, receive_position, column_position)


def local(
    hidden_states,
    grad_out,
    nbr_embed,
    nbr_index,
    gain,
    w_query,
    w_out,
    w_key,
    w_value,
    enc_gain,
    enc_qkv,
    enc_out,
):
    gen_count = lax.axis_size("gen")
    per_device = nbr_embed.shape[0]
    row_size = per_device * lax.axis_size("enc")
    capacity = max(2, 2 * row_size // gen_count)
    tables = routing(nbr_index, lax.axis_index("gen"), gen_count, per_device, row_size, capacity)
    grad_encoded, grad_key, grad_out_proj, grad_value = (
        whole(
            tables,
            nbr_embed,
            enc_gain,
            gain,
            enc_qkv,
            enc_out,
            hidden_states,
            grad_out,
            w_query,
            w_out,
            w_key,
            w_value,
        )
    )
    return widen((grad_encoded, grad_out_proj, grad_key, grad_value))


def solution(mesh):
    return jax.shard_map(
        local,
        mesh=mesh,
        in_specs=(
            P("gen", None),
            P("gen", None),
            P(("enc", "gen"), None, None),
            P(),
            P(),
            P(None, "enc"),
            P("enc", None),
            P(None, "enc"),
            P(None, "enc"),
            P(),
            P(),
            P(),
        ),
        out_specs=(
            P(("enc", "gen"), None, None),
            P("enc", "gen"),
            P("gen", "enc"),
            P("gen", "enc"),
        ),
        check_vma=False,
    )
```

```python
import functools
import types

import jax
import jax.numpy as jnp
from jax import lax
from jax.experimental import pallas as pl
from jax.experimental.pallas import tpu as pltpu
from jax.sharding import PartitionSpec as P

EH = 8
CH = 64
SOFTCAP = 5.0
EPSILON = 1e-06
MESH = pl.DeviceIdType.MESH


def neighbours():
    enc, gen = lax.axis_index("enc"), lax.axis_index("gen")
    z, core, x, y = enc // 2, enc % 2, gen // 4, gen % 4

    def at(axis, step):
        if axis == "x":
            return (enc, (x + step) % 4 * 4 + y)
        if axis == "y":
            return (enc, x * 4 + (y + step) % 4)
        if axis == "z":
            return ((z + step) % 4 * 2 + core, gen)
        return (z * 2 + (1 - core), gen)

    return enc, gen, {"x": x, "y": y, "z": z, "core": core}, at


def send(src, dst, sems, number, device):
    return pltpu.make_async_remote_copy(
        src_ref=src,
        dst_ref=dst,
        send_sem=sems.at[0, number],
        recv_sem=sems.at[1, number],
        device_id=device,
        device_id_type=MESH,
    )


def add_rows(out, out_at, terms, rows, step):
    def body(i, carry):
        total = None
        for ref, at in terms:
            value = ref[pl.ds(pl.multiple_of(at + i * step, step), step), :].astype(jnp.float32)
            total = value if total is None else total + value
        if len(out.shape) == 3:
            out[out_at + i] = total.astype(out.dtype)
        else:
            out[pl.ds(pl.multiple_of(out_at + i * step, step), step), :] = total.astype(out.dtype)
        return carry

    lax.fori_loop(0, rows // step, body, 0)


class Ring:
    def __init__(self, src, buf, sems, axis, where, at):
        self.src, self.buf = src, buf
        self.rows = src.shape[0] // 4
        self.half = self.rows // 2
        self.me = where[axis]
        half = self.half
        self.plus, self.minus = (self.me + 1) % 4, (self.me + 3) % 4
        across = (self.me + 2) % 4
        pieces = (
            (across, 0, 1),
            (self.plus, 1, 1),
            (self.plus, 0, 1),
            (across, 1, 3),
            (self.minus, 0, 3),
            (self.minus, 1, 3),
        )
        self.copies = []
        for number, (chunk, side, step) in enumerate(pieces):
            start = pl.multiple_of(chunk * self.rows + side * half, half)
            self.copies.append(
                send(
                    src.at[pl.ds(start, half), :],
                    buf.at[pl.ds(number * half, half), :],
                    sems,
                    number,
                    at(axis, step),
                )
            )

    def first(self):
        self.copies[0].start()
        self.copies[3].start()

    def second(self):
        self.copies[1].start()
        self.copies[4].start()

    def third(self, step, with_second=False):
        half = self.half
        self.copies[0].wait_recv()
        if with_second:
            self.copies[3].wait_recv()
            self.second()
        start = self.plus * self.rows
        add_rows(self.src, start, ((self.src, start), (self.buf, 0)), half, step)
        self.copies[2].start()
        if not with_second:
            self.copies[3].wait_recv()
        start = self.minus * self.rows + half
        add_rows(self.src, start, ((self.src, start), (self.buf, 3 * half)), half, step)
        self.copies[5].start()

    def last(self, out, out_at, step):
        half = self.half
        for number in (1, 2, 4, 5):
            self.copies[number].wait_recv()
        start = self.me * self.rows
        add_rows(out, out_at, ((self.src, start), (self.buf, 2 * half), (self.buf, 4 * half)), half, step)
        add_rows(
            out, out_at + (half // step if len(out.shape) == 3 else half), ((self.src, start + half), (self.buf, half), (self.buf, 5 * half)), half, step
        )

    def drain(self):
        for copy in self.copies:
            copy.wait_send()


HALVES = 2
DOWN = (((0,), (0,)), ((), ()))
ACROSS = (((1,), (1,)), ((), ()))


def dot(a, b, dims=(((1,), (0,)), ((), ()))):
    return lax.dot_general(a, b, dims, preferred_element_type=jnp.float32)


def loop(low, high, body):
    def step(i, carry):
        body(i)
        return carry

    lax.fori_loop(low, high, step, 0)


def rows_of(start, size):
    return pl.ds(pl.multiple_of(start, size), size)


def normalise(values, gain, out):
    def body(i):
        at = rows_of(i * 16, 16)
        wide = values[at, :].astype(jnp.float32)
        factor = lax.rsqrt(jnp.mean(wide * wide, axis=-1, keepdims=True) + EPSILON)
        out[at, :] = (wide * factor * gain[...]).astype(jnp.bfloat16)

    loop(0, values.shape[0] // 16, body)


def softcapped(q, k):
    scale = q.shape[-1] ** (-0.5)
    slope = jnp.tanh(dot(q, k, ACROSS) * (scale / SOFTCAP))
    expo = jnp.exp(SOFTCAP * slope)
    return slope, expo / jnp.sum(expo, axis=-1, keepdims=True)


def encoder_attention(i, projected, attended):
    at = rows_of(i * 128, 128)
    for h in range(EH):
        q, k, v = (projected[at, part * 1024 + h * 128 : part * 1024 + h * 128 + 128] for part in range(3))
        _, probs = softcapped(q, k)
        attended[at, h * 128 : h * 128 + 128] = dot(probs.astype(jnp.bfloat16), v).astype(jnp.bfloat16)


def pair_refs(b, p, r):
    keys, rows = rows_of(b * 32, 32), rows_of((b * 2 + p) * 128, 128)
    k = r.kv[:, keys, p * 256 : p * 256 + 256].reshape(256, 256)
    v = r.kv[:, keys, 512 + p * 256 : 512 + p * 256 + 256].reshape(256, 256)
    return keys, rows, k, v


def pair_probs(k, q_pair):
    slope = jnp.tanh(dot(k, q_pair, ACROSS) * (128 ** (-0.5) / SOFTCAP))
    expo = jnp.exp(SOFTCAP * slope)
    return slope, expo * (1.0 / jnp.sum(expo, axis=0, keepdims=True))


def attention_forward(b, r, mixed):
    tokens = rows_of(b * CH, CH)
    for p in range(2):
        keys, rows, k, v = pair_refs(b, p, r)
        slope, probs = pair_probs(k, r.q_pairs[rows, :])
        low = probs.astype(jnp.bfloat16)
        lanes = pl.ds(pl.multiple_of((b * 2 + p) * 128, 128), 128)
        r.wo[0:256, lanes] = low
        r.wo[256:512, lanes] = ((1.0 - slope * slope) * 128 ** (-0.5)).astype(jnp.bfloat16)
        both = dot(low, v, DOWN).astype(jnp.bfloat16)
        mixed[tokens, p * 256 : p * 256 + 128] = both[0:64, 0:128]
        mixed[tokens, p * 256 + 128 : p * 256 + 256] = both[64:128, 128:256]


def attention_backward(b, r):
    for p in range(2):
        keys, rows, k, v = pair_refs(b, p, r)
        q_pair, dm_pair = r.q_pairs[rows, :], r.dm_pairs[rows, :]
        lanes = pl.ds(pl.multiple_of((b * 2 + p) * 128, 128), 128)
        low, slope = r.wo[0:256, lanes], r.wo[256:512, lanes].astype(jnp.float32)
        probs = low.astype(jnp.float32)
        d_probs = dot(v, dm_pair, ACROSS)
        d_capped = probs * (d_probs - jnp.sum(probs * d_probs, axis=0, keepdims=True))
        d_raw = (d_capped * slope).astype(jnp.bfloat16)
        d_keys = dot(d_raw, q_pair).astype(jnp.bfloat16)
        d_values = dot(low, dm_pair).astype(jnp.bfloat16)
        r.dkv[:, keys, p * 256 : p * 256 + 256] = d_keys.reshape(8, 32, 256)
        r.dkv[:, keys, 512 + p * 256 : 512 + p * 256 + 256] = d_values.reshape(8, 32, 256)


class Exchange:
    def __init__(self, count, copy):
        self.count, self.copy = count, copy

    def start(self):
        loop(1, self.count, lambda step: self.copy(step).start())

    def receive(self):
        loop(1, self.count, lambda step: self.copy(step).wait_recv())

    def drain(self):
        loop(1, self.count, lambda step: self.copy(step).wait_send())


def whole_kernel(tree, *refs):
    r = jax.tree.unflatten(tree, refs)
    r = types.SimpleNamespace(**{name: ref for part in r for name, ref in part.items()})
    r.ringed = types.SimpleNamespace(**r.ringed)

    def load(number):
        src = (r.eo_hbm, r.hidden_hbm, r.wq_hbm, r.cot_hbm, r.wo_hbm, r.wk_hbm, r.wv_hbm)[number]
        w_pair = [r.wkv.at[:, pl.ds(at, 512)] for at in (0, 512)]
        dst = (r.eo, r.hidden, r.wq, r.cot, r.wo, *w_pair)[number]
        return pltpu.make_async_copy(src, dst, r.load_sems.at[number])

    def load_third(third):
        lanes = pl.ds(third * 1024, 1024)
        return pltpu.make_async_copy(r.qkv_hbm.at[:, lanes], r.qkv.at[:, lanes], r.load_sems.at[7 + third])

    for third in range(3):
        load_third(third).start()
    load(0).start()
    enc, gen, where, at = neighbours()
    x, y, z, core = where["x"], where["y"], where["z"], where["core"]
    barrier = pltpu.get_barrier_semaphore()
    loop(1, 16, lambda step: pl.semaphore_signal(barrier, inc=1, device_id=(enc, (gen + step) % 16), device_id_type=MESH))
    loop(1, 8, lambda step: pl.semaphore_signal(barrier, inc=1, device_id=((enc + step) % 8, gen), device_id_type=MESH))

    normalise(r.nbr, r.enc_gain, r.enc_normed)
    for third in range(3):
        load_third(third).wait()
        lanes = slice(third * 1024, third * 1024 + 1024)
        r.projected[:, lanes] = dot(r.enc_normed[...], r.qkv[:, lanes]).astype(jnp.bfloat16)
    for number in range(1, 7):
        load(number).start()
    loop(0, 2, lambda i: encoder_attention(i, r.projected, r.enc_normed))
    load(0).wait()

    def finish(half):
        lanes = slice(half * 512, half * 512 + 512)
        update = dot(r.enc_normed[...], r.eo[:, lanes])
        low = (r.nbr[:, lanes].astype(jnp.float32) + update).astype(jnp.bfloat16)
        r.encoded[:, :, lanes] = low.reshape(2, 128, 512)

    finish(0)
    pl.semaphore_wait(barrier, 22)

    own_rows = rows_of(enc * 16, 16)

    def out_enc(half):
        lanes = pl.ds(half * 512, 512)

        def copy(step):
            peer = (enc + step) % 8
            return send(
                r.encoded.at[:, rows_of(peer * 16, 16), lanes],
                r.columns[half].at[pl.ds(enc * 2, 2)],
                r.s_oenc[half],
                step - 1,
                (peer, gen),
            )

        return Exchange(8, copy)

    def over_gen(half, target, sems):
        def copy(step):
            peer = (gen + step) % 16
            return send(
                r.outgoing[half].at[pl.ds(peer * 2, 2)],
                target[half].at[pl.ds(gen * 2, 2)],
                sems[half],
                step - 1,
                (enc, peer),
            )

        return Exchange(16, copy)

    out_encs = [out_enc(half) for half in range(HALVES)]
    out_gens = [over_gen(half, r.incoming, r.s_ogen) for half in range(HALVES)]
    out_encs[0].start()
    finish(1)
    for half in range(HALVES):
        r.columns[half][pl.ds(enc * 2, 2)] = r.encoded[:, own_rows, half * 512 : half * 512 + 512]

    def pick_out_gen(half):
        for j in range(32):
            r.outgoing[half][j] = r.columns[half][r.send[j]]
        own = pl.ds(gen * 2, 2)
        r.incoming[half][own] = r.outgoing[half][own]

    def store_pairs(out, i, low):
        for block in range(4):
            for head in range(4):
                start = i * 1024 + block * 256 + head // 2 * 128 + head % 2 * 64
                out[rows_of(start, 64), head % 2 * 128 : head % 2 * 128 + 128] = low[
                    block * 64 : block * 64 + 64, head * 128 : head * 128 + 128
                ]

    def query_tile(i):
        low = dot(r.hidden[rows_of(i * 256, 256), :], r.wq[...]).astype(jnp.bfloat16)
        store_pairs(r.q_pairs, i, low)

    def cotangent_tile(i):
        low = dot(r.cot[rows_of(i * 256, 256), :], r.wo[...], ACROSS).astype(jnp.bfloat16)
        store_pairs(r.dm_pairs, i, low)

    r.q_pairs[...] = jnp.zeros_like(r.q_pairs)
    r.dm_pairs[...] = jnp.zeros_like(r.dm_pairs)
    out_encs[0].receive()
    out_encs[1].start()
    pick_out_gen(0)
    out_gens[0].start()
    load(1).wait()
    normalise(r.hidden, r.gain, r.hidden)
    load(2).wait()
    loop(0, 2, query_tile)
    out_encs[1].receive()
    pick_out_gen(1)
    load(3).wait()
    load(4).wait()

    minus, plus, across = (z + 3) % 4 * 2 + core, (z + 1) % 4 * 2 + core, (z + 2) % 4 * 2 + core
    up, down, peer = at("z", 1), at("z", 3), at("core", 1)
    rings, crosses = [], []
    for half in range(HALVES):
        rows = r.rows.at[:, :, pl.ds(half * 512, 512)]
        first, second = pl.ds(0, 128), pl.ds(128, 128)

        def share(ref, sems, number, device):
            return send(ref, ref, sems, number, device)

        rings.append(
            [
                share(rows.at[enc, first], r.s_ring[half], 0, up),
                share(rows.at[enc, second], r.s_ring[half], 1, down),
                share(rows.at[minus, first], r.s_ring[half], 2, up),
                share(rows.at[plus, second], r.s_ring[half], 3, down),
                share(rows.at[enc, second], r.s_ring[half], 4, up),
                share(rows.at[enc, first], r.s_ring[half], 5, down),
            ]
        )
        crosses.append(
            [
                share(rows.at[enc], r.s_cross[half], 0, peer),
                share(rows.at[minus], r.s_cross[half], 1, peer),
                share(rows.at[plus], r.s_cross[half], 2, peer),
                share(rows.at[across, first], r.s_cross[half], 3, peer),
                share(rows.at[across, second], r.s_cross[half], 4, peer),
            ]
        )

    def take_slots(half):
        out_gens[half].receive()
        for j in range(16):
            r.rows[enc, j * 16 : j * 16 + 16, half * 512 : half * 512 + 512] = r.incoming[half][r.receive[j]]

    def gather_own(half):
        rings[half][0].start()
        rings[half][1].start()
        rings[half][4].start()
        rings[half][5].start()
        crosses[half][0].start()

    def gather_next(half):
        rings[half][0].wait_recv()
        rings[half][2].start()
        rings[half][1].wait_recv()
        rings[half][3].start()
        rings[half][4].wait_recv()
        crosses[half][1].start()
        rings[half][5].wait_recv()
        crosses[half][2].start()

    def gather_last(half):
        rings[half][2].wait_recv()
        crosses[half][3].start()
        rings[half][3].wait_recv()
        crosses[half][4].start()

    def of_peer(piece):
        return piece + 1 - 2 * core

    def project(piece):
        r.kv[piece] = dot(r.rows[piece], r.wkv[...]).astype(jnp.bfloat16)

    def project_some(pieces):
        def body(i):
            piece = pieces[0]
            for number in range(1, len(pieces)):
                piece = jnp.where(i == number, pieces[number], piece)
            project(piece)

        loop(0, len(pieces), body)

    load(5).wait()
    load(6).wait()
    take_slots(0)
    gather_own(0)
    out_gens[1].start()
    loop(0, 2, cotangent_tile)
    gather_next(0)
    take_slots(1)
    gather_own(1)
    gather_last(0)
    crosses[1][0].wait_recv()
    crosses[0][0].wait_recv()
    project_some((enc, of_peer(enc)))
    gather_next(1)
    for number in (1, 2):
        crosses[0][number].wait_recv()
    project_some((minus, plus))
    for number in (1, 2):
        crosses[1][number].wait_recv()
    project_some((of_peer(minus), of_peer(plus)))
    gather_last(1)
    project_some((across,))
    for number in (3, 4):
        crosses[0][number].wait_recv()
        crosses[1][number].wait_recv()
    project_some((of_peer(across),))

    ot_a, ot_b = r.wq.at[:, pl.ds(0, 256)], r.wq.at[:, pl.ds(256, 256)]
    kt, vt = r.eo.at[:, pl.ds(0, 512)], r.eo.at[:, pl.ds(512, 512)]
    mixed, mixed_t = r.hidden.at[:, pl.ds(0, 512)], r.hidden.at[:, pl.ds(512, 512)]
    ring_oa = Ring(ot_a, r.ringed.ota[0], r.ringed.ota[1], "x", where, at)
    ring_ob = Ring(ot_b, r.ringed.otb[0], r.ringed.otb[1], "y", where, at)
    ring_k = Ring(kt, r.ringed.kt[0], r.ringed.kt[1], "x", where, at)
    ring_v = Ring(vt, r.ringed.vt[0], r.ringed.vt[1], "y", where, at)
    ring_oa2 = Ring(r.ot_a2, r.ringed.ota2[0], r.ringed.ota2[1], "y", where, at)
    ring_ob2 = Ring(r.ot_b2, r.ringed.otb2[0], r.ringed.otb2[1], "x", where, at)
    ring_k2 = Ring(r.kt2, r.ringed.kt2[0], r.ringed.kt2[1], "y", where, at)
    ring_v2 = Ring(r.vt2, r.ringed.vt2[0], r.ringed.vt2[1], "x", where, at)
    mine = [r.qkv.at[:, pl.ds(half * 512, 512)] for half in range(HALVES)]
    peers = [r.qkv.at[:, pl.ds(1024 + half * 512, 512)] for half in range(HALVES)]
    from_peer = [r.qkv.at[:, pl.ds(2048 + half * 512, 512)] for half in range(HALVES)]
    ring_z = [Ring(mine[half], r.ring_z[half][0], r.ring_z[half][1], "z", where, at) for half in range(HALVES)]

    loop(0, 8, lambda b: attention_forward(b, r, mixed))
    mixed_t[...] = mixed[...].T

    def out_terms(i):
        to_x, to_y = (x + 2 - i + 4) % 4, (y + 2 - i + 4) % 4

        def tile(j):
            lane_a = pl.multiple_of((to_x * 4 + j) * 256, 256)
            term = dot(mixed_t[0:256, :], r.cot[:, pl.ds(lane_a, 256)])
            ot_a[pl.ds(lane_a, 256), :] = term.astype(jnp.bfloat16)
            lane_b = pl.multiple_of((j * 4 + to_y) * 256, 256)
            term = dot(mixed_t[256:512, :], r.cot[:, pl.ds(lane_b, 256)])
            ot_b[rows_of((to_y * 4 + j) * 256, 256), :] = term.astype(jnp.bfloat16)

        loop(0, 4, tile)

    loop(0, 1, out_terms)
    ring_oa.first()
    ring_ob.first()
    loop(1, 4, out_terms)
    ring_oa.second()
    ring_ob.second()
    loop(0, 8, lambda b: attention_backward(b, r))

    core_copies = [
        [
            send(
                peers[half].at[pl.ds(k * 256, 256), :],
                from_peer[half].at[pl.ds(k * 256, 256), :],
                r.s_core[half],
                k,
                peer,
            )
            for k in range(4)
        ]
        for half in range(HALVES)
    ]

    def enc_piece(half, piece_at, out, out_at):
        feats = slice(half * 512, half * 512 + 512)
        term = dot(r.dkv[piece_at], r.wkv[feats, :], ACROSS)
        out[rows_of(out_at, 256), :] = term.astype(jnp.bfloat16)

    def enc_half(half):
        def to_peer(k):
            enc_piece(half, k * 2 + (1 - core), peers[half], k * 256)
            for number in range(4):

                @pl.when(k == number)
                def _():
                    core_copies[half][number].start()

        loop(0, 4, to_peer)
        loop(0, 4, lambda k: enc_piece(half, k * 2 + core, mine[half], k * 256))

    def add_peer(half):
        for k in range(4):
            core_copies[half][k].wait_recv()
        add_rows(mine[half], 0, ((mine[half], 0), (from_peer[half], 0)), 1024, 64)

    def key_terms(part):
        lanes = pl.ds(pl.multiple_of(part * 128, 128), 128)
        term = dot(r.rows[:, :, lanes].reshape(2048, 128), r.dkv[...].reshape(2048, 1024), DOWN)
        low = term.astype(jnp.bfloat16)
        kt[rows_of(part * 128, 128), :] = low[:, 0:512]
        for side in range(2):
            to_x, to_y = (part * 2 + side) // 4, (part * 2 + side) % 4
            vt[rows_of(to_y * 256 + to_x * 64, 64), :] = low[side * 64 : side * 64 + 64, 512:1024]

    enc_half(0)
    add_peer(0)
    ring_z[0].first()
    ring_oa.third(64)
    ring_ob.third(64)
    loop(0, 4, key_terms)
    ring_z[0].third(64, True)
    loop(4, 8, key_terms)
    ring_k.first()
    ring_v.first()
    ring_k.second()
    ring_v.second()
    enc_half(1)
    add_peer(1)
    ring_z[1].first()

    back_gens = [over_gen(half, r.returned, r.s_bgen) for half in range(HALVES)]

    def start_back_gen(half):
        ring_z[half].last(r.piece[half], 0, 16)
        out_gens[half].drain()
        for j in range(32):
            r.outgoing[half][j] = r.piece[half][r.position[j]]
        back_gens[half].start()
        own = pl.ds(gen * 2, 2)
        r.returned[half][own] = r.outgoing[half][own]

    def back_enc(half):
        def copy(step):
            to = (enc + step) % 8
            return send(
                r.grads[half].at[to],
                r.home.at[:, own_rows, pl.ds(half * 512, 512)],
                r.s_benc[half],
                step - 1,
                (to, gen),
            )

        return Exchange(8, copy)

    back_encs = [back_enc(half) for half in range(HALVES)]

    def start_back_enc(half):
        back_gens[half].receive()
        for j in range(16):
            r.grads[half][j // 2, j % 2] = r.returned[half][r.column[j]]
        back_encs[half].start()
        r.home[:, own_rows, half * 512 : half * 512 + 512] = r.grads[half][enc]

    start_back_gen(0)
    ring_oa.last(r.ot_a2, 0, 64)
    ring_oa2.first()
    ring_oa2.second()
    ring_ob.last(r.ot_b2, 0, 64)
    ring_ob2.first()
    ring_ob2.second()
    ring_z[1].third(64, True)
    ring_k.third(64)
    ring_v.third(64)
    ring_oa2.third(64)
    ring_ob2.third(64)
    start_back_gen(1)
    start_back_enc(0)
    ring_k.last(r.kt2, 0, 64)
    ring_k2.first()
    ring_k2.second()
    ring_v.last(r.vt2, 0, 64)
    ring_v2.first()
    ring_v2.second()
    ring_oa2.last(r.wo_out, 0, 64)
    ring_ob2.last(r.wo_out, 256, 64)
    ring_k2.third(32)
    ring_v2.third(32)
    start_back_enc(1)
    ring_k2.last(r.wk_out, 0, 32)
    ring_v2.last(r.wv_out, 0, 32)
    for half in range(HALVES):
        back_encs[half].receive()
    r.enc_out[...] = r.home[...]

    rings_all = [ring_oa, ring_ob, ring_k, ring_v, ring_oa2, ring_ob2, ring_k2, ring_v2] + ring_z
    for ring in rings_all:
        ring.drain()
    for half in range(HALVES):
        for copy in core_copies[half] + rings[half] + crosses[half]:
            copy.wait_send()
        for exchange in (out_encs[half], back_gens[half], back_encs[half]):
            exchange.drain()


def whole(tables, nbr, enc_gain, gain, qkv, eo, hidden, cot, wq, wo, wk, wv):
    low = jnp.bfloat16
    vmem = lambda *shape: pltpu.VMEM(shape, low)
    sems = lambda *shape: pltpu.SemaphoreType.DMA(shape)
    both = lambda make, *shape: [make(*shape) for _ in range(HALVES)]
    ring = lambda count, width: [vmem(count // 4 * 3, width), sems(2, 6)]
    anywhere = pl.BlockSpec(memory_space=pl.ANY)
    scalars = pl.BlockSpec(memory_space=pltpu.SMEM)
    local = pl.BlockSpec(memory_space=pltpu.VMEM)
    send_table, position_table, receive_table, column_table = tables
    small = dict(send=send_table, position=position_table, receive=receive_table, column=column_table)
    near = dict(nbr=nbr.reshape(256, 1024), enc_gain=enc_gain.reshape(1, -1), gain=gain.reshape(1, -1))
    big = dict(
        qkv_hbm=qkv, eo_hbm=eo, hidden_hbm=hidden, wq_hbm=wq, cot_hbm=cot, wo_hbm=wo, wk_hbm=wk, wv_hbm=wv
    )
    outputs = dict(
        enc_out=jax.ShapeDtypeStruct((2, 128, 1024), low),
        wo_out=jax.ShapeDtypeStruct((512, 256), low),
        wk_out=jax.ShapeDtypeStruct((64, 512), low),
        wv_out=jax.ShapeDtypeStruct((64, 512), low),
    )
    scratch = dict(
        qkv=vmem(1024, 3072),
        eo=vmem(1024, 1024),
        hidden=vmem(512, 4096),
        wq=vmem(4096, 512),
        cot=vmem(512, 4096),
        wo=vmem(512, 4096),
        wkv=vmem(1024, 1024),
        enc_normed=vmem(256, 1024),
        projected=vmem(256, 3072),
        encoded=vmem(2, 128, 1024),
        q_pairs=vmem(2048, 256),
        dm_pairs=vmem(2048, 256),
        kv=vmem(8, 256, 1024),
        dkv=vmem(8, 256, 1024),
        rows=vmem(8, 256, 1024),
        ot_a2=vmem(1024, 256),
        ot_b2=vmem(1024, 256),
        kt2=vmem(256, 512),
        vt2=vmem(256, 512),
        home=vmem(2, 128, 1024),
        ringed=dict(
            ota=ring(4096, 256),
            otb=ring(4096, 256),
            kt=ring(1024, 512),
            vt=ring(1024, 512),
            ota2=ring(1024, 256),
            otb2=ring(1024, 256),
            kt2=ring(256, 512),
            vt2=ring(256, 512),
        ),
        ring_z=both(ring, 1024, 512),
        columns=both(vmem, 16, 16, 512),
        outgoing=both(vmem, 32, 16, 512),
        incoming=both(vmem, 32, 16, 512),
        returned=both(vmem, 32, 16, 512),
        piece=both(vmem, 16, 16, 512),
        grads=both(vmem, 8, 2, 16, 512),
        s_oenc=both(sems, 2, 7),
        s_benc=both(sems, 2, 7),
        s_ogen=both(sems, 2, 15),
        s_bgen=both(sems, 2, 15),
        s_ring=both(sems, 2, 6),
        s_cross=both(sems, 2, 5),
        s_core=both(sems, 2, 4),
        load_sems=sems(10),
    )
    operands = small | near | big
    leaves, _ = jax.tree.flatten(scratch)
    tree = jax.tree.structure((operands, outputs, scratch))
    by_name = lambda part: [part[name] for name in sorted(part)]
    place = dict.fromkeys(small, scalars) | dict.fromkeys(near, local) | dict.fromkeys(big, anywhere)
    return pl.pallas_call(
        functools.partial(whole_kernel, tree),
        name="retro_whole",
        out_shape=tuple(by_name(outputs)),
        in_specs=by_name(place),
        out_specs=(local,) * len(outputs),
        scratch_shapes=leaves,
        compiler_params=pltpu.CompilerParams(
            collective_id=1, has_side_effects=True, vmem_limit_bytes=61 * 1024 * 1024
        ),
    )(*by_name(operands))


def widen_kernel(*refs):
    sources, targets, near, sems = refs[:4], refs[4:8], refs[8:12], refs[12]
    copies = [
        pltpu.make_async_copy(src, dst, sems.at[number]) for number, (src, dst) in enumerate(zip(sources, near))
    ]
    for copy in copies:
        copy.start()
    for copy, src, dst in zip(copies, near, targets):
        copy.wait()
        dst[...] = src[...].astype(jnp.float32)


def widen(values):
    return pl.pallas_call(
        widen_kernel,
        name="widen",
        out_shape=tuple(jax.ShapeDtypeStruct(value.shape, jnp.float32) for value in values),
        in_specs=[pl.BlockSpec(memory_space=pl.ANY)] * 4,
        out_specs=(pl.BlockSpec(memory_space=pltpu.VMEM),) * 4,
        scratch_shapes=[pltpu.VMEM(value.shape, value.dtype) for value in values] + [pltpu.SemaphoreType.DMA((4,))],
        compiler_params=pltpu.CompilerParams(vmem_limit_bytes=60 * 1024 * 1024),
    )(*values)


def routing(nbr_index, row_index, gen_count, per_device, row_size, capacity):
    entries = nbr_index.reshape(gen_count, row_size)
    source = entries // per_device % gen_count
    column = entries // (per_device * gen_count) * per_device + entries % per_device
    places = jnp.arange(row_size, dtype=jnp.int32)
    same = (source[:, :, None] == source[:, None, :]) & (places[None, None, :] < places[None, :, None])
    rank = jnp.sum(same.astype(jnp.int32), axis=2)
    rows = jnp.arange(gen_count, dtype=jnp.int32)
    send_slot = (rows[:, None] * capacity + rank).reshape(-1)
    mine = (source == row_index).reshape(-1)
    flat_column = column.reshape(-1)
    buffers = jnp.arange(gen_count * capacity, dtype=jnp.int32)
    send_match = (send_slot[:, None] == buffers[None, :]) & mine[:, None]
    send_column = jnp.sum(jnp.where(send_match, flat_column[:, None], 0), axis=0)
    column_match = (flat_column[:, None] == places[None, :]) & mine[:, None]
    column_position = jnp.sum(jnp.where(column_match, send_slot[:, None], 0), axis=0)
    own = (rows == row_index)[:, None]
    receive_position = jnp.sum(jnp.where(own, source * capacity + rank, 0), axis=0)
    receive_match = receive_position[:, None] == buffers[None, :]
    position_slot = jnp.sum(jnp.where(receive_match, places[:, None], 0), axis=0)
    return (send_column, position_slot, receive_position, column_position)


def local(
    hidden_states,
    grad_out,
    nbr_embed,
    nbr_index,
    gain,
    w_query,
    w_out,
    w_key,
    w_value,
    enc_gain,
    enc_qkv,
    enc_out,
):
    gen_count = lax.axis_size("gen")
    per_device = nbr_embed.shape[0]
    row_size = per_device * lax.axis_size("enc")
    capacity = max(2, 2 * row_size // gen_count)
    tables = routing(nbr_index, lax.axis_index("gen"), gen_count, per_device, row_size, capacity)
    grad_encoded, grad_key, grad_out_proj, grad_value = (
        whole(
            tables,
            nbr_embed,
            enc_gain,
            gain,
            enc_qkv,
            enc_out,
            hidden_states,
            grad_out,
            w_query,
            w_out,
            w_key,
            w_value,
        )
    )
    return widen((grad_encoded, grad_out_proj, grad_key, grad_value))


def solution(mesh):
    return jax.shard_map(
        local,
        mesh=mesh,
        in_specs=(
            P("gen", None),
            P("gen", None),
            P(("enc", "gen"), None, None),
            P(),
            P(),
            P(None, "enc"),
            P("enc", None),
            P(None, "enc"),
            P(None, "enc"),
            P(),
            P(),
            P(),
        ),
        out_specs=(
            P(("enc", "gen"), None, None),
            P("enc", "gen"),
            P("gen", "enc"),
            P("gen", "enc"),
        ),
        check_vma=False,
    )
```

```python
import functools
import types

import jax
import jax.numpy as jnp
from jax import lax
from jax.experimental import pallas as pl
from jax.experimental.pallas import tpu as pltpu
from jax.sharding import PartitionSpec as P

EH = 8
CH = 64
SOFTCAP = 5.0
EPSILON = 1e-06
MESH = pl.DeviceIdType.MESH


def neighbours():
    enc, gen = lax.axis_index("enc"), lax.axis_index("gen")
    z, core, x, y = enc // 2, enc % 2, gen // 4, gen % 4

    def at(axis, step):
        if axis == "x":
            return (enc, (x + step) % 4 * 4 + y)
        if axis == "y":
            return (enc, x * 4 + (y + step) % 4)
        if axis == "z":
            return ((z + step) % 4 * 2 + core, gen)
        return (z * 2 + (1 - core), gen)

    return enc, gen, {"x": x, "y": y, "z": z, "core": core}, at


def send(src, dst, sems, number, device):
    return pltpu.make_async_remote_copy(
        src_ref=src,
        dst_ref=dst,
        send_sem=sems.at[0, number],
        recv_sem=sems.at[1, number],
        device_id=device,
        device_id_type=MESH,
    )


def add_rows(out, out_at, terms, rows, step):
    def body(i, carry):
        total = None
        for ref, at in terms:
            value = ref[pl.ds(pl.multiple_of(at + i * step, step), step), :].astype(jnp.float32)
            total = value if total is None else total + value
        if len(out.shape) == 3:
            out[out_at + i] = total.astype(out.dtype)
        else:
            out[pl.ds(pl.multiple_of(out_at + i * step, step), step), :] = total.astype(out.dtype)
        return carry

    lax.fori_loop(0, rows // step, body, 0)


class Ring:
    def __init__(self, src, buf, sems, axis, where, at):
        self.src, self.buf = src, buf
        self.rows = src.shape[0] // 4
        self.half = self.rows // 2
        self.me = where[axis]
        half = self.half
        self.plus, self.minus = (self.me + 1) % 4, (self.me + 3) % 4
        across = (self.me + 2) % 4
        pieces = (
            (across, 0, 1),
            (self.plus, 1, 1),
            (self.plus, 0, 1),
            (across, 1, 3),
            (self.minus, 0, 3),
            (self.minus, 1, 3),
        )
        self.copies = []
        for number, (chunk, side, step) in enumerate(pieces):
            start = pl.multiple_of(chunk * self.rows + side * half, half)
            self.copies.append(
                send(
                    src.at[pl.ds(start, half), :],
                    buf.at[pl.ds(number * half, half), :],
                    sems,
                    number,
                    at(axis, step),
                )
            )

    def first(self):
        self.copies[0].start()
        self.copies[3].start()

    def second(self):
        self.copies[1].start()
        self.copies[4].start()

    def third(self, step, with_second=False):
        half = self.half
        self.copies[0].wait_recv()
        if with_second:
            self.copies[3].wait_recv()
            self.second()
        start = self.plus * self.rows
        add_rows(self.src, start, ((self.src, start), (self.buf, 0)), half, step)
        self.copies[2].start()
        if not with_second:
            self.copies[3].wait_recv()
        start = self.minus * self.rows + half
        add_rows(self.src, start, ((self.src, start), (self.buf, 3 * half)), half, step)
        self.copies[5].start()

    def last(self, out, out_at, step):
        half = self.half
        for number in (1, 2, 4, 5):
            self.copies[number].wait_recv()
        start = self.me * self.rows
        add_rows(out, out_at, ((self.src, start), (self.buf, 2 * half), (self.buf, 4 * half)), half, step)
        add_rows(
            out, out_at + (half // step if len(out.shape) == 3 else half), ((self.src, start + half), (self.buf, half), (self.buf, 5 * half)), half, step
        )

    def drain(self):
        for copy in self.copies:
            copy.wait_send()


HALVES = 2
DOWN = (((0,), (0,)), ((), ()))
ACROSS = (((1,), (1,)), ((), ()))


def dot(a, b, dims=(((1,), (0,)), ((), ()))):
    return lax.dot_general(a, b, dims, preferred_element_type=jnp.float32)


def loop(low, high, body):
    def step(i, carry):
        body(i)
        return carry

    lax.fori_loop(low, high, step, 0)


def rows_of(start, size):
    return pl.ds(pl.multiple_of(start, size), size)


def normalise(values, gain, out):
    def body(i):
        at = rows_of(i * 16, 16)
        wide = values[at, :].astype(jnp.float32)
        factor = lax.rsqrt(jnp.mean(wide * wide, axis=-1, keepdims=True) + EPSILON)
        out[at, :] = (wide * factor * gain[...]).astype(jnp.bfloat16)

    loop(0, values.shape[0] // 16, body)


def softcapped(q, k):
    scale = q.shape[-1] ** (-0.5)
    slope = jnp.tanh(dot(q, k, ACROSS) * (scale / SOFTCAP))
    expo = jnp.exp(SOFTCAP * slope)
    return slope, expo / jnp.sum(expo, axis=-1, keepdims=True)


def encoder_attention(i, projected, attended):
    at = rows_of(i * 128, 128)
    for h in range(EH):
        q, k, v = (projected[at, part * 1024 + h * 128 : part * 1024 + h * 128 + 128] for part in range(3))
        _, probs = softcapped(q, k)
        attended[at, h * 128 : h * 128 + 128] = dot(probs.astype(jnp.bfloat16), v).astype(jnp.bfloat16)


def pair_refs(b, p, r):
    keys, rows = rows_of(b * 32, 32), rows_of((b * 2 + p) * 128, 128)
    k = r.kv[:, keys, p * 256 : p * 256 + 256].reshape(256, 256)
    v = r.kv[:, keys, 512 + p * 256 : 512 + p * 256 + 256].reshape(256, 256)
    return keys, rows, k, v


def pair_probs(k, q_pair):
    slope = jnp.tanh(dot(k, q_pair, ACROSS) * (128 ** (-0.5) / SOFTCAP))
    expo = jnp.exp(SOFTCAP * slope)
    return slope, expo * (1.0 / jnp.sum(expo, axis=0, keepdims=True))


def attention_forward(b, r, mixed):
    tokens = rows_of(b * CH, CH)
    for p in range(2):
        keys, rows, k, v = pair_refs(b, p, r)
        slope, probs = pair_probs(k, r.q_pairs[rows, :])
        low = probs.astype(jnp.bfloat16)
        lanes = pl.ds(pl.multiple_of((b * 2 + p) * 128, 128), 128)
        r.wo[0:256, lanes] = low
        r.wo[256:512, lanes] = ((1.0 - slope * slope) * 128 ** (-0.5)).astype(jnp.bfloat16)
        both = dot(low, v, DOWN).astype(jnp.bfloat16)
        mixed[tokens, p * 256 : p * 256 + 128] = both[0:64, 0:128]
        mixed[tokens, p * 256 + 128 : p * 256 + 256] = both[64:128, 128:256]


def attention_backward(b, r):
    for p in range(2):
        keys, rows, k, v = pair_refs(b, p, r)
        q_pair, dm_pair = r.q_pairs[rows, :], r.dm_pairs[rows, :]
        lanes = pl.ds(pl.multiple_of((b * 2 + p) * 128, 128), 128)
        low, slope = r.wo[0:256, lanes], r.wo[256:512, lanes].astype(jnp.float32)
        probs = low.astype(jnp.float32)
        d_probs = dot(v, dm_pair, ACROSS)
        d_capped = probs * (d_probs - jnp.sum(probs * d_probs, axis=0, keepdims=True))
        d_raw = (d_capped * slope).astype(jnp.bfloat16)
        d_keys = dot(d_raw, q_pair).astype(jnp.bfloat16)
        d_values = dot(low, dm_pair).astype(jnp.bfloat16)
        r.dkv[:, keys, p * 256 : p * 256 + 256] = d_keys.reshape(8, 32, 256)
        r.dkv[:, keys, 512 + p * 256 : 512 + p * 256 + 256] = d_values.reshape(8, 32, 256)


class Exchange:
    def __init__(self, count, copy):
        self.count, self.copy = count, copy

    def start(self):
        loop(1, self.count, lambda step: self.copy(step).start())

    def receive(self):
        loop(1, self.count, lambda step: self.copy(step).wait_recv())

    def drain(self):
        loop(1, self.count, lambda step: self.copy(step).wait_send())


def whole_kernel(tree, *refs):
    r = jax.tree.unflatten(tree, refs)
    r = types.SimpleNamespace(**{name: ref for part in r for name, ref in part.items()})
    r.ringed = types.SimpleNamespace(**r.ringed)

    def load(number):
        src = (r.eo_hbm, r.hidden_hbm, r.wq_hbm, r.cot_hbm, r.wo_hbm, r.wk_hbm, r.wv_hbm)[number]
        w_pair = [r.wkv.at[:, pl.ds(at, 512)] for at in (0, 512)]
        dst = (r.eo, r.hidden, r.wq, r.cot, r.wo, *w_pair)[number]
        return pltpu.make_async_copy(src, dst, r.load_sems.at[number])

    def load_third(third):
        lanes = pl.ds(third * 1024, 1024)
        return pltpu.make_async_copy(r.qkv_hbm.at[:, lanes], r.qkv.at[:, lanes], r.load_sems.at[7 + third])

    for third in range(3):
        load_third(third).start()
    load(0).start()
    enc, gen, where, at = neighbours()
    x, y, z, core = where["x"], where["y"], where["z"], where["core"]
    barrier = pltpu.get_barrier_semaphore()
    loop(1, 16, lambda step: pl.semaphore_signal(barrier, inc=1, device_id=(enc, (gen + step) % 16), device_id_type=MESH))
    loop(1, 8, lambda step: pl.semaphore_signal(barrier, inc=1, device_id=((enc + step) % 8, gen), device_id_type=MESH))

    normalise(r.nbr, r.enc_gain, r.enc_normed)
    for third in range(3):
        load_third(third).wait()
        lanes = slice(third * 1024, third * 1024 + 1024)
        r.projected[:, lanes] = dot(r.enc_normed[...], r.qkv[:, lanes]).astype(jnp.bfloat16)
    for number in range(1, 7):
        load(number).start()
    loop(0, 2, lambda i: encoder_attention(i, r.projected, r.enc_normed))
    load(0).wait()

    def finish(half):
        lanes = slice(half * 512, half * 512 + 512)
        update = dot(r.enc_normed[...], r.eo[:, lanes])
        low = (r.nbr[:, lanes].astype(jnp.float32) + update).astype(jnp.bfloat16)
        r.encoded[:, :, lanes] = low.reshape(2, 128, 512)

    finish(0)
    pl.semaphore_wait(barrier, 22)

    own_rows = rows_of(enc * 16, 16)

    def out_enc(half):
        lanes = pl.ds(half * 512, 512)

        def copy(step):
            peer = (enc + step) % 8
            return send(
                r.encoded.at[:, rows_of(peer * 16, 16), lanes],
                r.columns[half].at[pl.ds(enc * 2, 2)],
                r.s_oenc[half],
                step - 1,
                (peer, gen),
            )

        return Exchange(8, copy)

    def over_gen(half, target, sems):
        def copy(step):
            peer = (gen + step) % 16
            return send(
                r.outgoing[half].at[pl.ds(peer * 2, 2)],
                target[half].at[pl.ds(gen * 2, 2)],
                sems[half],
                step - 1,
                (enc, peer),
            )

        return Exchange(16, copy)

    out_encs = [out_enc(half) for half in range(HALVES)]
    out_gens = [over_gen(half, r.incoming, r.s_ogen) for half in range(HALVES)]
    out_encs[0].start()
    finish(1)
    for half in range(HALVES):
        r.columns[half][pl.ds(enc * 2, 2)] = r.encoded[:, own_rows, half * 512 : half * 512 + 512]

    def pick_out_gen(half):
        for j in range(32):
            r.outgoing[half][j] = r.columns[half][r.send[j]]
        own = pl.ds(gen * 2, 2)
        r.incoming[half][own] = r.outgoing[half][own]

    def store_pairs(out, i, low):
        for block in range(4):
            for head in range(4):
                start = i * 1024 + block * 256 + head // 2 * 128 + head % 2 * 64
                out[rows_of(start, 64), head % 2 * 128 : head % 2 * 128 + 128] = low[
                    block * 64 : block * 64 + 64, head * 128 : head * 128 + 128
                ]

    def query_tile(i):
        low = dot(r.hidden[rows_of(i * 256, 256), :], r.wq[...]).astype(jnp.bfloat16)
        store_pairs(r.q_pairs, i, low)

    def cotangent_tile(i):
        low = dot(r.cot[rows_of(i * 256, 256), :], r.wo[...], ACROSS).astype(jnp.bfloat16)
        store_pairs(r.dm_pairs, i, low)

    r.q_pairs[...] = jnp.zeros_like(r.q_pairs)
    r.dm_pairs[...] = jnp.zeros_like(r.dm_pairs)
    out_encs[0].receive()
    out_encs[1].start()
    pick_out_gen(0)
    out_gens[0].start()
    load(1).wait()
    normalise(r.hidden, r.gain, r.hidden)
    load(2).wait()
    loop(0, 2, query_tile)
    out_encs[1].receive()
    pick_out_gen(1)
    load(3).wait()
    load(4).wait()

    minus, plus, across = (z + 3) % 4 * 2 + core, (z + 1) % 4 * 2 + core, (z + 2) % 4 * 2 + core
    up, down, peer = at("z", 1), at("z", 3), at("core", 1)
    rings, crosses = [], []
    for half in range(HALVES):
        rows = r.rows.at[:, :, pl.ds(half * 512, 512)]
        first, second = pl.ds(0, 128), pl.ds(128, 128)

        def share(ref, sems, number, device):
            return send(ref, ref, sems, number, device)

        rings.append(
            [
                share(rows.at[enc, first], r.s_ring[half], 0, up),
                share(rows.at[enc, second], r.s_ring[half], 1, down),
                share(rows.at[minus, first], r.s_ring[half], 2, up),
                share(rows.at[plus, second], r.s_ring[half], 3, down),
                share(rows.at[enc, second], r.s_ring[half], 4, up),
                share(rows.at[enc, first], r.s_ring[half], 5, down),
            ]
        )
        crosses.append(
            [
                share(rows.at[enc], r.s_cross[half], 0, peer),
                share(rows.at[minus], r.s_cross[half], 1, peer),
                share(rows.at[plus], r.s_cross[half], 2, peer),
                share(rows.at[across, first], r.s_cross[half], 3, peer),
                share(rows.at[across, second], r.s_cross[half], 4, peer),
            ]
        )

    def take_slots(half):
        out_gens[half].receive()
        for j in range(16):
            r.rows[enc, j * 16 : j * 16 + 16, half * 512 : half * 512 + 512] = r.incoming[half][r.receive[j]]

    def gather_own(half):
        rings[half][0].start()
        rings[half][1].start()
        rings[half][4].start()
        rings[half][5].start()
        crosses[half][0].start()

    def gather_next(half):
        rings[half][0].wait_recv()
        rings[half][2].start()
        rings[half][1].wait_recv()
        rings[half][3].start()
        rings[half][4].wait_recv()
        crosses[half][1].start()
        rings[half][5].wait_recv()
        crosses[half][2].start()

    def gather_last(half):
        rings[half][2].wait_recv()
        crosses[half][3].start()
        rings[half][3].wait_recv()
        crosses[half][4].start()

    def of_peer(piece):
        return piece + 1 - 2 * core

    def project(piece):
        r.kv[piece] = dot(r.rows[piece], r.wkv[...]).astype(jnp.bfloat16)

    def project_some(pieces):
        def body(i):
            piece = pieces[0]
            for number in range(1, len(pieces)):
                piece = jnp.where(i == number, pieces[number], piece)
            project(piece)

        loop(0, len(pieces), body)

    load(5).wait()
    load(6).wait()
    out_gens[0].drain()
    out_gens[1].start()
    take_slots(0)
    gather_own(0)
    loop(0, 2, cotangent_tile)
    gather_next(0)
    take_slots(1)
    gather_own(1)
    gather_last(0)
    crosses[1][0].wait_recv()
    crosses[0][0].wait_recv()
    project_some((enc, of_peer(enc)))
    gather_next(1)
    for number in (1, 2):
        crosses[0][number].wait_recv()
    project_some((minus, plus))
    for number in (1, 2):
        crosses[1][number].wait_recv()
    project_some((of_peer(minus), of_peer(plus)))
    gather_last(1)
    project_some((across,))
    for number in (3, 4):
        crosses[0][number].wait_recv()
        crosses[1][number].wait_recv()
    project_some((of_peer(across),))

    ot_a, ot_b = r.wq.at[:, pl.ds(0, 256)], r.wq.at[:, pl.ds(256, 256)]
    kt, vt = r.eo.at[:, pl.ds(0, 512)], r.eo.at[:, pl.ds(512, 512)]
    mixed, mixed_t = r.hidden.at[:, pl.ds(0, 512)], r.hidden.at[:, pl.ds(512, 512)]
    ring_oa = Ring(ot_a, r.ringed.ota[0], r.ringed.ota[1], "x", where, at)
    ring_ob = Ring(ot_b, r.ringed.otb[0], r.ringed.otb[1], "y", where, at)
    ring_k = Ring(kt, r.ringed.kt[0], r.ringed.kt[1], "x", where, at)
    ring_v = Ring(vt, r.ringed.vt[0], r.ringed.vt[1], "y", where, at)
    ring_oa2 = Ring(r.ot_a2, r.ringed.ota2[0], r.ringed.ota2[1], "y", where, at)
    ring_ob2 = Ring(r.ot_b2, r.ringed.otb2[0], r.ringed.otb2[1], "x", where, at)
    ring_k2 = Ring(r.kt2, r.ringed.kt2[0], r.ringed.kt2[1], "y", where, at)
    ring_v2 = Ring(r.vt2, r.ringed.vt2[0], r.ringed.vt2[1], "x", where, at)
    mine = [r.qkv.at[:, pl.ds(half * 512, 512)] for half in range(HALVES)]
    peers = [r.qkv.at[:, pl.ds(1024 + half * 512, 512)] for half in range(HALVES)]
    from_peer = [r.qkv.at[:, pl.ds(2048 + half * 512, 512)] for half in range(HALVES)]
    ring_z = [Ring(mine[half], r.ring_z[half][0], r.ring_z[half][1], "z", where, at) for half in range(HALVES)]

    def forward_two(i):
        attention_forward(i * 2, r, mixed)
        attention_forward(i * 2 + 1, r, mixed)

    def backward_two(i):
        attention_backward(i * 2, r)
        attention_backward(i * 2 + 1, r)

    loop(0, 4, forward_two)
    mixed_t[...] = mixed[...].T

    def out_terms(i):
        to_x, to_y = (x + 2 - i + 4) % 4, (y + 2 - i + 4) % 4

        def tile(j):
            lane_a = pl.multiple_of((to_x * 4 + j) * 256, 256)
            term = dot(mixed_t[0:256, :], r.cot[:, pl.ds(lane_a, 256)])
            ot_a[pl.ds(lane_a, 256), :] = term.astype(jnp.bfloat16)
            lane_b = pl.multiple_of((j * 4 + to_y) * 256, 256)
            term = dot(mixed_t[256:512, :], r.cot[:, pl.ds(lane_b, 256)])
            ot_b[rows_of((to_y * 4 + j) * 256, 256), :] = term.astype(jnp.bfloat16)

        loop(0, 4, tile)

    loop(0, 1, out_terms)
    ring_oa.first()
    ring_ob.first()
    loop(1, 4, out_terms)
    ring_oa.second()
    ring_ob.second()
    loop(0, 4, backward_two)

    core_copies = [
        [
            send(
                peers[half].at[pl.ds(k * 256, 256), :],
                from_peer[half].at[pl.ds(k * 256, 256), :],
                r.s_core[half],
                k,
                peer,
            )
            for k in range(4)
        ]
        for half in range(HALVES)
    ]

    def enc_piece(half, piece_at, out, out_at):
        feats = slice(half * 512, half * 512 + 512)
        term = dot(r.dkv[piece_at], r.wkv[feats, :], ACROSS)
        out[rows_of(out_at, 256), :] = term.astype(jnp.bfloat16)

    def enc_half(half):
        def to_peer(k):
            enc_piece(half, k * 2 + (1 - core), peers[half], k * 256)
            for number in range(4):

                @pl.when(k == number)
                def _():
                    core_copies[half][number].start()

        loop(0, 4, to_peer)
        loop(0, 4, lambda k: enc_piece(half, k * 2 + core, mine[half], k * 256))

    def add_peer(half):
        for k in range(4):
            core_copies[half][k].wait_recv()
        add_rows(mine[half], 0, ((mine[half], 0), (from_peer[half], 0)), 1024, 64)

    def key_terms(part):
        lanes = pl.ds(pl.multiple_of(part * 128, 128), 128)
        term = dot(r.rows[:, :, lanes].reshape(2048, 128), r.dkv[...].reshape(2048, 1024), DOWN)
        low = term.astype(jnp.bfloat16)
        kt[rows_of(part * 128, 128), :] = low[:, 0:512]
        for side in range(2):
            to_x, to_y = (part * 2 + side) // 4, (part * 2 + side) % 4
            vt[rows_of(to_y * 256 + to_x * 64, 64), :] = low[side * 64 : side * 64 + 64, 512:1024]

    enc_half(0)
    add_peer(0)
    ring_z[0].first()
    ring_oa.third(64)
    ring_ob.third(64)
    loop(0, 4, key_terms)
    ring_z[0].third(64, True)
    loop(4, 8, key_terms)
    ring_k.first()
    ring_v.first()
    ring_k.second()
    ring_v.second()
    enc_half(1)
    add_peer(1)
    ring_z[1].first()

    back_gens = [over_gen(half, r.returned, r.s_bgen) for half in range(HALVES)]

    def start_back_gen(half):
        ring_z[half].last(r.piece[half], 0, 16)
        if half == 1:
            out_gens[half].drain()
        for j in range(32):
            r.outgoing[half][j] = r.piece[half][r.position[j]]
        back_gens[half].start()
        own = pl.ds(gen * 2, 2)
        r.returned[half][own] = r.outgoing[half][own]

    def back_enc(half):
        def copy(step):
            to = (enc + step) % 8
            return send(
                r.grads[half].at[to],
                r.home.at[:, own_rows, pl.ds(half * 512, 512)],
                r.s_benc[half],
                step - 1,
                (to, gen),
            )

        return Exchange(8, copy)

    back_encs = [back_enc(half) for half in range(HALVES)]

    def start_back_enc(half):
        back_gens[half].receive()
        for j in range(16):
            r.grads[half][j // 2, j % 2] = r.returned[half][r.column[j]]
        back_encs[half].start()
        r.home[:, own_rows, half * 512 : half * 512 + 512] = r.grads[half][enc]

    start_back_gen(0)
    ring_oa.last(r.ot_a2, 0, 64)
    ring_oa2.first()
    ring_oa2.second()
    ring_ob.last(r.ot_b2, 0, 64)
    ring_ob2.first()
    ring_ob2.second()
    ring_z[1].third(64, True)
    ring_k.third(64)
    ring_v.third(64)
    ring_oa2.third(64)
    ring_ob2.third(64)
    start_back_gen(1)
    start_back_enc(0)
    ring_k.last(r.kt2, 0, 64)
    ring_k2.first()
    ring_k2.second()
    ring_v.last(r.vt2, 0, 64)
    ring_v2.first()
    ring_v2.second()
    ring_oa2.last(r.wo_out, 0, 64)
    ring_ob2.last(r.wo_out, 256, 64)
    ring_k2.third(32)
    ring_v2.third(32)
    start_back_enc(1)
    ring_k2.last(r.wk_out, 0, 32)
    ring_v2.last(r.wv_out, 0, 32)
    for half in range(HALVES):
        back_encs[half].receive()
    r.enc_out[...] = r.home[...]

    rings_all = [ring_oa, ring_ob, ring_k, ring_v, ring_oa2, ring_ob2, ring_k2, ring_v2] + ring_z
    for ring in rings_all:
        ring.drain()
    for half in range(HALVES):
        for copy in core_copies[half] + rings[half] + crosses[half]:
            copy.wait_send()
        for exchange in (out_encs[half], back_gens[half], back_encs[half]):
            exchange.drain()


def whole(tables, nbr, enc_gain, gain, qkv, eo, hidden, cot, wq, wo, wk, wv):
    low = jnp.bfloat16
    vmem = lambda *shape: pltpu.VMEM(shape, low)
    sems = lambda *shape: pltpu.SemaphoreType.DMA(shape)
    both = lambda make, *shape: [make(*shape) for _ in range(HALVES)]
    ring = lambda count, width: [vmem(count // 4 * 3, width), sems(2, 6)]
    anywhere = pl.BlockSpec(memory_space=pl.ANY)
    scalars = pl.BlockSpec(memory_space=pltpu.SMEM)
    local = pl.BlockSpec(memory_space=pltpu.VMEM)
    send_table, position_table, receive_table, column_table = tables
    small = dict(send=send_table, position=position_table, receive=receive_table, column=column_table)
    near = dict(nbr=nbr.reshape(256, 1024), enc_gain=enc_gain.reshape(1, -1), gain=gain.reshape(1, -1))
    big = dict(
        qkv_hbm=qkv, eo_hbm=eo, hidden_hbm=hidden, wq_hbm=wq, cot_hbm=cot, wo_hbm=wo, wk_hbm=wk, wv_hbm=wv
    )
    outputs = dict(
        enc_out=jax.ShapeDtypeStruct((2, 128, 1024), low),
        wo_out=jax.ShapeDtypeStruct((512, 256), low),
        wk_out=jax.ShapeDtypeStruct((64, 512), low),
        wv_out=jax.ShapeDtypeStruct((64, 512), low),
    )
    scratch = dict(
        qkv=vmem(1024, 3072),
        eo=vmem(1024, 1024),
        hidden=vmem(512, 4096),
        wq=vmem(4096, 512),
        cot=vmem(512, 4096),
        wo=vmem(512, 4096),
        wkv=vmem(1024, 1024),
        enc_normed=vmem(256, 1024),
        projected=vmem(256, 3072),
        encoded=vmem(2, 128, 1024),
        q_pairs=vmem(2048, 256),
        dm_pairs=vmem(2048, 256),
        kv=vmem(8, 256, 1024),
        dkv=vmem(8, 256, 1024),
        rows=vmem(8, 256, 1024),
        ot_a2=vmem(1024, 256),
        ot_b2=vmem(1024, 256),
        kt2=vmem(256, 512),
        vt2=vmem(256, 512),
        home=vmem(2, 128, 1024),
        ringed=dict(
            ota=ring(4096, 256),
            otb=ring(4096, 256),
            kt=ring(1024, 512),
            vt=ring(1024, 512),
            ota2=ring(1024, 256),
            otb2=ring(1024, 256),
            kt2=ring(256, 512),
            vt2=ring(256, 512),
        ),
        ring_z=both(ring, 1024, 512),
        columns=both(vmem, 16, 16, 512),
        outgoing=both(vmem, 32, 16, 512),
        incoming=both(vmem, 32, 16, 512),
        returned=both(vmem, 32, 16, 512),
        piece=both(vmem, 16, 16, 512),
        grads=both(vmem, 8, 2, 16, 512),
        s_oenc=both(sems, 2, 7),
        s_benc=both(sems, 2, 7),
        s_ogen=both(sems, 2, 15),
        s_bgen=both(sems, 2, 15),
        s_ring=both(sems, 2, 6),
        s_cross=both(sems, 2, 5),
        s_core=both(sems, 2, 4),
        load_sems=sems(10),
    )
    operands = small | near | big
    leaves, _ = jax.tree.flatten(scratch)
    tree = jax.tree.structure((operands, outputs, scratch))
    by_name = lambda part: [part[name] for name in sorted(part)]
    place = dict.fromkeys(small, scalars) | dict.fromkeys(near, local) | dict.fromkeys(big, anywhere)
    return pl.pallas_call(
        functools.partial(whole_kernel, tree),
        name="retro_whole",
        out_shape=tuple(by_name(outputs)),
        in_specs=by_name(place),
        out_specs=(local,) * len(outputs),
        scratch_shapes=leaves,
        compiler_params=pltpu.CompilerParams(
            collective_id=1, has_side_effects=True, vmem_limit_bytes=61 * 1024 * 1024
        ),
    )(*by_name(operands))


def widen_kernel(*refs):
    sources, targets, near, sems = refs[:4], refs[4:8], refs[8:12], refs[12]
    copies = [
        pltpu.make_async_copy(src, dst, sems.at[number]) for number, (src, dst) in enumerate(zip(sources, near))
    ]
    for copy in copies:
        copy.start()
    for copy, src, dst in zip(copies, near, targets):
        copy.wait()
        dst[...] = src[...].astype(jnp.float32)


def widen(values):
    return pl.pallas_call(
        widen_kernel,
        name="widen",
        out_shape=tuple(jax.ShapeDtypeStruct(value.shape, jnp.float32) for value in values),
        in_specs=[pl.BlockSpec(memory_space=pl.ANY)] * 4,
        out_specs=(pl.BlockSpec(memory_space=pltpu.VMEM),) * 4,
        scratch_shapes=[pltpu.VMEM(value.shape, value.dtype) for value in values] + [pltpu.SemaphoreType.DMA((4,))],
        compiler_params=pltpu.CompilerParams(vmem_limit_bytes=60 * 1024 * 1024),
    )(*values)


def routing(nbr_index, row_index, gen_count, per_device, row_size, capacity):
    entries = nbr_index.reshape(gen_count, row_size)
    source = entries // per_device % gen_count
    column = entries // (per_device * gen_count) * per_device + entries % per_device
    places = jnp.arange(row_size, dtype=jnp.int32)
    same = (source[:, :, None] == source[:, None, :]) & (places[None, None, :] < places[None, :, None])
    rank = jnp.sum(same.astype(jnp.int32), axis=2)
    rows = jnp.arange(gen_count, dtype=jnp.int32)
    send_slot = (rows[:, None] * capacity + rank).reshape(-1)
    mine = (source == row_index).reshape(-1)
    flat_column = column.reshape(-1)
    buffers = jnp.arange(gen_count * capacity, dtype=jnp.int32)
    send_match = (send_slot[:, None] == buffers[None, :]) & mine[:, None]
    send_column = jnp.sum(jnp.where(send_match, flat_column[:, None], 0), axis=0)
    column_match = (flat_column[:, None] == places[None, :]) & mine[:, None]
    column_position = jnp.sum(jnp.where(column_match, send_slot[:, None], 0), axis=0)
    own = (rows == row_index)[:, None]
    receive_position = jnp.sum(jnp.where(own, source * capacity + rank, 0), axis=0)
    receive_match = receive_position[:, None] == buffers[None, :]
    position_slot = jnp.sum(jnp.where(receive_match, places[:, None], 0), axis=0)
    return (send_column, position_slot, receive_position, column_position)


def local(
    hidden_states,
    grad_out,
    nbr_embed,
    nbr_index,
    gain,
    w_query,
    w_out,
    w_key,
    w_value,
    enc_gain,
    enc_qkv,
    enc_out,
):
    gen_count = lax.axis_size("gen")
    per_device = nbr_embed.shape[0]
    row_size = per_device * lax.axis_size("enc")
    capacity = max(2, 2 * row_size // gen_count)
    tables = routing(nbr_index, lax.axis_index("gen"), gen_count, per_device, row_size, capacity)
    grad_encoded, grad_key, grad_out_proj, grad_value = (
        whole(
            tables,
            nbr_embed,
            enc_gain,
            gain,
            enc_qkv,
            enc_out,
            hidden_states,
            grad_out,
            w_query,
            w_out,
            w_key,
            w_value,
        )
    )
    return widen((grad_encoded, grad_out_proj, grad_key, grad_value))


def solution(mesh):
    return jax.shard_map(
        local,
        mesh=mesh,
        in_specs=(
            P("gen", None),
            P("gen", None),
            P(("enc", "gen"), None, None),
            P(),
            P(),
            P(None, "enc"),
            P("enc", None),
            P(None, "enc"),
            P(None, "enc"),
            P(),
            P(),
            P(),
        ),
        out_specs=(
            P(("enc", "gen"), None, None),
            P("enc", "gen"),
            P("gen", "enc"),
            P("gen", "enc"),
        ),
        check_vma=False,
    )
```
